128 devices in a mesh: row: 16 (over y, x), col: 8 (over z, core).
Axes of the slice: x: 4, y: 4, z: 4, core: 2. Of those that a mesh axis runs over, the one named last changes fastest.
Arguments:
- samples: bfloat16 [16384, 768], P(('row', 'col')), may hold values from -8 to 8, as said below
Outputs:
- factored: float32 [16384, 16384], P('row', 'col')
The draws below stay inside these ranges and needn't reach their ends.
Inputs may be any that keep to these rules, and one draw needn't show every extreme that they name: `samples`: every entry is a feature value.
All inputs are finite; a program needn't handle non-finite values.
Results may differ from the reference program's by a relative error of at most 0.0003.
Values may be sent and summed in bfloat16 or wider, within the bound.
No kernel may reach another device: no remote copies, remote signals or barrier semaphores. Data moves between devices by JAX's collectives and lax.ppermute only.
A program may use at most 128 MiB of HBM per device.

```python
import math
import jax
import jax.numpy as jnp
from jax import lax

FEAT = 768
PANEL = 512
LAYERS = 8
ROWS_DEV = 1024
SAMPLES = 16384
ROW_BLOCK = 32
COL_BLOCK = 64
N_ROW = 16
N_COL = 8


def draw_samples(key, part):
    subkeys = jax.random.split(jax.random.fold_in(key, 11), 7)
    cluster_count = 64
    prototypes = jax.random.normal(subkeys[0], (4, FEAT), jnp.float32)
    mixing = 0.5 * jax.random.normal(subkeys[1], (cluster_count, 4), jnp.float32)
    own_part = jax.random.normal(subkeys[2], (cluster_count, FEAT), jnp.float32)
    centers = jnp.dot(mixing, prototypes) + 0.7 * own_part
    centers = centers / jnp.sqrt(jnp.mean(centers * centers, axis=1, keepdims=True))
    spreads = jnp.exp(jax.random.uniform(subkeys[3], (cluster_count,), jnp.float32, math.log(0.12), math.log(1.0)))
    member = jax.random.randint(subkeys[4], (SAMPLES,), 0, cluster_count)
    flip_sign = jnp.where(jax.random.bernoulli(subkeys[5], 0.5, (SAMPLES,)), 1.0, -1.0)
    noise_part = jax.random.normal(subkeys[6], (SAMPLES, FEAT), jnp.float32)
    row_scales = jnp.ones((SAMPLES,), jnp.float32)
    sample_rows = centers[member] + spreads[member][:, None] * noise_part
    sample_rows = (flip_sign * row_scales)[:, None] * sample_rows
    return jnp.clip(sample_rows, -8.0, 8.0).astype(jnp.bfloat16)


def setup_inputs(seed: int = 0) -> dict:
    streams_of = jax.random.split(jax.random.key(seed), 2)
    return {
        "samples": draw_samples(jax.random.fold_in(streams_of[1], 71), 0),
    }


def ntk_block(left_rows, right_rows, row_ids, col_ids):
    left_f = left_rows.astype(jnp.float32)
    right_f = right_rows.astype(jnp.float32)
    gram_tile = jnp.dot(left_f, right_f.T, precision=lax.Precision.HIGHEST) / FEAT
    row_norms = lax.optimization_barrier(jnp.sum(left_f * left_f, axis=1)) / FEAT
    col_norms = lax.optimization_barrier(jnp.sum(right_f * right_f, axis=1)) / FEAT
    on_diag = row_ids[:, None] == col_ids[None, :]
    norm_scale = jnp.sqrt(row_norms[:, None] * col_norms[None, :])
    covariance = gram_tile
    tangent = gram_tile
    for layer_step in range(LAYERS):
        cosine = jnp.where(on_diag, jnp.float32(1.0), covariance / norm_scale)
        angles = jnp.arccos(cosine)
        sine_part = jnp.sqrt(jnp.maximum(1.0 - cosine * cosine, 0.0))
        covariance = norm_scale / math.pi * (sine_part + (math.pi - angles) * cosine)
        tangent = covariance + tangent * (1.0 - angles / math.pi)
    return tangent / (LAYERS + 1.0) + jnp.where(on_diag, jnp.float32(1.0), jnp.float32(0.0))

def reference(samples):
    blocks = SAMPLES // PANEL
    ordered = samples.reshape(N_ROW, blocks, ROW_BLOCK, FEAT).transpose(1, 0, 2, 3).reshape(SAMPLES, FEAT)
    natural_ids = jnp.arange(SAMPLES, dtype=jnp.int32)
    leading = ntk_block(ordered, ordered[:PANEL], natural_ids, natural_ids[:PANEL])
    corner_factor = jnp.linalg.cholesky(leading[:PANEL])
    solved = lax.linalg.triangular_solve(corner_factor, leading, left_side=False, lower=True, transpose_a=True)
    panel = jnp.concatenate([corner_factor, solved[PANEL:]], axis=0)
    col_ids = natural_ids.reshape(blocks, N_COL, COL_BLOCK).transpose(1, 0, 2).reshape(SAMPLES)
    col_feats = ordered.reshape(blocks, N_COL, COL_BLOCK, FEAT).transpose(1, 0, 2, 3).reshape(SAMPLES, FEAT)
    col_panel = panel.reshape(blocks, N_COL, COL_BLOCK, PANEL).transpose(1, 0, 2, 3).reshape(SAMPLES, PANEL)
    row_ids_all = natural_ids.reshape(blocks, N_ROW, ROW_BLOCK).transpose(1, 0, 2).reshape(SAMPLES)
    row_panel = panel.reshape(blocks, N_ROW, ROW_BLOCK, PANEL).transpose(1, 0, 2, 3).reshape(SAMPLES, PANEL)
    left_index = jnp.minimum(col_ids, PANEL - 1)

    def one_block(block_index):
        start = (block_index * ROWS_DEV).astype(jnp.int32)
        block_rows = lax.dynamic_slice_in_dim(samples, start, ROWS_DEV, 0)
        row_ids = lax.dynamic_slice_in_dim(row_ids_all, start, ROWS_DEV, 0)
        panel_part = lax.dynamic_slice_in_dim(row_panel, start, ROWS_DEV, 0)
        kernel = ntk_block(block_rows, col_feats, row_ids, col_ids)
        update = kernel - jnp.dot(panel_part, col_panel.T, precision=lax.Precision.HIGHEST)
        left_part = jnp.take(panel_part, left_index, axis=1)
        result = jnp.where(col_ids[None, :] < PANEL, left_part, update)
        return jnp.where(row_ids[:, None] >= col_ids[None, :], result, jnp.float32(0.0))
    stacked = lax.map(one_block, jnp.arange(N_ROW, dtype=jnp.int32))
    return stacked.reshape(SAMPLES, SAMPLES)
```

```python
import functools
import math

import jax
import jax.numpy as jnp
from jax import lax
from jax.experimental import pallas as pl
from jax.experimental.pallas import tpu as pltpu
from jax.sharding import PartitionSpec as P

FEAT = 768
PANEL = 512
LAYERS = 8
TILE_R = 128
TILE_C = 256
HIGH = lax.Precision.HIGHEST

ARC = (
    (4.501581511e-01, 3.751401299e-02, 8.424092758e-03, 2.633635570e-03, 4.183752006e-04, 1.140004682e-03, -6.902463010e-04, 4.019670222e-04),
    (4.501581511e-01, 3.751401299e-02, 8.424092758e-03, 2.633635570e-03, 4.183752006e-04, 1.140004682e-03, -6.902463010e-04, 4.019670222e-04),
    (4.501581596e-01, 3.751297114e-02, 8.445134407e-03, 2.473200384e-03, 1.005950977e-03, 2.413872371e-05, 3.721950193e-04),
    (4.501581559e-01, 3.751348376e-02, 8.433736400e-03, 2.565977952e-03, 6.640548863e-04, 6.060103696e-04),
    (4.501581678e-01, 3.751198578e-02, 8.463767294e-03, 2.355179154e-03, 1.268131146e-03),
    (4.501581611e-01, 3.751271895e-02, 8.451689076e-03, 2.417491958e-03, 1.169168271e-03),
    (4.501581592e-01, 3.751297767e-02, 8.446445380e-03, 2.450729231e-03, 1.104390918e-03),
    (4.501581377e-01, 3.751604518e-02, 8.377770913e-03, 2.943260388e-03),
)


def polynomial(coefs, d):
    value = jnp.full_like(d, coefs[-1])
    for coef in coefs[-2::-1]:
        value = value * d + coef
    return value


def tangent_of(cosine, tangent):
    for layer in range(LAYERS):
        size = jnp.abs(cosine) if layer == 0 else cosine
        d = jnp.maximum(1.0 - size, 1e-30)
        w = d * lax.rsqrt(d)
        e = size * (1.0 / math.pi**2) + 1.0 / math.pi**2
        sine = w * (e * lax.rsqrt(e))
        arc = w * polynomial(ARC[layer], d)
        rest = 1.0 - arc
        if layer == 0:
            rest = jnp.where(cosine < 0.0, arc, rest)
        cosine = sine + rest * cosine
        tangent = cosine + tangent * rest
    return tangent


def squares(x):
    xf = x.astype(jnp.float32)
    sq = xf * xf
    hi = sq.astype(jnp.bfloat16)
    lo = (sq - hi.astype(jnp.float32)).astype(jnp.bfloat16)
    return hi, lo


def dot_nt(a, b, precision=None):
    return lax.dot_general(
        a, b, (((1,), (1,)), ((), ())), precision=precision, preferred_element_type=jnp.float32
    )


def norms_down(x):
    hi, lo = squares(x)
    ones = jnp.ones((128, x.shape[1]), jnp.bfloat16)
    return dot_nt(hi, ones) + dot_nt(lo, ones)


def norms_across(x):
    hi, lo = squares(x)
    ones = jnp.ones((16, x.shape[1]), jnp.bfloat16)
    return (dot_nt(ones, hi) + dot_nt(ones, lo))[:8]


SCALE = 1.0 / math.sqrt(FEAT * (LAYERS + 1.0))


def in_order(x):
    return jnp.concatenate(
        [x[m * 128 + a * 32 : m * 128 + a * 32 + 32] for a in range(4) for m in range(2)], axis=0
    )


def factor_kernel(where_ref, lead_ref, own_ref, out_ref, mat, work, inv_dn, scl_dn, inv_ac, scl_ac):
    row_index = where_ref[0]
    col_index = where_ref[1]

    def norms(x_ref, start, count, across):
        x = x_ref[...]
        n = norms_down(x)
        r = lax.rsqrt(n)
        inv_dn[start : start + count, :] = r
        scl_dn[start : start + count, :] = n * r * SCALE
        if across:
            n = norms_across(x)
            r = lax.rsqrt(n)
            inv_ac[...] = r
            scl_ac[...] = n * r * SCALE

    norms(lead_ref, 0, PANEL, True)
    norms(own_ref, PANEL, 128, False)
    chunk = 64
    for jb in range(4):
        lanes = slice(jb * 128, jb * 128 + 128)
        cols = lead_ref[lanes, :]
        mat[jb * 128 : PANEL, lanes] = dot_nt(lead_ref[jb * 128 :, :], cols)
        mat[PANEL:, lanes] = dot_nt(own_ref[...], cols)
        inv_c = inv_ac[0:1, lanes]
        scl_c = scl_ac[0:1, lanes]

        def body(step, carry):
            start = pl.multiple_of(step * chunk, chunk)
            rows = pl.ds(start, chunk)
            raw = mat[rows, lanes] * inv_dn[rows, :] * inv_c
            local = start + lax.broadcasted_iota(jnp.int32, (chunk, 128), 0)
            own = local - PANEL
            own_block = own // 32
            own_id = (col_index * 4 + own_block) * PANEL + row_index * 32 + own - own_block * 32
            row_id = jnp.where(local < PANEL, local, own_id)
            col_id = jb * 128 + lax.broadcasted_iota(jnp.int32, (chunk, 128), 1)
            on_diag = row_id == col_id
            tangent = tangent_of(jnp.where(on_diag, 1.0, raw), raw)
            mat[rows, lanes] = tangent * scl_dn[rows, :] * scl_c + jnp.where(on_diag, 1.0, 0.0)
            return carry

        lax.fori_loop(jb * (128 // chunk), 640 // chunk, body, 0)

    lane = lax.broadcasted_iota(jnp.int32, (128, 128), 1)
    sub = lax.broadcasted_iota(jnp.int32, (128, 128), 0)
    eye = jnp.where(lane == sub, 1.0, 0.0)
    sub8 = lax.broadcasted_iota(jnp.int32, (8, 256), 0)
    for kb in range(4):
        lanes = slice(kb * 128, kb * 128 + 128)
        work[:, :128] = mat[lanes, lanes]
        work[:, 128:] = eye
        for jb in range(16):
            j = jb * 8
            rows = [jnp.broadcast_to(work[j + p : j + p + 1, :], (8, 256)) for p in range(8)]
            e = [[None] * 8 for _ in range(8)]
            for p in range(8):
                for q in range(p, 8):
                    e[p][q] = jnp.broadcast_to(rows[p][:, j + q : j + q + 1], (8, 128))
            block = None
            done = []
            for p in range(8):
                rinv = lax.rsqrt(e[p][p])
                for q in range(p + 1, 8):
                    e[p][q] = e[p][q] * rinv
                for q in range(p + 1, 8):
                    for s in range(q, 8):
                        e[q][s] = e[q][s] - e[p][q] * e[p][s]
                row = rows[p]
                for m in range(p):
                    row = row - jnp.concatenate([e[m][p]] * 2, axis=1) * done[m]
                row = row * jnp.concatenate([rinv] * 2, axis=1)
                done.append(row)
                block = row if p == 0 else jnp.where(sub8 == p, row, block)
            work[j : j + 8, :] = block
            if jb < 15:
                outer = lax.dot_general(
                    block[:, :128], block, (((0,), (0,)), ((), ())), precision=HIGH,
                    preferred_element_type=jnp.float32,
                )
                work[j + 8 :, :] = work[j + 8 :, :] - outer[j + 8 :, :]
        linv = work[:, 128:]
        below = (kb + 1) * 128
        solved = dot_nt(mat[below:, lanes], linv, HIGH)
        mine = solved[PANEL - below :, :]
        hi = mine.astype(jnp.bfloat16)
        out_ref[:, lanes] = hi
        out_ref[:, PANEL + kb * 128 : PANEL + kb * 128 + 128] = (
            mine - hi.astype(jnp.float32)
        ).astype(jnp.bfloat16)
        if kb < 3:
            mat[below:, below:] = mat[below:, below:] - dot_nt(solved, solved[: PANEL - below], HIGH)


def factor(where, lead, own):
    return pl.pallas_call(
        factor_kernel,
        out_shape=jax.ShapeDtypeStruct((128, 2 * PANEL), jnp.bfloat16),
        in_specs=[
            pl.BlockSpec(memory_space=pltpu.SMEM),
            pl.BlockSpec(memory_space=pltpu.VMEM),
            pl.BlockSpec(memory_space=pltpu.VMEM),
        ],
        out_specs=pl.BlockSpec(memory_space=pltpu.VMEM),
        scratch_shapes=[
            pltpu.VMEM((PANEL + 128, PANEL), jnp.float32),
            pltpu.VMEM((128, 256), jnp.float32),
            pltpu.VMEM((PANEL + 128, 128), jnp.float32),
            pltpu.VMEM((PANEL + 128, 128), jnp.float32),
            pltpu.VMEM((8, PANEL), jnp.float32),
            pltpu.VMEM((8, PANEL), jnp.float32),
        ],
        name="factor",
        cost_estimate=pl.CostEstimate(flops=int(1e9), bytes_accessed=int(2e6), transcendentals=0),
    )(where, lead, own)


def tiles_kernel(where_ref, rows_ref, cols_ref, out_ref, cols, gram, inv_ac, scl_ac, inv_dn, scl_dn):
    step = pl.program_id(0)
    row_index = where_ref[0]
    col_index = where_ref[1]
    count = cols_ref.shape[0] // TILE_C

    @pl.when(step == 0)
    def _():
        def body(t, carry):
            rows = pl.ds(pl.multiple_of(t * TILE_C, TILE_C), TILE_C)
            x = in_order(cols_ref[rows, :])
            cols[rows, :] = x
            n = norms_across(x)
            r = lax.rsqrt(n)
            inv_ac[t] = r
            scl_ac[t] = n * r * SCALE
            return carry

        lax.fori_loop(0, count, body, 0)

    x = rows_ref[...]
    n = norms_down(x)
    r = lax.rsqrt(n)
    inv_dn[...] = r
    scl_dn[...] = n * r * SCALE

    def tile(t, carry):
        start = pl.multiple_of(t * TILE_C, TILE_C)
        gram[...] = dot_nt(x, cols[pl.ds(start, TILE_C), :])
        inv_c = inv_ac[t][0:1]
        scl_c = scl_ac[t][0:1]
        chunk = 32

        def body(k, carry, diag):
            first = pl.multiple_of(k * chunk, chunk)
            rows = pl.ds(first, chunk)
            inv_r = jnp.concatenate([inv_dn[rows, :]] * 2, axis=1)
            scl_r = jnp.concatenate([scl_dn[rows, :]] * 2, axis=1)
            raw = gram[rows, :] * inv_r * inv_c
            if diag:
                u = lax.broadcasted_iota(jnp.int32, (chunk, TILE_C), 0)
                v = lax.broadcasted_iota(jnp.int32, (chunk, TILE_C), 1)
                row_id = (step * 4 + k) * PANEL + row_index * 32 + u
                col_id = (t * 4 + v // 64) * PANEL + col_index * 64 + v % 64
                on_diag = row_id == col_id
                tangent = tangent_of(jnp.where(on_diag, 1.0, raw), raw)
                value = tangent * scl_r * scl_c + jnp.where(on_diag, 1.0, 0.0)
            else:
                value = tangent_of(raw, raw) * scl_r * scl_c
            out_ref[rows, pl.ds(start, TILE_C)] = value
            return carry

        @pl.when(t == step)
        def _():
            lax.fori_loop(0, TILE_R // chunk, functools.partial(body, diag=True), 0)

        @pl.when(t != step)
        def _():
            lax.fori_loop(0, TILE_R // chunk, functools.partial(body, diag=False), 0)

        return carry

    lax.fori_loop(0, step + 1, tile, 0)


def tiles(where, rows, cols):
    n_rows, n_cols = rows.shape[0], cols.shape[0]
    return pl.pallas_call(
        tiles_kernel,
        out_shape=jax.ShapeDtypeStruct((n_rows, n_cols), jnp.float32),
        grid=(n_rows // TILE_R,),
        in_specs=[
            pl.BlockSpec(memory_space=pltpu.SMEM),
            pl.BlockSpec((TILE_R, FEAT), lambda i: (i, 0)),
            pl.BlockSpec((n_cols, FEAT), lambda i: (0, 0)),
        ],
        out_specs=pl.BlockSpec((TILE_R, n_cols), lambda i: (i, 0)),
        scratch_shapes=[
            pltpu.VMEM((n_cols, FEAT), jnp.bfloat16),
            pltpu.VMEM((TILE_R, TILE_C), jnp.float32),
            pltpu.VMEM((n_cols // TILE_C, 8, TILE_C), jnp.float32),
            pltpu.VMEM((n_cols // TILE_C, 8, TILE_C), jnp.float32),
            pltpu.VMEM((TILE_R, 128), jnp.float32),
            pltpu.VMEM((TILE_R, 128), jnp.float32),
        ],
        name="tiles",
        cost_estimate=pl.CostEstimate(flops=int(30e9), bytes_accessed=int(12e6), transcendentals=0),
    )(where, rows, cols)


def update_kernel(where_ref, kernel_ref, rows_ref, cols_ref, out_ref):
    step = pl.program_id(0)
    row_index = where_ref[0]
    col_index = where_ref[1]
    count = cols_ref.shape[0] // TILE_C
    for half in range(2):
        row_tile = step * 2 + half
        mine = slice(half * TILE_R, half * TILE_R + TILE_R)
        hi_r = rows_ref[mine, :PANEL]
        lo_r = rows_ref[mine, PANEL:]
        for t in range(count):
            lanes = slice(t * TILE_C, t * TILE_C + TILE_C)

            @pl.when(row_tile < t)
            def _():
                out_ref[mine, lanes] = jnp.zeros((TILE_R, TILE_C), jnp.float32)

            @pl.when(row_tile >= t)
            def _():
                both = in_order(cols_ref[lanes, :])
                hi_c = both[:, :PANEL]
                lo_c = both[:, PANEL:]
                drop = dot_nt(hi_r, hi_c) + dot_nt(hi_r, lo_c) + dot_nt(lo_r, hi_c)
                value = kernel_ref[mine, lanes] - drop
                s = lax.broadcasted_iota(jnp.int32, (TILE_R, TILE_C), 0)
                v = lax.broadcasted_iota(jnp.int32, (TILE_R, TILE_C), 1)
                if t == 0:
                    first = pl.multiple_of(col_index // 2 * 128, 128)
                    left = rows_ref[mine, pl.ds(first, 128)].astype(jnp.float32)
                    left = left + rows_ref[mine, pl.ds(first + PANEL, 128)].astype(jnp.float32)
                    left = jnp.where(col_index % 2 == 1, pltpu.roll(left, 64, 1), left)
                    left = jnp.concatenate([left, left], axis=1)
                    value = jnp.where(v < 64, left, value)
                row_id = (row_tile * 4 + s // 32) * PANEL + row_index * 32 + s % 32
                col_id = (t * 4 + v // 64) * PANEL + col_index * 64 + v % 64
                out_ref[mine, lanes] = jnp.where(row_id >= col_id, value, 0.0)


def update(where, kernel, rows, cols):
    n_rows, n_cols = kernel.shape
    return pl.pallas_call(
        update_kernel,
        out_shape=jax.ShapeDtypeStruct((n_rows, n_cols), jnp.float32),
        grid=(n_rows // (2 * TILE_R),),
        in_specs=[
            pl.BlockSpec(memory_space=pltpu.SMEM),
            pl.BlockSpec((2 * TILE_R, n_cols), lambda i: (i, 0)),
            pl.BlockSpec((2 * TILE_R, 2 * PANEL), lambda i: (i, 0)),
            pl.BlockSpec((n_cols, 2 * PANEL), lambda i: (0, 0)),
        ],
        out_specs=pl.BlockSpec((2 * TILE_R, n_cols), lambda i: (i, 0)),
        name="update",
        cost_estimate=pl.CostEstimate(flops=int(6e9), bytes_accessed=int(20e6), transcendentals=0),
    )(where, kernel, rows, cols)


def per_device(samples):
    row_count = lax.axis_size("row")
    col_count = lax.axis_size("col")
    where = jnp.stack([lax.axis_index("row"), lax.axis_index("col")]).astype(jnp.int32)
    share = row_count // col_count
    route = [
        (r * col_count + k, (k * share + r % share) * col_count + r // share)
        for r in range(row_count)
        for k in range(col_count)
    ]

    def to_columns(x):
        moved = lax.ppermute(x, ("row", "col"), route)
        return lax.all_gather(moved, "row", axis=0, tiled=True)

    head = lax.all_gather(samples[: PANEL // row_count], "col", axis=0)[0]
    lead = lax.all_gather(head, "row", axis=0, tiled=True)
    row_feats = lax.all_gather(samples, "col", axis=0, tiled=True)
    col_feats = to_columns(samples)
    mine = factor(where, lead, samples)
    panel_row = lax.all_gather(mine, "col", axis=0, tiled=True)
    panel_col = to_columns(mine)
    kernel = tiles(where, row_feats, col_feats)
    return update(where, kernel, panel_row, panel_col)


def solution(mesh):
    return jax.shard_map(
        per_device,
        mesh=mesh,
        in_specs=(P(("row", "col"), None),),
        out_specs=P("row", "col"),
        check_vma=False,
    )
```

```python
import functools
import math

import jax
import jax.numpy as jnp
import numpy as np
from jax import lax
from jax.experimental import pallas as pl
from jax.experimental.pallas import tpu as pltpu
from jax.sharding import PartitionSpec as P

FEAT = 768
PANEL = 512
LAYERS = 8
TILE_R = 128
TILE_C = 256
HIGH = lax.Precision.HIGHEST

ARC = (
    (1.570796265e+00, -9.999884905e-01, 7.850416849e-01, -6.623695706e-01, 5.625094387e-01, -4.372503233e-01, 2.693842319e-01, -1.086155413e-01, 2.049311747e-02),
    (1.570796265e+00, -9.999884905e-01, 7.850416849e-01, -6.623695706e-01, 5.625094387e-01, -4.372503233e-01, 2.693842319e-01, -1.086155413e-01, 2.049311747e-02),
    (1.570326531e+00, -9.935370566e-01, 7.471319178e-01, -5.376914312e-01, 3.111383121e-01, -1.187027540e-01, 2.133516172e-02),
    (1.567898155e+00, -9.719742948e-01, 6.682907781e-01, -3.857788817e-01, 1.484597498e-01, -2.689621130e-02),
    (1.566642297e+00, -9.635808948e-01, 6.460403822e-01, -3.565340200e-01, 1.294006162e-01, -2.196850873e-02),
    (1.558633208e+00, -9.141686374e-01, 5.246089379e-01, -2.079489415e-01, 3.887608390e-02),
    (1.557122831e+00, -9.070176865e-01, 5.119586953e-01, -1.980387362e-01, 3.597512846e-02),
    (1.555954084e+00, -9.016562063e-01, 5.027575168e-01, -1.910373211e-01, 3.398202014e-02),
)


def scales():
    out = [np.float32(1.0)]
    for _ in range(LAYERS):
        out.append(np.float32(np.float32(math.pi) * out[-1]))
    return out


KAPPA = scales()


def polynomial(coefs, c):
    value = c * coefs[-1] + coefs[-2]
    for coef in coefs[-3::-1]:
        value = value * c + coef
    return value


def tangent_of(cosine, tangent):
    for layer in range(LAYERS):
        kappa = KAPPA[layer]
        coefs = [float(a / np.float64(kappa) ** (k + 1)) for k, a in enumerate(ARC[layer])]
        size = jnp.abs(cosine) if layer == 0 else cosine
        square = jnp.maximum(float(np.float32(kappa * kappa)) - size * size, 1e-30)
        sine = square * lax.rsqrt(square)
        angle = sine * polynomial(coefs, size)
        rest = math.pi - angle
        if layer == 0:
            rest = jnp.where(cosine < 0.0, angle, rest)
        cosine = sine + rest * cosine
        tangent = cosine + rest * tangent
    return tangent


def squares(x):
    xf = x.astype(jnp.float32)
    sq = xf * xf
    hi = sq.astype(jnp.bfloat16)
    lo = (sq - hi.astype(jnp.float32)).astype(jnp.bfloat16)
    return hi, lo


def dot_nt(a, b, precision=None):
    return lax.dot_general(
        a, b, (((1,), (1,)), ((), ())), precision=precision, preferred_element_type=jnp.float32
    )


def norms_down(x):
    hi, lo = squares(x)
    ones = jnp.ones((128, x.shape[1]), jnp.bfloat16)
    return dot_nt(hi, ones) + dot_nt(lo, ones)


def norms_across(x):
    hi, lo = squares(x)
    ones = jnp.ones((16, x.shape[1]), jnp.bfloat16)
    return (dot_nt(ones, hi) + dot_nt(ones, lo))[:8]


SCALE = 1.0 / math.sqrt(FEAT * (LAYERS + 1.0) * float(KAPPA[LAYERS]))


def in_order(x):
    return jnp.concatenate(
        [x[m * 128 + a * 32 : m * 128 + a * 32 + 32] for a in range(4) for m in range(2)], axis=0
    )


def split(x):
    hi = x.astype(jnp.bfloat16)
    return hi, (x - hi.astype(jnp.float32)).astype(jnp.bfloat16)


def slot_of(step, where):
    other = (step + where[1]) % 2
    mine = where[1] + other * (1 - 2 * (where[1] % 2))
    return ((mine - step + 8) % 8) // 2, other


def leading_kernel(
    where_ref, g0, g1, g2, g3, own_ref, corner_ref, out_ref, lead, inv_dn, scl_dn, inv_ac, scl_ac
):
    row_index = where_ref[0]
    col_index = where_ref[1]
    for dx, piece in enumerate((g0, g1, g2, g3)):
        for dy in range(4):
            r = (row_index // 4 + 4 - dy) % 4 * 4 + (row_index % 4 + 4 - dx) % 4
            lead[pl.ds(pl.multiple_of(r * 32, 32), 32), :] = piece[dy]

    def norms(x, start, count):
        n = norms_down(x)
        r = lax.rsqrt(n)
        inv_dn[start : start + count, :] = r
        scl_dn[start : start + count, :] = n * r * SCALE

    x = lead[...]
    norms(x, 0, PANEL)
    n = norms_across(x)
    r = lax.rsqrt(n)
    inv_ac[...] = r
    scl_ac[...] = n * r * SCALE
    norms(own_ref[...], PANEL, 128)
    chunk = 64
    for jb in range(4):
        lanes = slice(jb * 128, jb * 128 + 128)
        cols = lead[lanes, :]
        corner_ref[jb * 128 :, lanes] = dot_nt(lead[jb * 128 :, :], cols)
        out_ref[:, lanes] = dot_nt(own_ref[...], cols)
        inv_c = inv_ac[0:1, lanes]
        scl_c = scl_ac[0:1, lanes]

        def body(step, carry, ref, base):
            start = pl.multiple_of(step * chunk, chunk)
            rows = pl.ds(start, chunk)
            down = pl.ds(start + base, chunk)
            raw = ref[rows, lanes] * inv_dn[down, :] * inv_c
            local = start + lax.broadcasted_iota(jnp.int32, (chunk, 128), 0)
            if base:
                block = local // 32
                local = (col_index * 4 + block) * PANEL + row_index * 32 + local - block * 32
            col_id = jb * 128 + lax.broadcasted_iota(jnp.int32, (chunk, 128), 1)
            on_diag = local == col_id
            tangent = tangent_of(jnp.where(on_diag, 1.0, raw), raw)
            ref[rows, lanes] = tangent * scl_dn[down, :] * scl_c + jnp.where(on_diag, 1.0, 0.0)
            return carry

        lax.fori_loop(0, 128 // chunk, functools.partial(body, ref=out_ref, base=PANEL), 0, unroll=2)
        lax.fori_loop(
            jb * (128 // chunk), PANEL // chunk, functools.partial(body, ref=corner_ref, base=0), 0
        )


def leading(where, pieces, own):
    vmem = pl.BlockSpec(memory_space=pltpu.VMEM)
    return pl.pallas_call(
        leading_kernel,
        out_shape=(
            jax.ShapeDtypeStruct((PANEL, PANEL), jnp.float32),
            jax.ShapeDtypeStruct((128, PANEL), jnp.float32),
        ),
        in_specs=[pl.BlockSpec(memory_space=pltpu.SMEM)] + [vmem] * 5,
        out_specs=(vmem, vmem),
        scratch_shapes=[
            pltpu.VMEM((PANEL, FEAT), jnp.bfloat16),
            pltpu.VMEM((PANEL + 128, 128), jnp.float32),
            pltpu.VMEM((PANEL + 128, 128), jnp.float32),
            pltpu.VMEM((8, PANEL), jnp.float32),
            pltpu.VMEM((8, PANEL), jnp.float32),
        ],
        name="leading",
        cost_estimate=pl.CostEstimate(flops=int(8e9), bytes_accessed=int(2e6), transcendentals=0),
    )(where, *pieces, own)


def factor_kernel(corner_ref, out_ref, mat, work):
    eye = jnp.where(
        lax.broadcasted_iota(jnp.int32, (128, 128), 1)
        == lax.broadcasted_iota(jnp.int32, (128, 128), 0),
        1.0,
        0.0,
    )
    sub8 = lax.broadcasted_iota(jnp.int32, (8, 256), 0)
    mat[:PANEL, :] = corner_ref[...]
    mat[PANEL:, :] = jnp.zeros((PANEL, PANEL), jnp.float32)

    def eliminate(kb):
        lanes = slice(kb * 128, kb * 128 + 128)
        linv = work[:, 128:]
        inverse = jnp.transpose(linv)
        top = PANEL + kb * 128
        if kb:
            upper = dot_nt(mat[PANEL:top, lanes], linv, HIGH)
            mat[PANEL:top, lanes] = upper
            upper = jnp.concatenate([upper, inverse], axis=0)
        else:
            upper = inverse
        mat[top : top + 128, lanes] = inverse
        if kb < 3:
            below = (kb + 1) * 128
            solved = dot_nt(mat[below:PANEL, lanes], linv, HIGH)
            mat[below:PANEL, below:] = mat[below:PANEL, below:] - dot_nt(solved, solved, HIGH)
            mat[PANEL : top + 128, below:] = mat[PANEL : top + 128, below:] - dot_nt(
                upper, solved, HIGH
            )

    def column(kb, carry):
        first = pl.multiple_of(kb * 128, 128)
        work[:, :128] = mat[pl.ds(first, 128), pl.ds(first, 128)]
        work[:, 128:] = eye
        for jb in range(16):
            j = jb * 8
            rows = [jnp.broadcast_to(work[j + p : j + p + 1, :], (8, 256)) for p in range(8)]
            e = [[None] * 8 for _ in range(8)]
            for p in range(8):
                for q in range(p, 8):
                    e[p][q] = jnp.broadcast_to(rows[p][:, j + q : j + q + 1], (8, 128))
            block = None
            done = []
            for p in range(8):
                rinv = lax.rsqrt(e[p][p])
                for q in range(p + 1, 8):
                    e[p][q] = e[p][q] * rinv
                for q in range(p + 1, 8):
                    for s in range(q, 8):
                        e[q][s] = e[q][s] - e[p][q] * e[p][s]
                row = rows[p]
                for m in range(p):
                    row = row - jnp.concatenate([e[m][p]] * 2, axis=1) * done[m]
                row = row * jnp.concatenate([rinv] * 2, axis=1)
                done.append(row)
                block = row if p == 0 else jnp.where(sub8 == p, row, block)
            work[j : j + 8, :] = block
            if jb < 15:
                outer = lax.dot_general(
                    block[:, :128], block, (((0,), (0,)), ((), ())), precision=HIGH,
                    preferred_element_type=jnp.float32,
                )
                work[j + 8 :, :] = work[j + 8 :, :] - outer[j + 8 :, :]
        for n in range(4):
            pl.when(kb == n)(functools.partial(eliminate, n))
        return carry

    lax.fori_loop(0, 4, column, 0)
    hi, lo = split(mat[PANEL:, :])
    out_ref[:, :PANEL] = hi
    out_ref[:, PANEL:] = lo


def factor(corner):
    return pl.pallas_call(
        factor_kernel,
        out_shape=jax.ShapeDtypeStruct((PANEL, 2 * PANEL), jnp.bfloat16),
        in_specs=[pl.BlockSpec(memory_space=pltpu.VMEM)],
        out_specs=pl.BlockSpec(memory_space=pltpu.VMEM),
        scratch_shapes=[
            pltpu.VMEM((2 * PANEL, PANEL), jnp.float32),
            pltpu.VMEM((128, 256), jnp.float32),
        ],
        name="factor",
        cost_estimate=pl.CostEstimate(flops=int(25e9), bytes_accessed=int(2e6), transcendentals=0),
    )(corner)


def tiles_kernel(
    where_ref, near_ref, far_ref, cols_ref, out_ref, cols, gram, inv_ac, scl_ac, inv_dn, scl_dn
):
    step = pl.program_id(0)
    row_index = where_ref[0]
    col_index = where_ref[1]
    count = cols_ref.shape[0] // TILE_C

    @pl.when(step == 0)
    def _():
        def body(t, carry):
            rows = pl.ds(pl.multiple_of(t * TILE_C, TILE_C), TILE_C)
            x = in_order(cols_ref[rows, :])
            cols[rows, :] = x
            n = norms_across(x)
            r = lax.rsqrt(n)
            inv_ac[t] = r
            scl_ac[t] = n * r * SCALE
            return carry

        lax.fori_loop(0, count, body, 0)

    _, other = slot_of(step, where_ref)
    x = jnp.where(other == 1, far_ref[0], near_ref[0])
    n = norms_down(x)
    r = lax.rsqrt(n)
    inv_dn[...] = r
    scl_dn[...] = n * r * SCALE
    chunk = 32

    def product(t, slot):
        start = pl.multiple_of(t * TILE_C, TILE_C)
        gram[slot] = dot_nt(x, cols[pl.ds(start, TILE_C), :])

    def piece(t, slot, k):
        rows = slice(k * chunk, k * chunk + chunk)
        inv_r = jnp.concatenate([inv_dn[rows, :]] * 2, axis=1)
        scl_r = jnp.concatenate([scl_dn[rows, :]] * 2, axis=1)
        raw = gram[slot, rows, :] * inv_r * inv_ac[t][0:1]
        value = tangent_of(raw, raw) * scl_r * scl_ac[t][0:1]
        out_ref[rows, pl.ds(pl.multiple_of(t * TILE_C, TILE_C), TILE_C)] = value

    product(0, 0)

    def tile(t, carry):
        slot = t % 2
        product(t + 1, 1 - slot)
        for k in range(TILE_R // chunk):
            piece(t, slot, k)
        return carry

    lax.fori_loop(0, step, tile, 0)

    slot = step % 2
    for half in range(2):
        width = 128 * (half + 1)
        rows = slice(half * 64, half * 64 + 64)
        for lane in range(half + 1):
            lanes = slice(lane * 128, lane * 128 + 128)
            raw = gram[slot, rows, lanes] * inv_dn[rows, :] * inv_ac[step][0:1, lanes]
            u = half * 64 + lax.broadcasted_iota(jnp.int32, (64, 128), 0)
            v = lane * 128 + lax.broadcasted_iota(jnp.int32, (64, 128), 1)
            row_id = u // 32 * PANEL + row_index * 32 + u % 32
            col_id = v // 64 * PANEL + col_index * 64 + v % 64
            on_diag = row_id == col_id
            tangent = tangent_of(jnp.where(on_diag, 1.0, raw), raw)
            value = tangent * scl_dn[rows, :] * scl_ac[step][0:1, lanes]
            value = value + jnp.where(on_diag, 1.0, 0.0)
            first = pl.multiple_of(step * TILE_C + lane * 128, 128)
            out_ref[rows, pl.ds(first, 128)] = value


def tiles(where, near, far, cols):
    n_rows, n_cols = 8 * TILE_R, cols.shape[0]
    piece = (1, TILE_R, FEAT)
    return pl.pallas_call(
        tiles_kernel,
        out_shape=jax.ShapeDtypeStruct((n_rows, n_cols), jnp.float32),
        grid_spec=pltpu.PrefetchScalarGridSpec(
            num_scalar_prefetch=1,
            grid=(n_rows // TILE_R,),
            in_specs=[
                pl.BlockSpec(piece, lambda i, where: (slot_of(i, where)[0], 0, 0)),
                pl.BlockSpec(piece, lambda i, where: (slot_of(i, where)[0], 0, 0)),
                pl.BlockSpec((n_cols, FEAT), lambda i, where: (0, 0)),
            ],
            out_specs=pl.BlockSpec((TILE_R, n_cols), lambda i, where: (i, 0)),
            scratch_shapes=[
                pltpu.VMEM((n_cols, FEAT), jnp.bfloat16),
                pltpu.VMEM((2, TILE_R, TILE_C), jnp.float32),
                pltpu.VMEM((n_cols // TILE_C, 8, TILE_C), jnp.float32),
                pltpu.VMEM((n_cols // TILE_C, 8, TILE_C), jnp.float32),
                pltpu.VMEM((TILE_R, 128), jnp.float32),
                pltpu.VMEM((TILE_R, 128), jnp.float32),
            ],
        ),
        name="tiles",
        cost_estimate=pl.CostEstimate(flops=int(30e9), bytes_accessed=int(12e6), transcendentals=0),
    )(where, near, far, cols)


def solve(x, v_ref):
    hi, lo = split(x)
    parts = []
    for n in range(4):
        depth = n * 128 + 128
        v_hi = v_ref[:depth, n * 128 : depth]
        v_lo = v_ref[:depth, PANEL + n * 128 : PANEL + depth]
        dot = functools.partial(jnp.dot, preferred_element_type=jnp.float32)
        parts.append(dot(hi[:, :depth], v_hi) + dot(hi[:, :depth], v_lo) + dot(lo[:, :depth], v_hi))
    return jnp.concatenate(parts, axis=1)


def update_kernel(where_ref, kernel_ref, near_ref, far_ref, cols_ref, v_ref, out_ref, hi_c, lo_c, left):
    step = pl.program_id(0)
    row_index = where_ref[0]
    col_index = where_ref[1]
    count = cols_ref.shape[0] // TILE_C

    @pl.when(step == 0)
    def _():
        def body(t, carry):
            rows = pl.ds(pl.multiple_of(t * TILE_C, TILE_C), TILE_C)
            hi, lo = split(solve(in_order(cols_ref[rows, :]), v_ref))
            hi_c[rows, :] = hi
            lo_c[rows, :] = lo
            return carry

        lax.fori_loop(0, count, body, 0)

    _, other = slot_of(step, where_ref)
    solved = solve(jnp.where(other == 1, far_ref[0], near_ref[0]), v_ref)
    hi_r, lo_r = split(solved)
    for n in range(4):
        left[n] = solved[:, n * 128 : n * 128 + 128]

    def masked(value, t):
        s = lax.broadcasted_iota(jnp.int32, (TILE_R, TILE_C), 0)
        v = lax.broadcasted_iota(jnp.int32, (TILE_R, TILE_C), 1)
        row_id = (step * 4 + s // 32) * PANEL + row_index * 32 + s % 32
        col_id = (t * 4 + v // 64) * PANEL + col_index * 64 + v % 64
        return jnp.where(row_id >= col_id, value, 0.0)

    for t in range(count):
        lanes = slice(t * TILE_C, t * TILE_C + TILE_C)

        @pl.when(step < t)
        def _():
            out_ref[:, lanes] = jnp.zeros((TILE_R, TILE_C), jnp.float32)

        @pl.when(step >= t)
        def _():
            drop = (
                dot_nt(hi_r, hi_c[lanes, :])
                + dot_nt(hi_r, lo_c[lanes, :])
                + dot_nt(lo_r, hi_c[lanes, :])
            )
            value = kernel_ref[:, lanes] - drop
            if t == 0:
                mine = left[col_index // 2]
                mine = jnp.where(col_index % 2 == 1, pltpu.roll(mine, 64, 1), mine)
                mine = jnp.concatenate([mine, mine], axis=1)
                v = lax.broadcasted_iota(jnp.int32, (TILE_R, TILE_C), 1)
                value = jnp.where(v < 64, mine, value)
            out_ref[:, lanes] = value

            @pl.when(step == t)
            def _():
                out_ref[:, lanes] = masked(out_ref[:, lanes], t)


def update(where, kernel, near, far, cols, v):
    n_rows, n_cols = kernel.shape
    piece = (1, TILE_R, PANEL)
    return pl.pallas_call(
        update_kernel,
        out_shape=jax.ShapeDtypeStruct((n_rows, n_cols), jnp.float32),
        grid_spec=pltpu.PrefetchScalarGridSpec(
            num_scalar_prefetch=1,
            grid=(n_rows // TILE_R,),
            in_specs=[
                pl.BlockSpec((TILE_R, n_cols), lambda i, where: (i, 0)),
                pl.BlockSpec(piece, lambda i, where: (slot_of(i, where)[0], 0, 0)),
                pl.BlockSpec(piece, lambda i, where: (slot_of(i, where)[0], 0, 0)),
                pl.BlockSpec((n_cols, PANEL), lambda i, where: (0, 0)),
                pl.BlockSpec((PANEL, 2 * PANEL), lambda i, where: (0, 0)),
            ],
            out_specs=pl.BlockSpec((TILE_R, n_cols), lambda i, where: (i, 0)),
            scratch_shapes=[
                pltpu.VMEM((n_cols, PANEL), jnp.bfloat16),
                pltpu.VMEM((n_cols, PANEL), jnp.bfloat16),
                pltpu.VMEM((4, TILE_R, 128), jnp.float32),
            ],
        ),
        name="update",
        cost_estimate=pl.CostEstimate(flops=int(6e9), bytes_accessed=int(20e6), transcendentals=0),
    )(where, kernel, near, far, cols, v)


def send(x, target):
    pairs = [(r * 8 + k, target(r, k)) for r in range(16) for k in range(8)]
    return lax.ppermute(x, ("row", "col"), [(s, t[0] * 8 + t[1]) for s, t in pairs if t])


def along_z(d):
    return lambda r, k: (r, (k + 2 * d) % 8)


def along_y(d):
    return lambda r, k: ((r + 4 * d) % 16, k)


def along_x(d):
    return lambda r, k: (r // 4 * 4 + (r + d) % 4, k)


def other_core(r, k):
    return r, k ^ 1


def to_columns(x):
    moved = send(x, lambda r, k: (k * 2 + r % 2, r // 2))
    return lax.all_gather(moved, "row", axis=0, tiled=True)


def to_rows(x):
    near = jnp.stack([x] + [send(x, along_z(d)) for d in (1, 2, 3)])
    return near, send(near, other_core)


def to_all(x):
    head = jnp.where(lax.axis_index("col") == 0, x[:32], jnp.zeros((32, FEAT), x.dtype))
    for bit in (1, 2, 4):
        head = head + send(head, lambda r, k: (r, k | bit) if k < bit else None)
    column = jnp.stack([head] + [send(head, along_y(d)) for d in (1, 2, 3)])
    return [column] + [send(column, along_x(d)) for d in (1, 2, 3)]


def per_device(samples):
    where = jnp.stack([lax.axis_index("row"), lax.axis_index("col")]).astype(jnp.int32)
    pieces = to_all(samples)
    if WAIT:
        samples_later, pieces = lax.optimization_barrier((samples, pieces))
    else:
        samples_later = samples
    corner, own = leading(where, pieces, samples)
    col_feats = to_columns(samples_later)
    own_cols = to_columns(own)
    near_feats, far_feats = to_rows(samples_later)
    near, far = to_rows(own)
    v = factor(corner)
    kernel = tiles(where, near_feats, far_feats, col_feats)
    return update(where, kernel, near, far, own_cols, v)


WAIT = True


def solution(mesh):
    return jax.shard_map(
        per_device,
        mesh=mesh,
        in_specs=(P(("row", "col"), None),),
        out_specs=P("row", "col"),
        check_vma=False,
    )
```

```python
import functools
import math

import jax
import jax.numpy as jnp
import numpy as np
from jax import lax
from jax.experimental import pallas as pl
from jax.experimental.pallas import tpu as pltpu
from jax.sharding import PartitionSpec as P

FEAT = 768
PANEL = 512
LAYERS = 8
TILE_R = 128
TILE_C = 256
HIGH = lax.Precision.HIGHEST

ARC = (
    (1.570796265e+00, -9.999884905e-01, 7.850416849e-01, -6.623695706e-01, 5.625094387e-01, -4.372503233e-01, 2.693842319e-01, -1.086155413e-01, 2.049311747e-02),
    (1.570796265e+00, -9.999884905e-01, 7.850416849e-01, -6.623695706e-01, 5.625094387e-01, -4.372503233e-01, 2.693842319e-01, -1.086155413e-01, 2.049311747e-02),
    (1.570326531e+00, -9.935370566e-01, 7.471319178e-01, -5.376914312e-01, 3.111383121e-01, -1.187027540e-01, 2.133516172e-02),
    (1.567898155e+00, -9.719742948e-01, 6.682907781e-01, -3.857788817e-01, 1.484597498e-01, -2.689621130e-02),
    (1.566642297e+00, -9.635808948e-01, 6.460403822e-01, -3.565340200e-01, 1.294006162e-01, -2.196850873e-02),
    (1.558633208e+00, -9.141686374e-01, 5.246089379e-01, -2.079489415e-01, 3.887608390e-02),
    (1.557122831e+00, -9.070176865e-01, 5.119586953e-01, -1.980387362e-01, 3.597512846e-02),
    (1.555954084e+00, -9.016562063e-01, 5.027575168e-01, -1.910373211e-01, 3.398202014e-02),
)


def scales():
    out = [np.float32(1.0)]
    for _ in range(LAYERS):
        out.append(np.float32(np.float32(math.pi) * out[-1]))
    return out


KAPPA = scales()


def polynomial(coefs, c):
    value = c * coefs[-1] + coefs[-2]
    for coef in coefs[-3::-1]:
        value = value * c + coef
    return value


def tangent_of(cosine, tangent):
    for layer in range(LAYERS):
        kappa = KAPPA[layer]
        coefs = [float(a / np.float64(kappa) ** (k + 1)) for k, a in enumerate(ARC[layer])]
        size = jnp.abs(cosine) if layer == 0 else cosine
        square = jnp.maximum(float(np.float32(kappa * kappa)) - size * size, 1e-30)
        sine = square * lax.rsqrt(square)
        angle = sine * polynomial(coefs, size)
        rest = math.pi - angle
        if layer == 0:
            rest = jnp.where(cosine < 0.0, angle, rest)
        cosine = sine + rest * cosine
        tangent = cosine + rest * tangent
    return tangent


def squares(x):
    xf = x.astype(jnp.float32)
    sq = xf * xf
    hi = sq.astype(jnp.bfloat16)
    lo = (sq - hi.astype(jnp.float32)).astype(jnp.bfloat16)
    return hi, lo


def dot_nt(a, b, precision=None):
    return lax.dot_general(
        a, b, (((1,), (1,)), ((), ())), precision=precision, preferred_element_type=jnp.float32
    )


def norms_down(x):
    hi, lo = squares(x)
    ones = jnp.ones((128, x.shape[1]), jnp.bfloat16)
    return dot_nt(hi, ones) + dot_nt(lo, ones)


def norms_across(x):
    hi, lo = squares(x)
    ones = jnp.ones((16, x.shape[1]), jnp.bfloat16)
    return (dot_nt(ones, hi) + dot_nt(ones, lo))[:8]


SCALE = 1.0 / math.sqrt(FEAT * (LAYERS + 1.0) * float(KAPPA[LAYERS]))


def in_order(x):
    return jnp.concatenate(
        [x[m * 128 + a * 32 : m * 128 + a * 32 + 32] for a in range(4) for m in range(2)], axis=0
    )


def split(x):
    hi = x.astype(jnp.bfloat16)
    return hi, (x - hi.astype(jnp.float32)).astype(jnp.bfloat16)


def slot_of(step, where):
    other = (step + where[1]) % 2
    mine = where[1] + other * (1 - 2 * (where[1] % 2))
    return ((mine - step + 8) % 8) // 2, other


def leading_kernel(
    where_ref, g0, g1, g2, g3, own_ref, corner_ref, out_ref, lead, inv_dn, scl_dn, inv_ac, scl_ac
):
    row_index = where_ref[0]
    col_index = where_ref[1]
    for dx, piece in enumerate((g0, g1, g2, g3)):
        for dy in range(4):
            r = (row_index // 4 + 4 - dy) % 4 * 4 + (row_index % 4 + 4 - dx) % 4
            lead[pl.ds(pl.multiple_of(r * 32, 32), 32), :] = piece[dy]

    def norms(x, start, count):
        n = norms_down(x)
        r = lax.rsqrt(n)
        inv_dn[start : start + count, :] = r
        scl_dn[start : start + count, :] = n * r * SCALE

    x = lead[...]
    norms(x, 0, PANEL)
    n = norms_across(x)
    r = lax.rsqrt(n)
    inv_ac[...] = r
    scl_ac[...] = n * r * SCALE
    norms(own_ref[...], PANEL, 128)
    chunk = 64
    for jb in range(4):
        lanes = slice(jb * 128, jb * 128 + 128)
        cols = lead[lanes, :]
        corner_ref[jb * 128 :, lanes] = dot_nt(lead[jb * 128 :, :], cols)
        out_ref[:, lanes] = dot_nt(own_ref[...], cols)
        inv_c = inv_ac[0:1, lanes]
        scl_c = scl_ac[0:1, lanes]

        def body(step, carry, ref, base):
            start = pl.multiple_of(step * chunk, chunk)
            rows = pl.ds(start, chunk)
            down = pl.ds(start + base, chunk)
            raw = ref[rows, lanes] * inv_dn[down, :] * inv_c
            local = start + lax.broadcasted_iota(jnp.int32, (chunk, 128), 0)
            if base:
                block = local // 32
                local = (col_index * 4 + block) * PANEL + row_index * 32 + local - block * 32
            col_id = jb * 128 + lax.broadcasted_iota(jnp.int32, (chunk, 128), 1)
            on_diag = local == col_id
            tangent = tangent_of(jnp.where(on_diag, 1.0, raw), raw)
            ref[rows, lanes] = tangent * scl_dn[down, :] * scl_c + jnp.where(on_diag, 1.0, 0.0)
            return carry

        lax.fori_loop(0, 128 // chunk, functools.partial(body, ref=out_ref, base=PANEL), 0, unroll=2)
        lax.fori_loop(
            jb * (128 // chunk), PANEL // chunk, functools.partial(body, ref=corner_ref, base=0), 0
        )


def leading(where, pieces, own):
    vmem = pl.BlockSpec(memory_space=pltpu.VMEM)
    return pl.pallas_call(
        leading_kernel,
        out_shape=(
            jax.ShapeDtypeStruct((PANEL, PANEL), jnp.float32),
            jax.ShapeDtypeStruct((128, PANEL), jnp.float32),
        ),
        in_specs=[pl.BlockSpec(memory_space=pltpu.SMEM)] + [vmem] * 5,
        out_specs=(vmem, vmem),
        scratch_shapes=[
            pltpu.VMEM((PANEL, FEAT), jnp.bfloat16),
            pltpu.VMEM((PANEL + 128, 128), jnp.float32),
            pltpu.VMEM((PANEL + 128, 128), jnp.float32),
            pltpu.VMEM((8, PANEL), jnp.float32),
            pltpu.VMEM((8, PANEL), jnp.float32),
        ],
        name="leading",
        cost_estimate=pl.CostEstimate(flops=int(8e9), bytes_accessed=int(2e6), transcendentals=0),
    )(where, *pieces, own)


def factor_kernel(corner_ref, out_ref, mat, work):
    eye = jnp.where(
        lax.broadcasted_iota(jnp.int32, (128, 128), 1)
        == lax.broadcasted_iota(jnp.int32, (128, 128), 0),
        1.0,
        0.0,
    )
    sub8 = lax.broadcasted_iota(jnp.int32, (8, 256), 0)
    mat[:PANEL, :] = corner_ref[...]
    mat[PANEL:, :] = jnp.zeros((PANEL, PANEL), jnp.float32)

    def eliminate(kb):
        lanes = slice(kb * 128, kb * 128 + 128)
        linv = work[:, 128:]
        inverse = jnp.transpose(linv)
        top = PANEL + kb * 128
        if kb:
            upper = dot_nt(mat[PANEL:top, lanes], linv, HIGH)
            mat[PANEL:top, lanes] = upper
            upper = jnp.concatenate([upper, inverse], axis=0)
        else:
            upper = inverse
        mat[top : top + 128, lanes] = inverse
        if kb < 3:
            below = (kb + 1) * 128
            solved = dot_nt(mat[below:PANEL, lanes], linv, HIGH)
            mat[below:PANEL, below:] = mat[below:PANEL, below:] - dot_nt(solved, solved, HIGH)
            mat[PANEL : top + 128, below:] = mat[PANEL : top + 128, below:] - dot_nt(
                upper, solved, HIGH
            )

    def column(kb, carry):
        first = pl.multiple_of(kb * 128, 128)
        work[:, :128] = mat[pl.ds(first, 128), pl.ds(first, 128)]
        work[:, 128:] = eye
        for jb in range(16):
            j = jb * 8
            rows = [jnp.broadcast_to(work[j + p : j + p + 1, :], (8, 256)) for p in range(8)]
            e = [[None] * 8 for _ in range(8)]
            for p in range(8):
                for q in range(p, 8):
                    e[p][q] = jnp.broadcast_to(rows[p][:, j + q : j + q + 1], (8, 128))
            block = None
            done = []
            for p in range(8):
                rinv = lax.rsqrt(e[p][p])
                for q in range(p + 1, 8):
                    e[p][q] = e[p][q] * rinv
                for q in range(p + 1, 8):
                    for s in range(q, 8):
                        e[q][s] = e[q][s] - e[p][q] * e[p][s]
                row = rows[p]
                for m in range(p):
                    row = row - jnp.concatenate([e[m][p]] * 2, axis=1) * done[m]
                row = row * jnp.concatenate([rinv] * 2, axis=1)
                done.append(row)
                block = row if p == 0 else jnp.where(sub8 == p, row, block)
            work[j : j + 8, :] = block
            if jb < 15:
                outer = lax.dot_general(
                    block[:, :128], block, (((0,), (0,)), ((), ())), precision=HIGH,
                    preferred_element_type=jnp.float32,
                )
                work[j + 8 :, :] = work[j + 8 :, :] - outer[j + 8 :, :]
        for n in range(4):
            pl.when(kb == n)(functools.partial(eliminate, n))
        return carry

    lax.fori_loop(0, 4, column, 0)
    hi, lo = split(mat[PANEL:, :])
    out_ref[:, :PANEL] = hi
    out_ref[:, PANEL:] = lo


def factor(corner):
    return pl.pallas_call(
        factor_kernel,
        out_shape=jax.ShapeDtypeStruct((PANEL, 2 * PANEL), jnp.bfloat16),
        in_specs=[pl.BlockSpec(memory_space=pltpu.VMEM)],
        out_specs=pl.BlockSpec(memory_space=pltpu.VMEM),
        scratch_shapes=[
            pltpu.VMEM((2 * PANEL, PANEL), jnp.float32),
            pltpu.VMEM((128, 256), jnp.float32),
        ],
        name="factor",
        cost_estimate=pl.CostEstimate(flops=int(25e9), bytes_accessed=int(2e6), transcendentals=0),
    )(corner)


def tiles_kernel(
    where_ref, rows_ref, cols_ref, out_ref, cols, gram, inv_ac, scl_ac, inv_dn, scl_dn
):
    step = pl.program_id(0)
    row_index = where_ref[0]
    col_index = where_ref[1]
    count = cols_ref.shape[0] // TILE_C

    @pl.when(step == 0)
    def _():
        def body(t, carry):
            rows = pl.ds(pl.multiple_of(t * TILE_C, TILE_C), TILE_C)
            x = in_order(cols_ref[rows, :])
            cols[rows, :] = x
            n = norms_across(x)
            r = lax.rsqrt(n)
            inv_ac[t] = r
            scl_ac[t] = n * r * SCALE
            return carry

        lax.fori_loop(0, count, body, 0)

    x = rows_ref[...]
    n = norms_down(x)
    r = lax.rsqrt(n)
    inv_dn[...] = r
    scl_dn[...] = n * r * SCALE
    chunk = 32

    def product(t, slot):
        start = pl.multiple_of(t * TILE_C, TILE_C)
        gram[slot] = dot_nt(x, cols[pl.ds(start, TILE_C), :])

    def piece(t, slot, k):
        rows = slice(k * chunk, k * chunk + chunk)
        inv_r = jnp.concatenate([inv_dn[rows, :]] * 2, axis=1)
        scl_r = jnp.concatenate([scl_dn[rows, :]] * 2, axis=1)
        raw = gram[slot, rows, :] * inv_r * inv_ac[t][0:1]
        value = tangent_of(raw, raw) * scl_r * scl_ac[t][0:1]
        out_ref[rows, pl.ds(pl.multiple_of(t * TILE_C, TILE_C), TILE_C)] = value

    product(0, 0)

    def tile(t, carry):
        slot = t % 2
        product(t + 1, 1 - slot)
        for k in range(TILE_R // chunk):
            piece(t, slot, k)
        return carry

    lax.fori_loop(0, step, tile, 0)

    slot = step % 2
    for half in range(2):
        width = 128 * (half + 1)
        rows = slice(half * 64, half * 64 + 64)
        for lane in range(half + 1):
            lanes = slice(lane * 128, lane * 128 + 128)
            raw = gram[slot, rows, lanes] * inv_dn[rows, :] * inv_ac[step][0:1, lanes]
            u = half * 64 + lax.broadcasted_iota(jnp.int32, (64, 128), 0)
            v = lane * 128 + lax.broadcasted_iota(jnp.int32, (64, 128), 1)
            row_id = u // 32 * PANEL + row_index * 32 + u % 32
            col_id = v // 64 * PANEL + col_index * 64 + v % 64
            on_diag = row_id == col_id
            tangent = tangent_of(jnp.where(on_diag, 1.0, raw), raw)
            value = tangent * scl_dn[rows, :] * scl_ac[step][0:1, lanes]
            value = value + jnp.where(on_diag, 1.0, 0.0)
            first = pl.multiple_of(step * TILE_C + lane * 128, 128)
            out_ref[rows, pl.ds(first, 128)] = value


def tiles(where, rows, cols):
    n_rows, n_cols = rows.shape[0], cols.shape[0]
    return pl.pallas_call(
        tiles_kernel,
        out_shape=jax.ShapeDtypeStruct((n_rows, n_cols), jnp.float32),
        grid_spec=pltpu.PrefetchScalarGridSpec(
            num_scalar_prefetch=1,
            grid=(n_rows // TILE_R,),
            in_specs=[
                pl.BlockSpec((TILE_R, FEAT), lambda i, where: (i, 0)),
                pl.BlockSpec((n_cols, FEAT), lambda i, where: (0, 0)),
            ],
            out_specs=pl.BlockSpec((TILE_R, n_cols), lambda i, where: (i, 0)),
            scratch_shapes=[
                pltpu.VMEM((n_cols, FEAT), jnp.bfloat16),
                pltpu.VMEM((2, TILE_R, TILE_C), jnp.float32),
                pltpu.VMEM((n_cols // TILE_C, 8, TILE_C), jnp.float32),
                pltpu.VMEM((n_cols // TILE_C, 8, TILE_C), jnp.float32),
                pltpu.VMEM((TILE_R, 128), jnp.float32),
                pltpu.VMEM((TILE_R, 128), jnp.float32),
            ],
        ),
        name="tiles",
        cost_estimate=pl.CostEstimate(flops=int(30e9), bytes_accessed=int(12e6), transcendentals=0),
    )(where, rows, cols)


def solve(x, v_ref):
    hi, lo = split(x)
    parts = []
    for start in range(0, PANEL, 256):
        depth = start + 256
        v_hi = v_ref[:depth, start:depth]
        v_lo = v_ref[:depth, PANEL + start : PANEL + depth]
        left = jnp.concatenate([hi[:, :depth], hi[:, :depth], lo[:, :depth]], axis=1)
        right = jnp.concatenate([v_hi, v_lo, v_hi], axis=0)
        parts.append(jnp.dot(left, right, preferred_element_type=jnp.float32))
    return jnp.concatenate(parts, axis=1)


def update_kernel(where_ref, kernel_ref, *refs):
    near_refs, (cols_ref, v_ref, out_ref, both_c, left) = refs[:4], refs[4:]
    step = pl.program_id(0)
    row_index = where_ref[0]
    col_index = where_ref[1]
    count = cols_ref.shape[0] // TILE_C

    @pl.when(step == 0)
    def _():
        def body(t, carry):
            rows = pl.ds(pl.multiple_of(t * TILE_C, TILE_C), TILE_C)
            hi, lo = split(solve(in_order(cols_ref[rows, :]), v_ref))
            both_c[rows, :PANEL] = hi
            both_c[rows, PANEL:] = lo
            return carry

        lax.fori_loop(0, count, body, 0)

    pieces = []
    for half in range(2):
        _, other = slot_of(step * 2 + half, where_ref)
        pieces.append(jnp.where(other == 1, near_refs[2 * half + 1][0], near_refs[2 * half][0]))
    solved = solve(jnp.concatenate(pieces, axis=0), v_ref)
    hi_r, lo_r = split(solved)
    all_r = jnp.concatenate([hi_r, hi_r, lo_r], axis=1)
    for n in range(4):
        left[n] = solved[:, n * 128 : n * 128 + 128]
    tall = 2 * TILE_R

    for t in range(count):
        lanes = slice(t * TILE_C, t * TILE_C + TILE_C)

        @pl.when(step < t // 2)
        def _():
            out_ref[:, lanes] = jnp.zeros((tall, TILE_C), jnp.float32)

        @pl.when(step >= t // 2)
        def _():
            all_c = jnp.concatenate([both_c[lanes, :], both_c[lanes, :PANEL]], axis=1)
            value = kernel_ref[:, lanes] - dot_nt(all_r, all_c)
            if t == 0:
                mine = left[col_index // 2]
                mine = jnp.where(col_index % 2 == 1, pltpu.roll(mine, 64, 1), mine)
                mine = jnp.concatenate([mine, mine], axis=1)
                v = lax.broadcasted_iota(jnp.int32, (tall, TILE_C), 1)
                value = jnp.where(v < 64, mine, value)
            out_ref[:, lanes] = value

            @pl.when(step == t // 2)
            def _():
                s = lax.broadcasted_iota(jnp.int32, (tall, TILE_C), 0)
                v = lax.broadcasted_iota(jnp.int32, (tall, TILE_C), 1)
                row_id = (step * 8 + s // 32) * PANEL + row_index * 32 + s % 32
                col_id = (t * 4 + v // 64) * PANEL + col_index * 64 + v % 64
                out_ref[:, lanes] = jnp.where(row_id >= col_id, out_ref[:, lanes], 0.0)


def update(where, kernel, near, far, cols, v):
    n_rows, n_cols = kernel.shape
    piece = (1, TILE_R, PANEL)
    halves = [
        pl.BlockSpec(piece, lambda i, where, half=half: (slot_of(2 * i + half, where)[0], 0, 0))
        for half in (0, 0, 1, 1)
    ]
    return pl.pallas_call(
        update_kernel,
        out_shape=jax.ShapeDtypeStruct((n_rows, n_cols), jnp.float32),
        grid_spec=pltpu.PrefetchScalarGridSpec(
            num_scalar_prefetch=1,
            grid=(n_rows // (2 * TILE_R),),
            in_specs=[pl.BlockSpec((2 * TILE_R, n_cols), lambda i, where: (i, 0))]
            + halves
            + [
                pl.BlockSpec((n_cols, PANEL), lambda i, where: (0, 0)),
                pl.BlockSpec((PANEL, 2 * PANEL), lambda i, where: (0, 0)),
            ],
            out_specs=pl.BlockSpec((2 * TILE_R, n_cols), lambda i, where: (i, 0)),
            scratch_shapes=[
                pltpu.VMEM((n_cols, 2 * PANEL), jnp.bfloat16),
                pltpu.VMEM((4, 2 * TILE_R, 128), jnp.float32),
            ],
        ),
        name="update",
        cost_estimate=pl.CostEstimate(flops=int(6e9), bytes_accessed=int(20e6), transcendentals=0),
    )(where, kernel, near, far, near, far, cols, v)


def send(x, target):
    pairs = [(r * 8 + k, target(r, k)) for r in range(16) for k in range(8)]
    return lax.ppermute(x, ("row", "col"), [(s, t[0] * 8 + t[1]) for s, t in pairs if t])


def along_z(d):
    return lambda r, k: (r, (k + 2 * d) % 8)


def along_y(d):
    return lambda r, k: ((r + 4 * d) % 16, k)


def along_x(d):
    return lambda r, k: (r // 4 * 4 + (r + d) % 4, k)


def other_core(r, k):
    return r, k ^ 1


def across(r, k):
    return k * 2 + r % 2, r // 2


def to_all(x):
    head = jnp.where(lax.axis_index("col") == 0, x[:32], jnp.zeros((32, FEAT), x.dtype))
    for bit in (1, 2, 4):
        head = head + send(head, lambda r, k: (r, k | bit) if k < bit else None)
    column = jnp.stack([head] + [send(head, along_y(d)) for d in (1, 2, 3)])
    return [column] + [send(column, along_x(d)) for d in (1, 2, 3)]


def per_device(samples):
    where = jnp.stack([lax.axis_index("row"), lax.axis_index("col")]).astype(jnp.int32)
    row_feats = lax.all_gather(samples, "col", axis=0, tiled=True)
    moved = send(samples, across)
    moved, pieces = lax.optimization_barrier((moved, to_all(samples)))
    col_feats = lax.all_gather(moved, "row", axis=0, tiled=True)
    corner, own = leading(where, pieces, samples)
    moved = send(own, across)
    shifted = [send(own, along_z(d)) for d in (1, 2, 3)]
    v = factor(corner)
    moved, shifted, v = lax.optimization_barrier((moved, shifted, v))
    own_cols = lax.all_gather(moved, "row", axis=0, tiled=True)
    near = jnp.stack([own] + shifted)
    far = send(near, other_core)
    kernel = tiles(where, row_feats, col_feats)
    return update(where, kernel, near, far, own_cols, v)


def solution(mesh):
    return jax.shard_map(
        per_device,
        mesh=mesh,
        in_specs=(P(("row", "col"), None),),
        out_specs=P("row", "col"),
        check_vma=False,
    )
```

```python
import functools
import math

import jax
import jax.numpy as jnp
import numpy as np
from jax import lax
from jax.experimental import pallas as pl
from jax.experimental.pallas import tpu as pltpu
from jax.sharding import PartitionSpec as P

FEAT = 768
PANEL = 512
LAYERS = 8
TILE_R = 128
TILE_C = 256

ARC = (
    (1.570796265e+00, -9.999884905e-01, 7.850416849e-01, -6.623695706e-01, 5.625094387e-01, -4.372503233e-01, 2.693842319e-01, -1.086155413e-01, 2.049311747e-02),
    (1.570796265e+00, -9.999884905e-01, 7.850416849e-01, -6.623695706e-01, 5.625094387e-01, -4.372503233e-01, 2.693842319e-01, -1.086155413e-01, 2.049311747e-02),
    (1.570326531e+00, -9.935370566e-01, 7.471319178e-01, -5.376914312e-01, 3.111383121e-01, -1.187027540e-01, 2.133516172e-02),
    (1.567898155e+00, -9.719742948e-01, 6.682907781e-01, -3.857788817e-01, 1.484597498e-01, -2.689621130e-02),
    (1.566642297e+00, -9.635808948e-01, 6.460403822e-01, -3.565340200e-01, 1.294006162e-01, -2.196850873e-02),
    (1.558633208e+00, -9.141686374e-01, 5.246089379e-01, -2.079489415e-01, 3.887608390e-02),
    (1.557122831e+00, -9.070176865e-01, 5.119586953e-01, -1.980387362e-01, 3.597512846e-02),
    (1.555954084e+00, -9.016562063e-01, 5.027575168e-01, -1.910373211e-01, 3.398202014e-02),
)


def scales():
    out = [np.float32(1.0)]
    for _ in range(LAYERS):
        out.append(np.float32(np.float32(math.pi) * out[-1]))
    return out


KAPPA = scales()


def polynomial(coefs, c):
    value = c * coefs[-1] + coefs[-2]
    for coef in coefs[-3::-1]:
        value = value * c + coef
    return value


def tangent_of(cosine, tangent):
    for layer in range(LAYERS):
        kappa = KAPPA[layer]
        coefs = [float(a / np.float64(kappa) ** (k + 1)) for k, a in enumerate(ARC[layer])]
        size = jnp.abs(cosine) if layer == 0 else cosine
        square = jnp.maximum(float(np.float32(kappa * kappa)) - size * size, 1e-30)
        sine = square * lax.rsqrt(square)
        angle = sine * polynomial(coefs, size)
        rest = math.pi - angle
        if layer == 0:
            rest = jnp.where(cosine < 0.0, angle, rest)
        cosine = sine + rest * cosine
        tangent = cosine + rest * tangent
    return tangent


def squares(x):
    xf = x.astype(jnp.float32)
    sq = xf * xf
    hi = sq.astype(jnp.bfloat16)
    lo = (sq - hi.astype(jnp.float32)).astype(jnp.bfloat16)
    return hi, lo


def dot_nt(a, b, precision=None):
    return lax.dot_general(
        a, b, (((1,), (1,)), ((), ())), precision=precision, preferred_element_type=jnp.float32
    )


def norms_down(x):
    hi, lo = squares(x)
    ones = jnp.ones((128, x.shape[1]), jnp.bfloat16)
    return dot_nt(hi, ones) + dot_nt(lo, ones)


def norms_across(x):
    hi, lo = squares(x)
    ones = jnp.ones((16, x.shape[1]), jnp.bfloat16)
    return (dot_nt(ones, hi) + dot_nt(ones, lo))[:8]


SCALE = 1.0 / math.sqrt(FEAT * (LAYERS + 1.0) * float(KAPPA[LAYERS]))


def in_order(x):
    return jnp.concatenate(
        [x[m * 128 + a * 32 : m * 128 + a * 32 + 32] for a in range(4) for m in range(2)], axis=0
    )


def split(x):
    hi = x.astype(jnp.bfloat16)
    return hi, (x - hi.astype(jnp.float32)).astype(jnp.bfloat16)


def slot_of(step, where):
    other = (step + where[1]) % 2
    mine = where[1] + other * (1 - 2 * (where[1] % 2))
    return ((mine - step + 8) % 8) // 2, other


def leading_kernel(
    where_ref, g0, g1, g2, g3, own_ref, corner_ref, out_ref, lead, inv_dn, scl_dn, inv_ac, scl_ac
):
    row_index = where_ref[0]
    col_index = where_ref[1]
    for dx, piece in enumerate((g0, g1, g2, g3)):
        for dy in range(4):
            r = (row_index // 4 + 4 - dy) % 4 * 4 + (row_index % 4 + 4 - dx) % 4
            lead[pl.ds(pl.multiple_of(r * 32, 32), 32), :] = piece[dy]

    def norms(x, start, count):
        n = norms_down(x)
        r = lax.rsqrt(n)
        inv_dn[start : start + count, :] = r
        scl_dn[start : start + count, :] = n * r * SCALE

    x = lead[...]
    norms(x, 0, PANEL)
    n = norms_across(x)
    r = lax.rsqrt(n)
    inv_ac[...] = r
    scl_ac[...] = n * r * SCALE
    norms(own_ref[...], PANEL, 128)
    chunk = 64
    for jb in range(4):
        lanes = slice(jb * 128, jb * 128 + 128)
        cols = lead[lanes, :]
        corner_ref[jb * 128 :, lanes] = dot_nt(lead[jb * 128 :, :], cols)
        out_ref[:, lanes] = dot_nt(own_ref[...], cols)
        inv_c = inv_ac[0:1, lanes]
        scl_c = scl_ac[0:1, lanes]

        def body(step, carry, ref, base):
            start = pl.multiple_of(step * chunk, chunk)
            rows = pl.ds(start, chunk)
            down = pl.ds(start + base, chunk)
            raw = ref[rows, lanes] * inv_dn[down, :] * inv_c
            local = start + lax.broadcasted_iota(jnp.int32, (chunk, 128), 0)
            if base:
                block = local // 32
                local = (col_index * 4 + block) * PANEL + row_index * 32 + local - block * 32
            col_id = jb * 128 + lax.broadcasted_iota(jnp.int32, (chunk, 128), 1)
            on_diag = local == col_id
            tangent = tangent_of(jnp.where(on_diag, 1.0, raw), raw)
            ref[rows, lanes] = tangent * scl_dn[down, :] * scl_c + jnp.where(on_diag, 1.0, 0.0)
            return carry

        lax.fori_loop(0, 128 // chunk, functools.partial(body, ref=out_ref, base=PANEL), 0, unroll=2)
        lax.fori_loop(
            jb * (128 // chunk), PANEL // chunk, functools.partial(body, ref=corner_ref, base=0), 0
        )


def leading(where, pieces, own):
    vmem = pl.BlockSpec(memory_space=pltpu.VMEM)
    return pl.pallas_call(
        leading_kernel,
        out_shape=(
            jax.ShapeDtypeStruct((PANEL, PANEL), jnp.float32),
            jax.ShapeDtypeStruct((128, PANEL), jnp.float32),
        ),
        in_specs=[pl.BlockSpec(memory_space=pltpu.SMEM)] + [vmem] * 5,
        out_specs=(vmem, vmem),
        scratch_shapes=[
            pltpu.VMEM((PANEL, FEAT), jnp.bfloat16),
            pltpu.VMEM((PANEL + 128, 128), jnp.float32),
            pltpu.VMEM((PANEL + 128, 128), jnp.float32),
            pltpu.VMEM((8, PANEL), jnp.float32),
            pltpu.VMEM((8, PANEL), jnp.float32),
        ],
        name="leading",
        cost_estimate=pl.CostEstimate(flops=int(8e9), bytes_accessed=int(2e6), transcendentals=0),
    )(where, *pieces, own)


def thirds(x):
    wide = x.astype(jnp.bfloat16).astype(jnp.float32)
    rest = x - wide
    middle = rest.astype(jnp.bfloat16).astype(jnp.float32)
    return wide, middle, rest - middle


def six_products(x, y, axis):
    a, b, c = thirds(x)
    d, e, f = (a, b, c) if y is x else thirds(y)
    left = jnp.concatenate([a, a, b, a, b, c], axis=axis)
    right = jnp.concatenate([d, e, d, f, e, d], axis=axis)
    return left.astype(jnp.bfloat16), right.astype(jnp.bfloat16)


def product_nt(x, y):
    return dot_nt(*six_products(x, y, 1))


def factor_kernel(corner_ref, out_ref, mat, work):
    eye = jnp.where(
        lax.broadcasted_iota(jnp.int32, (128, 128), 1)
        == lax.broadcasted_iota(jnp.int32, (128, 128), 0),
        1.0,
        0.0,
    )
    sub8 = lax.broadcasted_iota(jnp.int32, (8, 256), 0)
    mat[:PANEL, :] = corner_ref[...]
    mat[PANEL:, :] = jnp.zeros((PANEL, PANEL), jnp.float32)

    def eliminate(kb):
        lanes = slice(kb * 128, kb * 128 + 128)
        linv = work[:, 128:]
        inverse = jnp.transpose(linv)
        top = PANEL + kb * 128
        if kb:
            upper = product_nt(mat[PANEL:top, lanes], linv)
            mat[PANEL:top, lanes] = upper
            upper = jnp.concatenate([upper, inverse], axis=0)
        else:
            upper = inverse
        mat[top : top + 128, lanes] = inverse
        if kb < 3:
            below = (kb + 1) * 128
            solved = product_nt(mat[below:PANEL, lanes], linv)
            mat[below:PANEL, below:] = mat[below:PANEL, below:] - product_nt(solved, solved)
            mat[PANEL : top + 128, below:] = mat[PANEL : top + 128, below:] - product_nt(
                upper, solved
            )

    def column(kb, carry):
        first = pl.multiple_of(kb * 128, 128)
        work[:, :128] = mat[pl.ds(first, 128), pl.ds(first, 128)]
        work[:, 128:] = eye
        rows = [jnp.broadcast_to(work[p : p + 1, :], (8, 256)) for p in range(8)]
        for jb in range(16):
            j = jb * 8
            e = [[None] * 8 for _ in range(8)]
            for p in range(8):
                for q in range(p, 8):
                    e[p][q] = jnp.broadcast_to(rows[p][:, j + q : j + q + 1], (8, 128))
            block = None
            done = []
            for p in range(8):
                rinv = lax.rsqrt(e[p][p])
                for q in range(p + 1, 8):
                    e[p][q] = e[p][q] * rinv
                for q in range(p + 1, 8):
                    for s in range(q, 8):
                        e[q][s] = e[q][s] - e[p][q] * e[p][s]
                row = rows[p]
                for m in range(p):
                    row = row - jnp.concatenate([e[m][p]] * 2, axis=1) * done[m]
                row = row * jnp.concatenate([rinv] * 2, axis=1)
                done.append(row)
                block = row if p == 0 else jnp.where(sub8 == p, row, block)
            work[j : j + 8, :] = block
            if jb < 15:
                rows = []
                for p in range(j + 8, j + 16):
                    row = jnp.broadcast_to(work[p : p + 1, :], (8, 256))
                    for m in range(8):
                        factor_m = jnp.broadcast_to(done[m][:, p : p + 1], (8, 128))
                        row = row - jnp.concatenate([factor_m] * 2, axis=1) * done[m]
                    rows.append(row)
            if jb < 14:
                left, right = six_products(block, block, 0)
                outer = lax.dot_general(
                    left[:, :128], right, (((0,), (0,)), ((), ())), preferred_element_type=jnp.float32
                )
                work[j + 16 :, :] = work[j + 16 :, :] - outer[j + 16 :, :]
        for n in range(4):
            pl.when(kb == n)(functools.partial(eliminate, n))
        return carry

    lax.fori_loop(0, 4, column, 0)
    hi, lo = split(mat[PANEL:, :])
    out_ref[:, :PANEL] = hi
    out_ref[:, PANEL:] = lo


def factor(corner):
    return pl.pallas_call(
        factor_kernel,
        out_shape=jax.ShapeDtypeStruct((PANEL, 2 * PANEL), jnp.bfloat16),
        in_specs=[pl.BlockSpec(memory_space=pltpu.VMEM)],
        out_specs=pl.BlockSpec(memory_space=pltpu.VMEM),
        scratch_shapes=[
            pltpu.VMEM((2 * PANEL, PANEL), jnp.float32),
            pltpu.VMEM((128, 256), jnp.float32),
        ],
        name="factor",
        cost_estimate=pl.CostEstimate(flops=int(25e9), bytes_accessed=int(2e6), transcendentals=0),
    )(corner)


def tiles_kernel(
    where_ref, near_ref, far_ref, cols_ref, out_ref, cols, gram, inv_ac, scl_ac, inv_dn, scl_dn
):
    step = pl.program_id(0)
    row_index = where_ref[0]
    col_index = where_ref[1]
    count = cols_ref.shape[0] // TILE_C

    @pl.when(step == 0)
    def _():
        def body(t, carry):
            rows = pl.ds(pl.multiple_of(t * TILE_C, TILE_C), TILE_C)
            x = in_order(cols_ref[rows, :])
            cols[rows, :] = x
            n = norms_across(x)
            r = lax.rsqrt(n)
            inv_ac[t] = r
            scl_ac[t] = n * r * SCALE
            return carry

        lax.fori_loop(0, count, body, 0)

    _, other = slot_of(step, where_ref)
    x = jnp.where(other == 1, far_ref[0], near_ref[0])
    n = norms_down(x)
    r = lax.rsqrt(n)
    inv_dn[...] = r
    scl_dn[...] = n * r * SCALE
    chunk = 32

    def product(t):
        start = pl.multiple_of(t * TILE_C, TILE_C)
        gram[...] = dot_nt(x, cols[pl.ds(start, TILE_C), :])

    def piece(t, k):
        rows = slice(k * chunk, k * chunk + chunk)
        inv_r = jnp.concatenate([inv_dn[rows, :]] * 2, axis=1)
        scl_r = jnp.concatenate([scl_dn[rows, :]] * 2, axis=1)
        raw = gram[rows, :] * inv_r * inv_ac[t][0:1]
        value = tangent_of(raw, raw) * scl_r * scl_ac[t][0:1]
        out_ref[rows, pl.ds(pl.multiple_of(t * TILE_C, TILE_C), TILE_C)] = value

    product(0)

    def tile(t, carry):
        for k in range(TILE_R // chunk):
            piece(t, k)
        product(t + 1)
        return carry

    lax.fori_loop(0, step, tile, 0)

    for half in range(2):
        rows = slice(half * 64, half * 64 + 64)
        for lane in range(half + 1):
            lanes = slice(lane * 128, lane * 128 + 128)
            raw = gram[rows, lanes] * inv_dn[rows, :] * inv_ac[step][0:1, lanes]
            u = half * 64 + lax.broadcasted_iota(jnp.int32, (64, 128), 0)
            v = lane * 128 + lax.broadcasted_iota(jnp.int32, (64, 128), 1)
            row_id = u // 32 * PANEL + row_index * 32 + u % 32
            col_id = v // 64 * PANEL + col_index * 64 + v % 64
            on_diag = row_id == col_id
            tangent = tangent_of(jnp.where(on_diag, 1.0, raw), raw)
            value = tangent * scl_dn[rows, :] * scl_ac[step][0:1, lanes]
            value = value + jnp.where(on_diag, 1.0, 0.0)
            first = pl.multiple_of(step * TILE_C + lane * 128, 128)
            out_ref[rows, pl.ds(first, 128)] = value


def tiles(where, near, far, cols):
    n_rows, n_cols = 8 * TILE_R, cols.shape[0]
    piece = pl.BlockSpec((1, TILE_R, FEAT), lambda i, where: (slot_of(i, where)[0], 0, 0))
    return pl.pallas_call(
        tiles_kernel,
        out_shape=jax.ShapeDtypeStruct((n_rows, n_cols), jnp.float32),
        grid_spec=pltpu.PrefetchScalarGridSpec(
            num_scalar_prefetch=1,
            grid=(n_rows // TILE_R,),
            in_specs=[
                piece,
                piece,
                pl.BlockSpec((n_cols, FEAT), lambda i, where: (0, 0)),
            ],
            out_specs=pl.BlockSpec((TILE_R, n_cols), lambda i, where: (i, 0)),
            scratch_shapes=[
                pltpu.VMEM((n_cols, FEAT), jnp.bfloat16),
                pltpu.VMEM((TILE_R, TILE_C), jnp.float32),
                pltpu.VMEM((n_cols // TILE_C, 8, TILE_C), jnp.float32),
                pltpu.VMEM((n_cols // TILE_C, 8, TILE_C), jnp.float32),
                pltpu.VMEM((TILE_R, 128), jnp.float32),
                pltpu.VMEM((TILE_R, 128), jnp.float32),
            ],
        ),
        name="tiles",
        cost_estimate=pl.CostEstimate(flops=int(30e9), bytes_accessed=int(12e6), transcendentals=0),
    )(where, near, far, cols)


def solve(x, v_ref):
    hi, lo = split(x)
    parts = []
    for start in range(0, PANEL, 256):
        depth = start + 256
        v_hi = v_ref[:depth, start:depth]
        v_lo = v_ref[:depth, PANEL + start : PANEL + depth]
        left = jnp.concatenate([hi[:, :depth], hi[:, :depth], lo[:, :depth]], axis=1)
        right = jnp.concatenate([v_hi, v_lo, v_hi], axis=0)
        parts.append(jnp.dot(left, right, preferred_element_type=jnp.float32))
    return jnp.concatenate(parts, axis=1)


def update_kernel(where_ref, kernel_ref, *refs):
    near_refs, (cols_ref, v_ref, out_ref, both_c, left) = refs[:4], refs[4:]
    count = both_c.shape[0] // TILE_C
    step = pl.program_id(0) - count

    @pl.when(step < 0)
    def _():
        rows = pl.ds(pl.multiple_of(pl.program_id(0) * TILE_C, TILE_C), TILE_C)
        hi, lo = split(solve(in_order(cols_ref[...]), v_ref))
        both_c[rows, :PANEL] = hi
        both_c[rows, PANEL:] = lo

    @pl.when(step >= 0)
    def _():
        update_rows(where_ref, step, kernel_ref, near_refs, v_ref, out_ref, both_c, left)


def update_rows(where_ref, step, kernel_ref, near_refs, v_ref, out_ref, both_c, left):
    row_index = where_ref[0]
    col_index = where_ref[1]
    count = both_c.shape[0] // TILE_C
    pieces = []
    for half in range(2):
        _, other = slot_of(step * 2 + half, where_ref)
        pieces.append(jnp.where(other == 1, near_refs[2 * half + 1][0], near_refs[2 * half][0]))
    solved = solve(jnp.concatenate(pieces, axis=0), v_ref)
    hi_r, lo_r = split(solved)
    all_r = jnp.concatenate([hi_r, hi_r, lo_r], axis=1)
    for n in range(4):
        left[n] = solved[:, n * 128 : n * 128 + 128]
    tall = 2 * TILE_R

    for t in range(count):
        lanes = slice(t * TILE_C, t * TILE_C + TILE_C)

        @pl.when(step < t // 2)
        def _():
            out_ref[:, lanes] = jnp.zeros((tall, TILE_C), jnp.float32)

        @pl.when(step >= t // 2)
        def _():
            all_c = jnp.concatenate([both_c[lanes, :], both_c[lanes, :PANEL]], axis=1)
            value = kernel_ref[:, lanes] - dot_nt(all_r, all_c)
            if t == 0:
                mine = left[col_index // 2]
                mine = jnp.where(col_index % 2 == 1, pltpu.roll(mine, 64, 1), mine)
                mine = jnp.concatenate([mine, mine], axis=1)
                v = lax.broadcasted_iota(jnp.int32, (tall, TILE_C), 1)
                value = jnp.where(v < 64, mine, value)
            out_ref[:, lanes] = value

            @pl.when(step == t // 2)
            def _():
                s = lax.broadcasted_iota(jnp.int32, (tall, TILE_C), 0)
                v = lax.broadcasted_iota(jnp.int32, (tall, TILE_C), 1)
                row_id = (step * 8 + s // 32) * PANEL + row_index * 32 + s % 32
                col_id = (t * 4 + v // 64) * PANEL + col_index * 64 + v % 64
                out_ref[:, lanes] = jnp.where(row_id >= col_id, out_ref[:, lanes], 0.0)


def update(where, kernel, near, far, cols, v):
    n_rows, n_cols = kernel.shape
    piece = (1, TILE_R, PANEL)
    tall = 2 * TILE_R
    count = n_cols // TILE_C

    def step_of(i):
        return jnp.maximum(i - count, 0)

    halves = [
        pl.BlockSpec(
            piece, lambda i, where, half=half: (slot_of(2 * step_of(i) + half, where)[0], 0, 0)
        )
        for half in (0, 0, 1, 1)
    ]
    return pl.pallas_call(
        update_kernel,
        out_shape=jax.ShapeDtypeStruct((n_rows, n_cols), jnp.float32),
        grid_spec=pltpu.PrefetchScalarGridSpec(
            num_scalar_prefetch=1,
            grid=(count + n_rows // tall,),
            in_specs=[pl.BlockSpec((tall, n_cols), lambda i, where: (step_of(i), 0))]
            + halves
            + [
                pl.BlockSpec((TILE_C, PANEL), lambda i, where: (jnp.minimum(i, count - 1), 0)),
                pl.BlockSpec((PANEL, 2 * PANEL), lambda i, where: (0, 0)),
            ],
            out_specs=pl.BlockSpec((tall, n_cols), lambda i, where: (step_of(i), 0)),
            scratch_shapes=[
                pltpu.VMEM((n_cols, 2 * PANEL), jnp.bfloat16),
                pltpu.VMEM((4, tall, 128), jnp.float32),
            ],
        ),
        name="update",
        cost_estimate=pl.CostEstimate(flops=int(6e9), bytes_accessed=int(20e6), transcendentals=0),
    )(where, kernel, near, far, near, far, cols, v)


def send(x, target):
    pairs = [(r * 8 + k, target(r, k)) for r in range(16) for k in range(8)]
    return lax.ppermute(x, ("row", "col"), [(s, t[0] * 8 + t[1]) for s, t in pairs if t])


def along_z(d):
    return lambda r, k: (r, (k + 2 * d) % 8)


def along_y(d):
    return lambda r, k: ((r + 4 * d) % 16, k)


def along_x(d):
    return lambda r, k: (r // 4 * 4 + (r + d) % 4, k)


def other_core(r, k):
    return r, k ^ 1


def across(r, k):
    return k * 2 + r % 2, r // 2


def to_all(x, moved):
    head = jnp.where(lax.axis_index("col") == 0, x[:32], jnp.zeros((32, FEAT), x.dtype))
    for bit in (1, 2, 4):
        head = head + send(head, lambda r, k: (r, k | bit) if k < bit else None)
    head, moved = lax.optimization_barrier((head, moved))
    column = jnp.stack([head] + [send(head, along_y(d)) for d in (1, 2, 3)])
    return [column] + [send(column, along_x(d)) for d in (1, 2, 3)], moved


def along_column(x):
    return [send(x, along_z(d)) for d in (1, 2, 3)]


def per_device(samples):
    where = jnp.stack([lax.axis_index("row"), lax.axis_index("col")]).astype(jnp.int32)
    pieces, moved = to_all(samples, send(samples, across))
    col_feats = lax.all_gather(moved, "row", axis=0, tiled=True)
    pieces, later = lax.optimization_barrier((pieces, samples))
    feats = along_column(later)
    corner, own = leading(where, pieces, samples)
    feats, own, corner = lax.optimization_barrier((feats, own, corner))
    moved = send(own, across)
    near_feats = jnp.stack([samples] + feats)
    far_feats = send(near_feats, other_core)
    columns = along_column(own)
    v = factor(corner)
    moved, far_feats, columns, v = lax.optimization_barrier((moved, far_feats, columns, v))
    own_cols = lax.all_gather(moved, "row", axis=0, tiled=True)
    near = jnp.stack([own] + columns)
    far = send(near, other_core)
    kernel = tiles(where, near_feats, far_feats, col_feats)
    return update(where, kernel, near, far, own_cols, v)


def solution(mesh):
    return jax.shard_map(
        per_device,
        mesh=mesh,
        in_specs=(P(("row", "col"), None),),
        out_specs=P("row", "col"),
        check_vma=False,
    )
```

```python
import functools
import math

import jax
import jax.numpy as jnp
import numpy as np
from jax import lax
from jax.experimental import pallas as pl
from jax.experimental.pallas import tpu as pltpu
from jax.sharding import PartitionSpec as P

FEAT = 768
PANEL = 512
LAYERS = 8
TILE_R = 128
TILE_C = 256

ARC = (
    (1.570796265e+00, -9.999884905e-01, 7.850416849e-01, -6.623695706e-01, 5.625094387e-01, -4.372503233e-01, 2.693842319e-01, -1.086155413e-01, 2.049311747e-02),
    (1.570796265e+00, -9.999884905e-01, 7.850416849e-01, -6.623695706e-01, 5.625094387e-01, -4.372503233e-01, 2.693842319e-01, -1.086155413e-01, 2.049311747e-02),
    (1.570326531e+00, -9.935370566e-01, 7.471319178e-01, -5.376914312e-01, 3.111383121e-01, -1.187027540e-01, 2.133516172e-02),
    (1.567898155e+00, -9.719742948e-01, 6.682907781e-01, -3.857788817e-01, 1.484597498e-01, -2.689621130e-02),
    (1.566642297e+00, -9.635808948e-01, 6.460403822e-01, -3.565340200e-01, 1.294006162e-01, -2.196850873e-02),
    (1.558633208e+00, -9.141686374e-01, 5.246089379e-01, -2.079489415e-01, 3.887608390e-02),
    (1.557122831e+00, -9.070176865e-01, 5.119586953e-01, -1.980387362e-01, 3.597512846e-02),
    (1.555954084e+00, -9.016562063e-01, 5.027575168e-01, -1.910373211e-01, 3.398202014e-02),
)


def scales():
    out = [np.float32(1.0)]
    for _ in range(LAYERS):
        out.append(np.float32(np.float32(math.pi) * out[-1]))
    return out


KAPPA = scales()


def polynomial(coefs, c):
    value = c * coefs[-1] + coefs[-2]
    for coef in coefs[-3::-1]:
        value = value * c + coef
    return value


def tangent_of(cosine, tangent):
    for layer in range(LAYERS):
        kappa = KAPPA[layer]
        coefs = [float(a / np.float64(kappa) ** (k + 1)) for k, a in enumerate(ARC[layer])]
        size = jnp.abs(cosine) if layer == 0 else cosine
        square = jnp.maximum(float(np.float32(kappa * kappa)) - size * size, 1e-30)
        sine = square * lax.rsqrt(square)
        angle = sine * polynomial(coefs, size)
        rest = math.pi - angle
        if layer == 0:
            rest = jnp.where(cosine < 0.0, angle, rest)
        cosine = sine + rest * cosine
        tangent = cosine + rest * tangent
    return tangent


def squares(x):
    xf = x.astype(jnp.float32)
    sq = xf * xf
    hi = sq.astype(jnp.bfloat16)
    lo = (sq - hi.astype(jnp.float32)).astype(jnp.bfloat16)
    return hi, lo


def dot_nt(a, b, precision=None):
    return lax.dot_general(
        a, b, (((1,), (1,)), ((), ())), precision=precision, preferred_element_type=jnp.float32
    )


def norms_down(x):
    hi, lo = squares(x)
    ones = jnp.ones((128, x.shape[1]), jnp.bfloat16)
    return dot_nt(hi, ones) + dot_nt(lo, ones)


def norms_across(x):
    hi, lo = squares(x)
    ones = jnp.ones((16, x.shape[1]), jnp.bfloat16)
    return (dot_nt(ones, hi) + dot_nt(ones, lo))[:8]


SCALE = 1.0 / math.sqrt(FEAT * (LAYERS + 1.0) * float(KAPPA[LAYERS]))


def in_order(x):
    return jnp.concatenate(
        [x[m * 128 + a * 32 : m * 128 + a * 32 + 32] for a in range(4) for m in range(2)], axis=0
    )


def split(x):
    hi = x.astype(jnp.bfloat16)
    return hi, (x - hi.astype(jnp.float32)).astype(jnp.bfloat16)


def slot_of(step, where):
    other = (step + where[1]) % 2
    mine = where[1] + other * (1 - 2 * (where[1] % 2))
    return ((mine - step + 8) % 8) // 2, other


def down(x):
    n = norms_down(x)
    r = lax.rsqrt(n)
    return r, n * r * SCALE


def across_lanes(x):
    n = norms_across(x)
    r = lax.rsqrt(n)
    return r, n * r * SCALE


def leading_kernel(where_ref, g0, g1, g2, g3, own_ref, lead, out_ref, inv_dn, scl_dn, inv_ac, scl_ac):
    row_index = where_ref[0]
    col_index = where_ref[1]
    for dx, piece in enumerate((g0, g1, g2, g3)):
        for dy in range(4):
            r = (row_index // 4 + 4 - dy) % 4 * 4 + (row_index % 4 + 4 - dx) % 4
            lead[pl.ds(pl.multiple_of(r * 32, 32), 32), :] = piece[dy]
    own = own_ref[...]
    inv_dn[...], scl_dn[...] = down(own)
    inv_ac[...], scl_ac[...] = across_lanes(lead[...])
    for jb in range(4):
        lanes = slice(jb * 128, jb * 128 + 128)
        out_ref[:, lanes] = dot_nt(own, lead[lanes, :])
    chunk = 32

    def body(step, carry):
        rows = pl.ds(pl.multiple_of(step * chunk, chunk), chunk)
        block = (col_index * 4 + step) * PANEL + row_index * 32
        for jb in range(4):
            lanes = slice(jb * 128, jb * 128 + 128)
            raw = out_ref[rows, lanes] * inv_dn[rows, :] * inv_ac[0:1, lanes]
            row_id = block + lax.broadcasted_iota(jnp.int32, (chunk, 128), 0)
            col_id = jb * 128 + lax.broadcasted_iota(jnp.int32, (chunk, 128), 1)
            on_diag = row_id == col_id
            tangent = tangent_of(jnp.where(on_diag, 1.0, raw), raw)
            value = tangent * scl_dn[rows, :] * scl_ac[0:1, lanes]
            out_ref[rows, lanes] = value + jnp.where(on_diag, 1.0, 0.0)
        return carry

    lax.fori_loop(0, 128 // chunk, body, 0)


def leading(where, pieces, own):
    vmem = pl.BlockSpec(memory_space=pltpu.VMEM)
    return pl.pallas_call(
        leading_kernel,
        out_shape=(
            jax.ShapeDtypeStruct((PANEL, FEAT), jnp.bfloat16),
            jax.ShapeDtypeStruct((128, PANEL), jnp.float32),
        ),
        in_specs=[pl.BlockSpec(memory_space=pltpu.SMEM)] + [vmem] * 5,
        out_specs=(vmem, vmem),
        scratch_shapes=[
            pltpu.VMEM((128, 128), jnp.float32),
            pltpu.VMEM((128, 128), jnp.float32),
            pltpu.VMEM((8, PANEL), jnp.float32),
            pltpu.VMEM((8, PANEL), jnp.float32),
        ],
        name="leading",
        cost_estimate=pl.CostEstimate(flops=int(4e9), bytes_accessed=int(2e6), transcendentals=0),
    )(where, *pieces, own)


def corner_kernel(lead_ref, out_ref, inv_dn, scl_dn, inv_ac, scl_ac):
    x = lead_ref[...]
    inv_dn[...], scl_dn[...] = down(x)
    inv_ac[...], scl_ac[...] = across_lanes(x)
    chunk = 64
    for jb in range(4):
        lanes = slice(jb * 128, jb * 128 + 128)
        out_ref[jb * 128 :, lanes] = dot_nt(lead_ref[jb * 128 :, :], lead_ref[lanes, :])
        inv_c = inv_ac[0:1, lanes]
        scl_c = scl_ac[0:1, lanes]

        def body(step, carry):
            for half in range(2):
                start = pl.multiple_of(step * 128 + half * chunk, chunk)
                rows = pl.ds(start, chunk)
                raw = out_ref[rows, lanes] * inv_dn[rows, :] * inv_c
                row_id = start + lax.broadcasted_iota(jnp.int32, (chunk, 128), 0)
                col_id = jb * 128 + lax.broadcasted_iota(jnp.int32, (chunk, 128), 1)
                on_diag = row_id == col_id
                tangent = tangent_of(jnp.where(on_diag, 1.0, raw), raw)
                value = tangent * scl_dn[rows, :] * scl_c
                out_ref[rows, lanes] = value + jnp.where(on_diag, 1.0, 0.0)
            return carry

        lax.fori_loop(jb, 4, body, 0)


def corner_of(lead):
    vmem = pl.BlockSpec(memory_space=pltpu.VMEM)
    return pl.pallas_call(
        corner_kernel,
        out_shape=jax.ShapeDtypeStruct((PANEL, PANEL), jnp.float32),
        in_specs=[vmem],
        out_specs=vmem,
        scratch_shapes=[
            pltpu.VMEM((PANEL, 128), jnp.float32),
            pltpu.VMEM((PANEL, 128), jnp.float32),
            pltpu.VMEM((8, PANEL), jnp.float32),
            pltpu.VMEM((8, PANEL), jnp.float32),
        ],
        name="corner",
        cost_estimate=pl.CostEstimate(flops=int(6e9), bytes_accessed=int(2e6), transcendentals=0),
    )(lead)


def thirds(x):
    wide = x.astype(jnp.bfloat16).astype(jnp.float32)
    rest = x - wide
    middle = rest.astype(jnp.bfloat16).astype(jnp.float32)
    return wide, middle, rest - middle


def six_products(x, y, axis):
    a, b, c = thirds(x)
    d, e, f = (a, b, c) if y is x else thirds(y)
    left = jnp.concatenate([a, a, b, a, b, c], axis=axis)
    right = jnp.concatenate([d, e, d, f, e, d], axis=axis)
    return left.astype(jnp.bfloat16), right.astype(jnp.bfloat16)


def product_nt(x, y):
    return dot_nt(*six_products(x, y, 1))


def factor_kernel(corner_ref, out_ref, mat, work):
    eye = jnp.where(
        lax.broadcasted_iota(jnp.int32, (128, 128), 1)
        == lax.broadcasted_iota(jnp.int32, (128, 128), 0),
        1.0,
        0.0,
    )
    sub8 = lax.broadcasted_iota(jnp.int32, (8, 256), 0)
    mat[:PANEL, :] = corner_ref[...]
    mat[PANEL:, :] = jnp.zeros((PANEL, PANEL), jnp.float32)

    def eliminate(kb):
        lanes = slice(kb * 128, kb * 128 + 128)
        linv = work[:, 128:]
        inverse = jnp.transpose(linv)
        top = PANEL + kb * 128
        if kb:
            upper = product_nt(mat[PANEL:top, lanes], linv)
            mat[PANEL:top, lanes] = upper
            upper = jnp.concatenate([upper, inverse], axis=0)
        else:
            upper = inverse
        mat[top : top + 128, lanes] = inverse
        if kb < 3:
            below = (kb + 1) * 128
            solved = product_nt(mat[below:PANEL, lanes], linv)
            mat[below:PANEL, below:] = mat[below:PANEL, below:] - product_nt(solved, solved)
            mat[PANEL : top + 128, below:] = mat[PANEL : top + 128, below:] - product_nt(
                upper, solved
            )

    def column(kb, carry):
        first = pl.multiple_of(kb * 128, 128)
        work[:, :128] = mat[pl.ds(first, 128), pl.ds(first, 128)]
        work[:, 128:] = eye
        rows = [jnp.broadcast_to(work[p : p + 1, :], (8, 256)) for p in range(8)]
        for jb in range(16):
            j = jb * 8
            e = [[None] * 8 for _ in range(8)]
            for p in range(8):
                for q in range(p, 8):
                    e[p][q] = jnp.broadcast_to(rows[p][:, j + q : j + q + 1], (8, 128))
            block = None
            done = []
            for p in range(8):
                rinv = lax.rsqrt(e[p][p])
                for q in range(p + 1, 8):
                    e[p][q] = e[p][q] * rinv
                for q in range(p + 1, 8):
                    for s in range(q, 8):
                        e[q][s] = e[q][s] - e[p][q] * e[p][s]
                row = rows[p]
                for m in range(p):
                    row = row - jnp.concatenate([e[m][p]] * 2, axis=1) * done[m]
                row = row * jnp.concatenate([rinv] * 2, axis=1)
                done.append(row)
                block = row if p == 0 else jnp.where(sub8 == p, row, block)
            work[j : j + 8, :] = block
            if jb < 15:
                rows = []
                for p in range(j + 8, j + 16):
                    row = jnp.broadcast_to(work[p : p + 1, :], (8, 256))
                    for m in range(8):
                        factor_m = jnp.broadcast_to(done[m][:, p : p + 1], (8, 128))
                        row = row - jnp.concatenate([factor_m] * 2, axis=1) * done[m]
                    rows.append(row)
            if jb < 14:
                left, right = six_products(block, block, 0)
                outer = lax.dot_general(
                    left[:, :128], right, (((0,), (0,)), ((), ())), preferred_element_type=jnp.float32
                )
                work[j + 16 :, :] = work[j + 16 :, :] - outer[j + 16 :, :]
        for n in range(4):
            pl.when(kb == n)(functools.partial(eliminate, n))
        return carry

    lax.fori_loop(0, 4, column, 0)
    hi, lo = split(mat[PANEL:, :])
    out_ref[:, :PANEL] = hi
    out_ref[:, PANEL:] = lo


def factor(corner):
    return pl.pallas_call(
        factor_kernel,
        out_shape=jax.ShapeDtypeStruct((PANEL, 2 * PANEL), jnp.bfloat16),
        in_specs=[pl.BlockSpec(memory_space=pltpu.VMEM)],
        out_specs=pl.BlockSpec(memory_space=pltpu.VMEM),
        scratch_shapes=[
            pltpu.VMEM((2 * PANEL, PANEL), jnp.float32),
            pltpu.VMEM((128, 256), jnp.float32),
        ],
        name="factor",
        cost_estimate=pl.CostEstimate(flops=int(25e9), bytes_accessed=int(2e6), transcendentals=0),
    )(corner)


def tiles_kernel(
    where_ref, near_ref, far_ref, cols_ref, out_ref, cols, gram, inv_ac, scl_ac, inv_dn, scl_dn
):
    step = pl.program_id(0)
    row_index = where_ref[0]
    col_index = where_ref[1]
    count = cols_ref.shape[0] // TILE_C

    @pl.when(step == 0)
    def _():
        def body(t, carry):
            rows = pl.ds(pl.multiple_of(t * TILE_C, TILE_C), TILE_C)
            x = in_order(cols_ref[rows, :])
            cols[rows, :] = x
            n = norms_across(x)
            r = lax.rsqrt(n)
            inv_ac[t] = r
            scl_ac[t] = n * r * SCALE
            return carry

        lax.fori_loop(0, count, body, 0)

    _, other = slot_of(step, where_ref)
    x = jnp.where(other == 1, far_ref[0], near_ref[0])
    n = norms_down(x)
    r = lax.rsqrt(n)
    inv_dn[...] = r
    scl_dn[...] = n * r * SCALE
    chunk = 32

    def product(t):
        start = pl.multiple_of(t * TILE_C, TILE_C)
        gram[...] = dot_nt(x, cols[pl.ds(start, TILE_C), :])

    def piece(t, k):
        rows = slice(k * chunk, k * chunk + chunk)
        inv_r = jnp.concatenate([inv_dn[rows, :]] * 2, axis=1)
        scl_r = jnp.concatenate([scl_dn[rows, :]] * 2, axis=1)
        raw = gram[rows, :] * inv_r * inv_ac[t][0:1]
        value = tangent_of(raw, raw) * scl_r * scl_ac[t][0:1]
        out_ref[rows, pl.ds(pl.multiple_of(t * TILE_C, TILE_C), TILE_C)] = value

    product(0)

    def tile(t, carry):
        for k in range(TILE_R // chunk):
            piece(t, k)
        product(t + 1)
        return carry

    lax.fori_loop(0, step, tile, 0)

    def above(t, carry):
        first = pl.multiple_of(t * TILE_C, TILE_C)
        out_ref[:, pl.ds(first, TILE_C)] = jnp.zeros((TILE_R, TILE_C), jnp.float32)
        return carry

    lax.fori_loop(step + 1, count, above, 0)
    out_ref[:64, pl.ds(pl.multiple_of(step * TILE_C + 128, 128), 128)] = jnp.zeros(
        (64, 128), jnp.float32
    )

    for half in range(2):
        rows = slice(half * 64, half * 64 + 64)
        for lane in range(half + 1):
            lanes = slice(lane * 128, lane * 128 + 128)
            raw = gram[rows, lanes] * inv_dn[rows, :] * inv_ac[step][0:1, lanes]
            u = half * 64 + lax.broadcasted_iota(jnp.int32, (64, 128), 0)
            v = lane * 128 + lax.broadcasted_iota(jnp.int32, (64, 128), 1)
            row_id = u // 32 * PANEL + row_index * 32 + u % 32
            col_id = v // 64 * PANEL + col_index * 64 + v % 64
            on_diag = row_id == col_id
            tangent = tangent_of(jnp.where(on_diag, 1.0, raw), raw)
            value = tangent * scl_dn[rows, :] * scl_ac[step][0:1, lanes]
            value = value + jnp.where(on_diag, 1.0, 0.0)
            first = pl.multiple_of(step * TILE_C + lane * 128, 128)
            out_ref[rows, pl.ds(first, 128)] = value


def tiles(where, near, far, cols):
    n_rows, n_cols = 8 * TILE_R, cols.shape[0]
    piece = pl.BlockSpec((1, TILE_R, FEAT), lambda i, where: (slot_of(i, where)[0], 0, 0))
    return pl.pallas_call(
        tiles_kernel,
        out_shape=jax.ShapeDtypeStruct((n_rows, n_cols), jnp.float32),
        grid_spec=pltpu.PrefetchScalarGridSpec(
            num_scalar_prefetch=1,
            grid=(n_rows // TILE_R,),
            in_specs=[
                piece,
                piece,
                pl.BlockSpec((n_cols, FEAT), lambda i, where: (0, 0)),
            ],
            out_specs=pl.BlockSpec((TILE_R, n_cols), lambda i, where: (i, 0)),
            scratch_shapes=[
                pltpu.VMEM((n_cols, FEAT), jnp.bfloat16),
                pltpu.VMEM((TILE_R, TILE_C), jnp.float32),
                pltpu.VMEM((n_cols // TILE_C, 8, TILE_C), jnp.float32),
                pltpu.VMEM((n_cols // TILE_C, 8, TILE_C), jnp.float32),
                pltpu.VMEM((TILE_R, 128), jnp.float32),
                pltpu.VMEM((TILE_R, 128), jnp.float32),
            ],
        ),
        name="tiles",
        cost_estimate=pl.CostEstimate(flops=int(30e9), bytes_accessed=int(12e6), transcendentals=0),
    )(where, near, far, cols)


def solve(x, v_ref):
    hi, lo = split(x)
    parts = []
    for start in range(0, PANEL, 256):
        depth = start + 256
        v_hi = v_ref[:depth, start:depth]
        v_lo = v_ref[:depth, PANEL + start : PANEL + depth]
        left = jnp.concatenate([hi[:, :depth], hi[:, :depth], lo[:, :depth]], axis=1)
        right = jnp.concatenate([v_hi, v_lo, v_hi], axis=0)
        parts.append(jnp.dot(left, right, preferred_element_type=jnp.float32))
    return jnp.concatenate(parts, axis=1)


def update_kernel(
    where_ref, kernel_hbm, near_hbm, far_hbm, cols_hbm, v_hbm, out_hbm, *scratch
):
    slabs = scratch[:4]
    cols, rows, v_ref, both_c, left, v_sem, cols_sem, rows_sem, in_sem, out_sem = scratch[4:]
    row_index = where_ref[0]
    col_index = where_ref[1]
    tall = 2 * TILE_R
    count = cols.shape[0] // TILE_C

    def v_copy():
        return pltpu.make_async_copy(v_hbm, v_ref, v_sem)

    def cols_copy(t):
        part = pl.ds(pl.multiple_of(t * TILE_C, TILE_C), TILE_C)
        return pltpu.make_async_copy(cols_hbm.at[part], cols.at[part], cols_sem.at[t])

    def rows_copy(k, start):
        slot, other = slot_of(k, where_ref)
        for source, match in ((near_hbm, 0), (far_hbm, 1)):

            @pl.when(other == match)
            def _():
                part = pl.ds(k * TILE_R, TILE_R)
                copy = pltpu.make_async_copy(source.at[slot], rows.at[part], rows_sem.at[k])
                if start:
                    copy.start()
                else:
                    copy.wait()

    def place(step):
        return pl.ds(step * tall, tall), pl.ds(0, (step + 1) * 2 * TILE_C)

    def in_copy(step):
        return pltpu.make_async_copy(kernel_hbm.at[place(step)], slabs[step], in_sem.at[step])

    def out_copy(step):
        return pltpu.make_async_copy(slabs[step], out_hbm.at[place(step)], out_sem.at[step])

    v_copy().start()
    for t in range(count):
        cols_copy(t).start()
    for k in range(8):
        rows_copy(k, True)
    for step in range(4):
        in_copy(step).start()
    v_copy().wait()

    def solve_columns(t, carry):
        cols_copy(t).wait()
        part = pl.ds(pl.multiple_of(t * TILE_C, TILE_C), TILE_C)
        hi, lo = split(solve(in_order(cols[part, :]), v_ref))
        both_c[part, :PANEL] = hi
        both_c[part, PANEL:] = lo
        return carry

    lax.fori_loop(0, count, solve_columns, 0)

    for step in range(4):
        slab = slabs[step]
        rows_copy(2 * step, False)
        rows_copy(2 * step + 1, False)
        solved = solve(rows[step * tall : step * tall + tall, :], v_ref)
        if step:
            out_copy(step - 1).start()
        hi_r, lo_r = split(solved)
        all_r = jnp.concatenate([hi_r, hi_r, lo_r], axis=1)
        for n in range(4):
            left[n] = solved[:, n * 128 : n * 128 + 128]
        in_copy(step).wait()
        for t in range(2 * step + 2):
            lanes = slice(t * TILE_C, t * TILE_C + TILE_C)
            all_c = jnp.concatenate([both_c[lanes, :], both_c[lanes, :PANEL]], axis=1)
            value = slab[:, lanes] - dot_nt(all_r, all_c)
            v = lax.broadcasted_iota(jnp.int32, (tall, TILE_C), 1)
            if t == 0:
                mine = left[col_index // 2]
                mine = jnp.where(col_index % 2 == 1, pltpu.roll(mine, 64, 1), mine)
                mine = jnp.concatenate([mine, mine], axis=1)
                value = jnp.where(v < 64, mine, value)
            if t >= 2 * step:
                s = lax.broadcasted_iota(jnp.int32, (tall, TILE_C), 0)
                row_id = (step * 8 + s // 32) * PANEL + row_index * 32 + s % 32
                col_id = (t * 4 + v // 64) * PANEL + col_index * 64 + v % 64
                value = jnp.where(row_id >= col_id, value, 0.0)
            slab[:, lanes] = value
    out_copy(3).start()
    for step in range(4):
        out_copy(step).wait()


def update(where, kernel, near, far, cols, v):
    n_rows, n_cols = kernel.shape
    tall = 2 * TILE_R
    count = n_cols // TILE_C
    hbm = pl.BlockSpec(memory_space=pl.ANY)
    return pl.pallas_call(
        update_kernel,
        out_shape=jax.ShapeDtypeStruct((n_rows, n_cols), jnp.float32),
        in_specs=[pl.BlockSpec(memory_space=pltpu.SMEM)] + [hbm] * 5,
        out_specs=hbm,
        scratch_shapes=[pltpu.VMEM((tall, (k + 1) * 2 * TILE_C), jnp.float32) for k in range(4)]
        + [
            pltpu.VMEM((n_cols, PANEL), jnp.float32),
            pltpu.VMEM((n_rows, PANEL), jnp.float32),
            pltpu.VMEM((PANEL, 2 * PANEL), jnp.bfloat16),
            pltpu.VMEM((n_cols, 2 * PANEL), jnp.bfloat16),
            pltpu.VMEM((4, tall, 128), jnp.float32),
            pltpu.SemaphoreType.DMA,
            pltpu.SemaphoreType.DMA((count,)),
            pltpu.SemaphoreType.DMA((8,)),
            pltpu.SemaphoreType.DMA((4,)),
            pltpu.SemaphoreType.DMA((4,)),
        ],
        input_output_aliases={1: 0},
        name="update",
        cost_estimate=pl.CostEstimate(flops=int(6e9), bytes_accessed=int(20e6), transcendentals=0),
    )(where, kernel, near, far, cols, v)


def send(x, target):
    pairs = [(r * 8 + k, target(r, k)) for r in range(16) for k in range(8)]
    return lax.ppermute(x, ("row", "col"), [(s, t[0] * 8 + t[1]) for s, t in pairs if t])


def along_z(d):
    return lambda r, k: (r, (k + 2 * d) % 8)


def along_y(d):
    return lambda r, k: ((r + 4 * d) % 16, k)


def along_x(d):
    return lambda r, k: (r // 4 * 4 + (r + d) % 4, k)


def other_core(r, k):
    return r, k ^ 1


def across(r, k):
    return k * 2 + r % 2, r // 2


def to_all(x):
    head = jnp.where(lax.axis_index("col") == 0, x[:32], jnp.zeros((32, FEAT), x.dtype))
    first = [send(head, lambda r, k: (r, t) if k == 0 else None) for t in (1, 2, 6)]
    head = head + (first[0] + first[1] + first[2])
    onward = {0: 3, 1: 7, 2: 4, 6: 5}
    head = head + send(head, lambda r, k: (r, onward[k]) if k in onward else None)
    head, x = lax.optimization_barrier((head, x))
    moved = send(x, across)
    column = jnp.stack([head] + [send(head, along_y(d)) for d in (1, 2, 3)])
    column, moved = lax.optimization_barrier((column, moved))
    return [column] + [send(column, along_x(d)) for d in (1, 2, 3)], moved


def along_column(x):
    return [send(x, along_z(d)) for d in (1, 2, 3)]


def per_device(samples):
    where = jnp.stack([lax.axis_index("row"), lax.axis_index("col")]).astype(jnp.int32)
    pieces, moved = to_all(samples)
    col_feats = lax.all_gather(moved, "row", axis=0, tiled=True)
    pieces, later = lax.optimization_barrier((pieces, samples))
    feats = along_column(later)
    lead, own = leading(where, pieces, samples)
    feats, own, lead = lax.optimization_barrier((feats, own, lead))
    moved = send(own, across)
    near_feats = jnp.stack([samples] + feats)
    far_feats = send(near_feats, other_core)
    columns = along_column(own)
    corner = corner_of(lead)
    moved, corner = lax.optimization_barrier((moved, corner))
    own_cols = lax.all_gather(moved, "row", axis=0, tiled=True)
    v = factor(corner)
    far_feats, columns, v = lax.optimization_barrier((far_feats, columns, v))
    near = jnp.stack([own] + columns)
    far = send(near, other_core)
    kernel = tiles(where, near_feats, far_feats, col_feats)
    return update(where, kernel, near, far, own_cols, v)


def solution(mesh):
    return jax.shard_map(
        per_device,
        mesh=mesh,
        in_specs=(P(("row", "col"), None),),
        out_specs=P("row", "col"),
        check_vma=False,
    )
```

```python
import functools
import math

import jax
import jax.numpy as jnp
import numpy as np
from jax import lax
from jax.experimental import pallas as pl
from jax.experimental.pallas import tpu as pltpu
from jax.sharding import PartitionSpec as P

FEAT = 768
PANEL = 512
LAYERS = 8
TILE_R = 128
TILE_C = 256

ARC = (
    (1.570796265e+00, -9.999884905e-01, 7.850416849e-01, -6.623695706e-01, 5.625094387e-01, -4.372503233e-01, 2.693842319e-01, -1.086155413e-01, 2.049311747e-02),
    (1.570796265e+00, -9.999884905e-01, 7.850416849e-01, -6.623695706e-01, 5.625094387e-01, -4.372503233e-01, 2.693842319e-01, -1.086155413e-01, 2.049311747e-02),
    (1.570326531e+00, -9.935370566e-01, 7.471319178e-01, -5.376914312e-01, 3.111383121e-01, -1.187027540e-01, 2.133516172e-02),
    (1.567898155e+00, -9.719742948e-01, 6.682907781e-01, -3.857788817e-01, 1.484597498e-01, -2.689621130e-02),
    (1.566642297e+00, -9.635808948e-01, 6.460403822e-01, -3.565340200e-01, 1.294006162e-01, -2.196850873e-02),
    (1.558633208e+00, -9.141686374e-01, 5.246089379e-01, -2.079489415e-01, 3.887608390e-02),
    (1.557122831e+00, -9.070176865e-01, 5.119586953e-01, -1.980387362e-01, 3.597512846e-02),
    (1.555954084e+00, -9.016562063e-01, 5.027575168e-01, -1.910373211e-01, 3.398202014e-02),
)


def scales():
    out = [np.float32(1.0)]
    for _ in range(LAYERS):
        out.append(np.float32(np.float32(math.pi) * out[-1]))
    return out


KAPPA = scales()


def polynomial(coefs, c):
    value = c * coefs[-1] + coefs[-2]
    for coef in coefs[-3::-1]:
        value = value * c + coef
    return value


def tangent_of(cosine, tangent):
    for layer in range(LAYERS):
        kappa = KAPPA[layer]
        coefs = [float(a / np.float64(kappa) ** (k + 1)) for k, a in enumerate(ARC[layer])]
        size = jnp.abs(cosine) if layer == 0 else cosine
        square = jnp.maximum(float(np.float32(kappa * kappa)) - size * size, 1e-30)
        sine = square * lax.rsqrt(square)
        angle = sine * polynomial(coefs, size)
        rest = math.pi - angle
        if layer == 0:
            rest = jnp.where(cosine < 0.0, angle, rest)
        cosine = sine + rest * cosine
        tangent = cosine + rest * tangent
    return tangent


def squares(x):
    xf = x.astype(jnp.float32)
    sq = xf * xf
    hi = sq.astype(jnp.bfloat16)
    lo = (sq - hi.astype(jnp.float32)).astype(jnp.bfloat16)
    return hi, lo


def dot_nt(a, b, precision=None):
    return lax.dot_general(
        a, b, (((1,), (1,)), ((), ())), precision=precision, preferred_element_type=jnp.float32
    )


def norms_down(x):
    hi, lo = squares(x)
    ones = jnp.ones((128, x.shape[1]), jnp.bfloat16)
    return dot_nt(hi, ones) + dot_nt(lo, ones)


def norms_across(x):
    hi, lo = squares(x)
    ones = jnp.ones((16, x.shape[1]), jnp.bfloat16)
    return (dot_nt(ones, hi) + dot_nt(ones, lo))[:8]


SCALE = 1.0 / math.sqrt(FEAT * (LAYERS + 1.0) * float(KAPPA[LAYERS]))


def in_order(x):
    return jnp.concatenate(
        [x[m * 128 + a * 32 : m * 128 + a * 32 + 32] for a in range(4) for m in range(2)], axis=0
    )


def gathered_at(t, where):
    return (where[1] // 2 + t // 2) % 4 * 2 + t % 2


def split(x):
    hi = x.astype(jnp.bfloat16)
    return hi, (x - hi.astype(jnp.float32)).astype(jnp.bfloat16)


def slot_of(step, where):
    other = (step + where[1]) % 2
    mine = where[1] + other * (1 - 2 * (where[1] % 2))
    return ((mine - step + 8) % 8) // 2, other


def leading_kernel(
    where_ref, g0, g1, g2, g3, own_ref, corner_ref, out_ref, lead, inv_dn, scl_dn, inv_ac, scl_ac
):
    row_index = where_ref[0]
    col_index = where_ref[1]
    for dx, piece in enumerate((g0, g1, g2, g3)):
        for dy in range(4):
            r = (row_index // 4 + 4 - dy) % 4 * 4 + (row_index % 4 + 4 - dx) % 4
            lead[pl.ds(pl.multiple_of(r * 32, 32), 32), :] = piece[dy]

    def norms(x, start, count):
        n = norms_down(x)
        r = lax.rsqrt(n)
        inv_dn[start : start + count, :] = r
        scl_dn[start : start + count, :] = n * r * SCALE

    x = lead[...]
    norms(x, 0, PANEL)
    n = norms_across(x)
    r = lax.rsqrt(n)
    inv_ac[...] = r
    scl_ac[...] = n * r * SCALE
    norms(own_ref[...], PANEL, 128)
    chunk = 64
    for jb in range(4):
        lanes = slice(jb * 128, jb * 128 + 128)
        cols = lead[lanes, :]
        corner_ref[jb * 128 :, lanes] = dot_nt(lead[jb * 128 :, :], cols)
        out_ref[:, lanes] = dot_nt(own_ref[...], cols)
        inv_c = inv_ac[0:1, lanes]
        scl_c = scl_ac[0:1, lanes]

        def body(step, carry, ref, base):
            start = pl.multiple_of(step * chunk, chunk)
            rows = pl.ds(start, chunk)
            down = pl.ds(start + base, chunk)
            raw = ref[rows, lanes] * inv_dn[down, :] * inv_c
            local = start + lax.broadcasted_iota(jnp.int32, (chunk, 128), 0)
            if base:
                block = local // 32
                local = (col_index * 4 + block) * PANEL + row_index * 32 + local - block * 32
            col_id = jb * 128 + lax.broadcasted_iota(jnp.int32, (chunk, 128), 1)
            on_diag = local == col_id
            tangent = tangent_of(jnp.where(on_diag, 1.0, raw), raw)
            ref[rows, lanes] = tangent * scl_dn[down, :] * scl_c + jnp.where(on_diag, 1.0, 0.0)
            return carry

        lax.fori_loop(0, 128 // chunk, functools.partial(body, ref=out_ref, base=PANEL), 0, unroll=2)
        lax.fori_loop(
            jb * (128 // chunk), PANEL // chunk, functools.partial(body, ref=corner_ref, base=0), 0
        )


def leading(where, pieces, own):
    vmem = pl.BlockSpec(memory_space=pltpu.VMEM)
    return pl.pallas_call(
        leading_kernel,
        out_shape=(
            jax.ShapeDtypeStruct((PANEL, PANEL), jnp.float32),
            jax.ShapeDtypeStruct((128, PANEL), jnp.float32),
        ),
        in_specs=[pl.BlockSpec(memory_space=pltpu.SMEM)] + [vmem] * 5,
        out_specs=(vmem, vmem),
        scratch_shapes=[
            pltpu.VMEM((PANEL, FEAT), jnp.bfloat16),
            pltpu.VMEM((PANEL + 128, 128), jnp.float32),
            pltpu.VMEM((PANEL + 128, 128), jnp.float32),
            pltpu.VMEM((8, PANEL), jnp.float32),
            pltpu.VMEM((8, PANEL), jnp.float32),
        ],
        name="leading",
        cost_estimate=pl.CostEstimate(flops=int(8e9), bytes_accessed=int(2e6), transcendentals=0),
    )(where, *pieces, own)


def thirds(x):
    wide = x.astype(jnp.bfloat16).astype(jnp.float32)
    rest = x - wide
    middle = rest.astype(jnp.bfloat16).astype(jnp.float32)
    return wide, middle, rest - middle


def six_products(x, y, axis):
    a, b, c = thirds(x)
    d, e, f = (a, b, c) if y is x else thirds(y)
    left = jnp.concatenate([a, a, b, a, b, c], axis=axis)
    right = jnp.concatenate([d, e, d, f, e, d], axis=axis)
    return left.astype(jnp.bfloat16), right.astype(jnp.bfloat16)


def product_nt(x, y):
    return dot_nt(*six_products(x, y, 1))


def factor_kernel(in_ref, out_ref, mat, work, *, half):
    eye = jnp.where(
        lax.broadcasted_iota(jnp.int32, (128, 128), 1)
        == lax.broadcasted_iota(jnp.int32, (128, 128), 0),
        1.0,
        0.0,
    )
    sub8 = lax.broadcasted_iota(jnp.int32, (8, 256), 0)
    if half:
        mat[...] = in_ref[...]
    else:
        mat = out_ref
        mat[:PANEL, :] = in_ref[...]
        mat[PANEL:, :] = jnp.zeros((PANEL, PANEL), jnp.float32)

    def eliminate(kb):
        lanes = slice(kb * 128, kb * 128 + 128)
        linv = work[:, 128:]
        inverse = jnp.transpose(linv)
        top = PANEL + kb * 128
        if kb:
            upper = product_nt(mat[PANEL:top, lanes], linv)
            mat[PANEL:top, lanes] = upper
            upper = jnp.concatenate([upper, inverse], axis=0)
        else:
            upper = inverse
        mat[top : top + 128, lanes] = inverse
        if kb < 3:
            below = (kb + 1) * 128
            solved = product_nt(mat[below:PANEL, lanes], linv)
            mat[below:PANEL, below:] = mat[below:PANEL, below:] - product_nt(solved, solved)
            mat[PANEL : top + 128, below:] = mat[PANEL : top + 128, below:] - product_nt(
                upper, solved
            )

    def column(kb, carry):
        first = pl.multiple_of(kb * 128, 128)
        work[:, :128] = mat[pl.ds(first, 128), pl.ds(first, 128)]
        work[:, 128:] = eye
        rows = [jnp.broadcast_to(work[p : p + 1, :], (8, 256)) for p in range(8)]
        for jb in range(16):
            j = jb * 8
            e = [[None] * 8 for _ in range(8)]
            for p in range(8):
                for q in range(p, 8):
                    e[p][q] = jnp.broadcast_to(rows[p][:, j + q : j + q + 1], (8, 128))
            block = None
            done = []
            for p in range(8):
                rinv = lax.rsqrt(e[p][p])
                for q in range(p + 1, 8):
                    e[p][q] = e[p][q] * rinv
                for q in range(p + 1, 8):
                    for s in range(q, 8):
                        e[q][s] = e[q][s] - e[p][q] * e[p][s]
                row = rows[p]
                for m in range(p):
                    row = row - jnp.concatenate([e[m][p]] * 2, axis=1) * done[m]
                row = row * jnp.concatenate([rinv] * 2, axis=1)
                done.append(row)
                block = row if p == 0 else jnp.where(sub8 == p, row, block)
            work[j : j + 8, :] = block
            if jb < 15:
                rows = []
                for p in range(j + 8, j + 16):
                    row = jnp.broadcast_to(work[p : p + 1, :], (8, 256))
                    for m in range(8):
                        factor_m = jnp.broadcast_to(done[m][:, p : p + 1], (8, 128))
                        row = row - jnp.concatenate([factor_m] * 2, axis=1) * done[m]
                    rows.append(row)
            if jb < 14:
                left, right = six_products(block, block, 0)
                outer = lax.dot_general(
                    left[:, :128], right, (((0,), (0,)), ((), ())), preferred_element_type=jnp.float32
                )
                work[j + 16 :, :] = work[j + 16 :, :] - outer[j + 16 :, :]
        for n in range(2 * half, 2 * half + 2):
            pl.when(kb == n)(functools.partial(eliminate, n))
        return carry

    lax.fori_loop(2 * half, 2 * half + 2, column, 0)
    if half:
        hi, lo = split(mat[PANEL:, :])
        out_ref[:, :PANEL] = hi
        out_ref[:, PANEL:] = lo


def factor_half(x, half):
    shape = (
        jax.ShapeDtypeStruct((PANEL, 2 * PANEL), jnp.bfloat16)
        if half
        else jax.ShapeDtypeStruct((2 * PANEL, PANEL), jnp.float32)
    )
    return pl.pallas_call(
        functools.partial(factor_kernel, half=half),
        out_shape=shape,
        in_specs=[pl.BlockSpec(memory_space=pltpu.VMEM)],
        out_specs=pl.BlockSpec(memory_space=pltpu.VMEM),
        scratch_shapes=[
            pltpu.VMEM((2 * PANEL, PANEL), jnp.float32),
            pltpu.VMEM((128, 256), jnp.float32),
        ],
        name="factor",
        cost_estimate=pl.CostEstimate(flops=int(12e9), bytes_accessed=int(2e6), transcendentals=0),
    )(x)


def tiles_kernel(
    where_ref, near_ref, far_ref, cols_ref, out_ref, cols, gram, inv_ac, scl_ac, inv_dn, scl_dn
):
    step = pl.program_id(0)
    row_index = where_ref[0]
    col_index = where_ref[1]
    count = cols_ref.shape[0] // TILE_C

    @pl.when(step == 0)
    def _():
        def body(t, carry):
            source = pl.multiple_of(gathered_at(t, where_ref) * TILE_C, TILE_C)
            x = in_order(cols_ref[pl.ds(source, TILE_C), :])
            cols[pl.ds(pl.multiple_of(t * TILE_C, TILE_C), TILE_C), :] = x
            n = norms_across(x)
            r = lax.rsqrt(n)
            inv_ac[t] = r
            scl_ac[t] = n * r * SCALE
            return carry

        lax.fori_loop(0, count, body, 0)

    _, other = slot_of(step, where_ref)
    x = jnp.where(other == 1, far_ref[0], near_ref[0])
    n = norms_down(x)
    r = lax.rsqrt(n)
    inv_dn[...] = r
    scl_dn[...] = n * r * SCALE
    chunk = 32

    def product(t):
        start = pl.multiple_of(t * TILE_C, TILE_C)
        gram[...] = dot_nt(x, cols[pl.ds(start, TILE_C), :])

    def piece(t, k):
        rows = slice(k * chunk, k * chunk + chunk)
        inv_r = jnp.concatenate([inv_dn[rows, :]] * 2, axis=1)
        scl_r = jnp.concatenate([scl_dn[rows, :]] * 2, axis=1)
        raw = gram[rows, :] * inv_r * inv_ac[t][0:1]
        value = tangent_of(raw, raw) * scl_r * scl_ac[t][0:1]
        out_ref[rows, pl.ds(pl.multiple_of(t * TILE_C, TILE_C), TILE_C)] = value

    product(0)

    def tile(t, carry):
        for k in range(TILE_R // chunk):
            piece(t, k)
        product(t + 1)
        return carry

    lax.fori_loop(0, step, tile, 0)

    def above(t, carry):
        first = pl.multiple_of(t * TILE_C, TILE_C)
        out_ref[:, pl.ds(first, TILE_C)] = jnp.zeros((TILE_R, TILE_C), jnp.float32)
        return carry

    lax.fori_loop(step + 1, count, above, 0)
    out_ref[:64, pl.ds(pl.multiple_of(step * TILE_C + 128, 128), 128)] = jnp.zeros(
        (64, 128), jnp.float32
    )

    for half in range(2):
        rows = slice(half * 64, half * 64 + 64)
        for lane in range(half + 1):
            lanes = slice(lane * 128, lane * 128 + 128)
            raw = gram[rows, lanes] * inv_dn[rows, :] * inv_ac[step][0:1, lanes]
            u = half * 64 + lax.broadcasted_iota(jnp.int32, (64, 128), 0)
            v = lane * 128 + lax.broadcasted_iota(jnp.int32, (64, 128), 1)
            row_id = u // 32 * PANEL + row_index * 32 + u % 32
            col_id = v // 64 * PANEL + col_index * 64 + v % 64
            on_diag = row_id == col_id
            tangent = tangent_of(jnp.where(on_diag, 1.0, raw), raw)
            value = tangent * scl_dn[rows, :] * scl_ac[step][0:1, lanes]
            value = value + jnp.where(on_diag, 1.0, 0.0)
            first = pl.multiple_of(step * TILE_C + lane * 128, 128)
            out_ref[rows, pl.ds(first, 128)] = value


def tiles(where, near, far, cols):
    n_rows, n_cols = 8 * TILE_R, cols.shape[0]
    piece = pl.BlockSpec((1, TILE_R, FEAT), lambda i, where: (slot_of(i, where)[0], 0, 0))
    return pl.pallas_call(
        tiles_kernel,
        out_shape=jax.ShapeDtypeStruct((n_rows, n_cols), jnp.float32),
        grid_spec=pltpu.PrefetchScalarGridSpec(
            num_scalar_prefetch=1,
            grid=(n_rows // TILE_R,),
            in_specs=[
                piece,
                piece,
                pl.BlockSpec((n_cols, FEAT), lambda i, where: (0, 0)),
            ],
            out_specs=pl.BlockSpec((TILE_R, n_cols), lambda i, where: (i, 0)),
            scratch_shapes=[
                pltpu.VMEM((n_cols, FEAT), jnp.bfloat16),
                pltpu.VMEM((TILE_R, TILE_C), jnp.float32),
                pltpu.VMEM((n_cols // TILE_C, 8, TILE_C), jnp.float32),
                pltpu.VMEM((n_cols // TILE_C, 8, TILE_C), jnp.float32),
                pltpu.VMEM((TILE_R, 128), jnp.float32),
                pltpu.VMEM((TILE_R, 128), jnp.float32),
            ],
        ),
        name="tiles",
        cost_estimate=pl.CostEstimate(flops=int(30e9), bytes_accessed=int(12e6), transcendentals=0),
    )(where, near, far, cols)


def solve(x, v_ref):
    hi, lo = split(x)
    parts = []
    for start in range(0, PANEL, 256):
        depth = start + 256
        v_hi = v_ref[:depth, start:depth]
        v_lo = v_ref[:depth, PANEL + start : PANEL + depth]
        left = jnp.concatenate([hi[:, :depth], hi[:, :depth], lo[:, :depth]], axis=1)
        right = jnp.concatenate([v_hi, v_lo, v_hi], axis=0)
        parts.append(jnp.dot(left, right, preferred_element_type=jnp.float32))
    return jnp.concatenate(parts, axis=1)


def update_kernel(
    where_ref, kernel_hbm, near_hbm, far_hbm, cols_hbm, v_hbm, out_hbm, *scratch
):
    slabs = scratch[:4]
    cols, rows, v_ref, both_c, left, v_sem, cols_sem, rows_sem, in_sem, out_sem = scratch[4:]
    row_index = where_ref[0]
    col_index = where_ref[1]
    tall = 2 * TILE_R
    count = cols.shape[0] // TILE_C

    def v_copy():
        return pltpu.make_async_copy(v_hbm, v_ref, v_sem)

    def cols_copy(t):
        part = pl.ds(pl.multiple_of(t * TILE_C, TILE_C), TILE_C)
        source = pl.multiple_of(gathered_at(t, where_ref) * TILE_C, TILE_C)
        return pltpu.make_async_copy(
            cols_hbm.at[pl.ds(source, TILE_C)], cols.at[part], cols_sem.at[t]
        )

    def rows_copy(k, start):
        slot, other = slot_of(k, where_ref)
        for source, match in ((near_hbm, 0), (far_hbm, 1)):

            @pl.when(other == match)
            def _():
                part = pl.ds(k * TILE_R, TILE_R)
                copy = pltpu.make_async_copy(source.at[slot], rows.at[part], rows_sem.at[k])
                if start:
                    copy.start()
                else:
                    copy.wait()

    def place(step):
        return pl.ds(step * tall, tall), pl.ds(0, (step + 1) * 2 * TILE_C)

    def in_copy(step):
        return pltpu.make_async_copy(kernel_hbm.at[place(step)], slabs[step], in_sem.at[step])

    def out_copy(step):
        return pltpu.make_async_copy(slabs[step], out_hbm.at[place(step)], out_sem.at[step])

    v_copy().start()
    for t in range(count):
        cols_copy(t).start()
    for k in range(8):
        rows_copy(k, True)
    for step in range(4):
        in_copy(step).start()
    v_copy().wait()

    def solve_columns(t, carry):
        cols_copy(t).wait()
        part = pl.ds(pl.multiple_of(t * TILE_C, TILE_C), TILE_C)
        hi, lo = split(solve(in_order(cols[part, :]), v_ref))
        both_c[part, :PANEL] = hi
        both_c[part, PANEL:] = lo
        return carry

    lax.fori_loop(0, count, solve_columns, 0)

    for step in range(4):
        slab = slabs[step]
        rows_copy(2 * step, False)
        rows_copy(2 * step + 1, False)
        solved = solve(rows[step * tall : step * tall + tall, :], v_ref)
        if step:
            out_copy(step - 1).start()
        hi_r, lo_r = split(solved)
        all_r = jnp.concatenate([hi_r, hi_r, lo_r], axis=1)
        for n in range(4):
            left[n] = solved[:, n * 128 : n * 128 + 128]
        in_copy(step).wait()
        for t in range(2 * step + 2):
            lanes = slice(t * TILE_C, t * TILE_C + TILE_C)
            all_c = jnp.concatenate([both_c[lanes, :], both_c[lanes, :PANEL]], axis=1)
            value = slab[:, lanes] - dot_nt(all_r, all_c)
            v = lax.broadcasted_iota(jnp.int32, (tall, TILE_C), 1)
            if t == 0:
                mine = left[col_index // 2]
                mine = jnp.where(col_index % 2 == 1, pltpu.roll(mine, 64, 1), mine)
                mine = jnp.concatenate([mine, mine], axis=1)
                value = jnp.where(v < 64, mine, value)
            if t >= 2 * step:
                s = lax.broadcasted_iota(jnp.int32, (tall, TILE_C), 0)
                row_id = (step * 8 + s // 32) * PANEL + row_index * 32 + s % 32
                col_id = (t * 4 + v // 64) * PANEL + col_index * 64 + v % 64
                value = jnp.where(row_id >= col_id, value, 0.0)
            slab[:, lanes] = value
    out_copy(3).start()
    for step in range(4):
        out_copy(step).wait()


def update(where, kernel, near, far, cols, v):
    n_rows, n_cols = kernel.shape
    tall = 2 * TILE_R
    count = n_cols // TILE_C
    hbm = pl.BlockSpec(memory_space=pl.ANY)
    return pl.pallas_call(
        update_kernel,
        out_shape=jax.ShapeDtypeStruct((n_rows, n_cols), jnp.float32),
        in_specs=[pl.BlockSpec(memory_space=pltpu.SMEM)] + [hbm] * 5,
        out_specs=hbm,
        scratch_shapes=[pltpu.VMEM((tall, (k + 1) * 2 * TILE_C), jnp.float32) for k in range(4)]
        + [
            pltpu.VMEM((n_cols, PANEL), jnp.float32),
            pltpu.VMEM((n_rows, PANEL), jnp.float32),
            pltpu.VMEM((PANEL, 2 * PANEL), jnp.bfloat16),
            pltpu.VMEM((n_cols, 2 * PANEL), jnp.bfloat16),
            pltpu.VMEM((4, tall, 128), jnp.float32),
            pltpu.SemaphoreType.DMA,
            pltpu.SemaphoreType.DMA((count,)),
            pltpu.SemaphoreType.DMA((8,)),
            pltpu.SemaphoreType.DMA((4,)),
            pltpu.SemaphoreType.DMA((4,)),
        ],
        input_output_aliases={1: 0},
        name="update",
        cost_estimate=pl.CostEstimate(flops=int(6e9), bytes_accessed=int(20e6), transcendentals=0),
    )(where, kernel, near, far, cols, v)


def send(x, target):
    pairs = [(r * 8 + k, target(r, k)) for r in range(16) for k in range(8)]
    return lax.ppermute(x, ("row", "col"), [(s, t[0] * 8 + t[1]) for s, t in pairs if t])


def along_z(d):
    return lambda r, k: (r, (k + 2 * d) % 8)


def along_y(d):
    return lambda r, k: ((r + 4 * d) % 16, k)


def along_x(d):
    return lambda r, k: (r // 4 * 4 + (r + d) % 4, k)


def other_core(r, k):
    return r, k ^ 1


def across(r, k):
    return (r // 4 + k // 2) % 4 * 4 + k % 2 * 2 + r % 2, r // 2


def to_all(x, moved):
    head = jnp.where(lax.axis_index("col") == 0, x[:32], jnp.zeros((32, FEAT), x.dtype))
    for bit in (1, 2, 4):
        head = head + send(head, lambda r, k: (r, k | bit) if k < bit else None)
    head, moved = lax.optimization_barrier((head, moved))
    column = jnp.stack([head] + [send(head, along_y(d)) for d in (1, 2, 3)])
    return [column] + [send(column, along_x(d)) for d in (1, 2, 3)], moved


def along_column(x):
    return [send(x, along_z(d)) for d in (1, 2, 3)]


def per_device(samples):
    where = jnp.stack([lax.axis_index("row"), lax.axis_index("col")]).astype(jnp.int32)
    pieces, moved = to_all(samples, send(samples, across))
    col_feats = lax.all_gather(moved, "row", axis=0, tiled=True)
    pieces, later = lax.optimization_barrier((pieces, samples))
    feats = along_column(later)
    corner, own = leading(where, pieces, samples)
    feats, own, corner = lax.optimization_barrier((feats, own, corner))
    moved = send(own, across)
    near_feats = jnp.stack([samples] + feats)
    far_feats = send(near_feats, other_core)
    columns = along_column(own)
    half = factor_half(corner, 0)
    moved, far_feats, columns, half = lax.optimization_barrier((moved, far_feats, columns, half))
    own_cols = lax.all_gather(moved, "row", axis=0, tiled=True)
    near = jnp.stack([own] + columns)
    far = send(near, other_core)
    v = factor_half(half, 1)
    kernel = tiles(where, near_feats, far_feats, col_feats)
    return update(where, kernel, near, far, own_cols, v)


def solution(mesh):
    return jax.shard_map(
        per_device,
        mesh=mesh,
        in_specs=(P(("row", "col"), None),),
        out_specs=P("row", "col"),
        check_vma=False,
    )
```

```python
import functools
import math

import jax
import jax.numpy as jnp
import numpy as np
from jax import lax
from jax.experimental import pallas as pl
from jax.experimental.pallas import tpu as pltpu
from jax.sharding import PartitionSpec as P

FEAT = 768
PANEL = 512
LAYERS = 8
TILE_R = 128
TILE_C = 256

ARC = (
    (1.570796265e+00, -9.999884905e-01, 7.850416849e-01, -6.623695706e-01, 5.625094387e-01, -4.372503233e-01, 2.693842319e-01, -1.086155413e-01, 2.049311747e-02),
    (1.570796265e+00, -9.999884905e-01, 7.850416849e-01, -6.623695706e-01, 5.625094387e-01, -4.372503233e-01, 2.693842319e-01, -1.086155413e-01, 2.049311747e-02),
    (1.570326531e+00, -9.935370566e-01, 7.471319178e-01, -5.376914312e-01, 3.111383121e-01, -1.187027540e-01, 2.133516172e-02),
    (1.567898155e+00, -9.719742948e-01, 6.682907781e-01, -3.857788817e-01, 1.484597498e-01, -2.689621130e-02),
    (1.566642297e+00, -9.635808948e-01, 6.460403822e-01, -3.565340200e-01, 1.294006162e-01, -2.196850873e-02),
    (1.558633208e+00, -9.141686374e-01, 5.246089379e-01, -2.079489415e-01, 3.887608390e-02),
    (1.557122831e+00, -9.070176865e-01, 5.119586953e-01, -1.980387362e-01, 3.597512846e-02),
    (1.555954084e+00, -9.016562063e-01, 5.027575168e-01, -1.910373211e-01, 3.398202014e-02),
)


def scales():
    out = [np.float32(1.0)]
    for _ in range(LAYERS):
        out.append(np.float32(np.float32(math.pi) * out[-1]))
    return out


KAPPA = scales()


def polynomial(coefs, c):
    value = c * coefs[-1] + coefs[-2]
    for coef in coefs[-3::-1]:
        value = value * c + coef
    return value


def tangent_of(cosine, tangent):
    for layer in range(LAYERS):
        kappa = KAPPA[layer]
        coefs = [float(a / np.float64(kappa) ** (k + 1)) for k, a in enumerate(ARC[layer])]
        size = jnp.abs(cosine) if layer == 0 else cosine
        square = jnp.maximum(float(np.float32(kappa * kappa)) - size * size, 1e-30)
        sine = square * lax.rsqrt(square)
        angle = sine * polynomial(coefs, size)
        rest = math.pi - angle
        if layer == 0:
            rest = jnp.where(cosine < 0.0, angle, rest)
        cosine = sine + rest * cosine
        tangent = cosine + rest * tangent
    return tangent


def squares(x):
    xf = x.astype(jnp.float32)
    sq = xf * xf
    hi = sq.astype(jnp.bfloat16)
    lo = (sq - hi.astype(jnp.float32)).astype(jnp.bfloat16)
    return hi, lo


def dot_nt(a, b, precision=None):
    return lax.dot_general(
        a, b, (((1,), (1,)), ((), ())), precision=precision, preferred_element_type=jnp.float32
    )


def norms_down(x):
    hi, lo = squares(x)
    ones = jnp.ones((128, x.shape[1]), jnp.bfloat16)
    return dot_nt(hi, ones) + dot_nt(lo, ones)


def norms_across(x):
    hi, lo = squares(x)
    ones = jnp.ones((16, x.shape[1]), jnp.bfloat16)
    return (dot_nt(ones, hi) + dot_nt(ones, lo))[:8]


SCALE = 1.0 / math.sqrt(FEAT * (LAYERS + 1.0) * float(KAPPA[LAYERS]))


def in_order(x):
    return jnp.concatenate(
        [x[m * 128 + a * 32 : m * 128 + a * 32 + 32] for a in range(4) for m in range(2)], axis=0
    )


def gathered_at(t, where):
    return (where[1] // 2 + t // 2) % 4 * 2 + t % 2


def split(x):
    hi = x.astype(jnp.bfloat16)
    return hi, (x - hi.astype(jnp.float32)).astype(jnp.bfloat16)


def slot_of(step, where):
    other = (step + where[1]) % 2
    mine = where[1] + other * (1 - 2 * (where[1] % 2))
    return ((mine - step + 8) % 8) // 2, other


def leading_kernel(
    where_ref, g0, g1, g2, g3, own_ref, corner_ref, out_ref, lead, inv_dn, scl_dn, inv_ac, scl_ac
):
    row_index = where_ref[0]
    col_index = where_ref[1]
    for dx, piece in enumerate((g0, g1, g2, g3)):
        for dy in range(4):
            r = (row_index // 4 + 4 - dy) % 4 * 4 + (row_index % 4 + 4 - dx) % 4
            lead[pl.ds(pl.multiple_of(r * 32, 32), 32), :] = piece[dy]

    def norms(x, start, count):
        n = norms_down(x)
        r = lax.rsqrt(n)
        inv_dn[start : start + count, :] = r
        scl_dn[start : start + count, :] = n * r * SCALE

    x = lead[...]
    norms(x, 0, PANEL)
    n = norms_across(x)
    r = lax.rsqrt(n)
    inv_ac[...] = r
    scl_ac[...] = n * r * SCALE
    norms(own_ref[...], PANEL, 128)
    chunk = 64
    for jb in range(4):
        lanes = slice(jb * 128, jb * 128 + 128)
        cols = lead[lanes, :]
        corner_ref[jb * 128 :, lanes] = dot_nt(lead[jb * 128 :, :], cols)
        out_ref[:, lanes] = dot_nt(own_ref[...], cols)
        inv_c = inv_ac[0:1, lanes]
        scl_c = scl_ac[0:1, lanes]

        def body(step, carry, ref, base):
            start = pl.multiple_of(step * chunk, chunk)
            rows = pl.ds(start, chunk)
            down = pl.ds(start + base, chunk)
            raw = ref[rows, lanes] * inv_dn[down, :] * inv_c
            local = start + lax.broadcasted_iota(jnp.int32, (chunk, 128), 0)
            if base:
                block = local // 32
                local = (col_index * 4 + block) * PANEL + row_index * 32 + local - block * 32
            col_id = jb * 128 + lax.broadcasted_iota(jnp.int32, (chunk, 128), 1)
            on_diag = local == col_id
            tangent = tangent_of(jnp.where(on_diag, 1.0, raw), raw)
            ref[rows, lanes] = tangent * scl_dn[down, :] * scl_c + jnp.where(on_diag, 1.0, 0.0)
            return carry

        lax.fori_loop(0, 128 // chunk, functools.partial(body, ref=out_ref, base=PANEL), 0, unroll=2)
        lax.fori_loop(
            jb * (128 // chunk), PANEL // chunk, functools.partial(body, ref=corner_ref, base=0), 0
        )


def leading(where, pieces, own):
    vmem = pl.BlockSpec(memory_space=pltpu.VMEM)
    return pl.pallas_call(
        leading_kernel,
        out_shape=(
            jax.ShapeDtypeStruct((PANEL, PANEL), jnp.float32),
            jax.ShapeDtypeStruct((128, PANEL), jnp.float32),
        ),
        in_specs=[pl.BlockSpec(memory_space=pltpu.SMEM)] + [vmem] * 5,
        out_specs=(vmem, vmem),
        scratch_shapes=[
            pltpu.VMEM((PANEL, FEAT), jnp.bfloat16),
            pltpu.VMEM((PANEL + 128, 128), jnp.float32),
            pltpu.VMEM((PANEL + 128, 128), jnp.float32),
            pltpu.VMEM((8, PANEL), jnp.float32),
            pltpu.VMEM((8, PANEL), jnp.float32),
        ],
        name="leading",
        cost_estimate=pl.CostEstimate(flops=int(8e9), bytes_accessed=int(2e6), transcendentals=0),
    )(where, *pieces, own)


def thirds(x):
    wide = x.astype(jnp.bfloat16).astype(jnp.float32)
    rest = x - wide
    middle = rest.astype(jnp.bfloat16).astype(jnp.float32)
    return wide, middle, rest - middle


def six_products(x, y, axis):
    a, b, c = thirds(x)
    d, e, f = (a, b, c) if y is x else thirds(y)
    left = jnp.concatenate([a, a, b, a, b, c], axis=axis)
    right = jnp.concatenate([d, e, d, f, e, d], axis=axis)
    return left.astype(jnp.bfloat16), right.astype(jnp.bfloat16)


def product_nt(x, y):
    return dot_nt(*six_products(x, y, 1))


def factor_kernel(in_ref, out_ref, mat, work, *, half):
    eye = jnp.where(
        lax.broadcasted_iota(jnp.int32, (128, 128), 1)
        == lax.broadcasted_iota(jnp.int32, (128, 128), 0),
        1.0,
        0.0,
    )
    sub8 = lax.broadcasted_iota(jnp.int32, (8, 256), 0)
    if half:
        mat[...] = in_ref[...]
    else:
        mat = out_ref
        mat[:PANEL, :] = in_ref[...]
        mat[PANEL:, :] = jnp.zeros((PANEL, PANEL), jnp.float32)

    def eliminate(kb):
        lanes = slice(kb * 128, kb * 128 + 128)
        linv = work[:, 128:]
        inverse = jnp.transpose(linv)
        top = PANEL + kb * 128
        if kb:
            upper = product_nt(mat[PANEL:top, lanes], linv)
            mat[PANEL:top, lanes] = upper
            upper = jnp.concatenate([upper, inverse], axis=0)
        else:
            upper = inverse
        mat[top : top + 128, lanes] = inverse
        if kb < 3:
            below = (kb + 1) * 128
            solved = product_nt(mat[below:PANEL, lanes], linv)
            mat[below:PANEL, below:] = mat[below:PANEL, below:] - product_nt(solved, solved)
            mat[PANEL : top + 128, below:] = mat[PANEL : top + 128, below:] - product_nt(
                upper, solved
            )

    def column(kb, carry):
        first = pl.multiple_of(kb * 128, 128)
        work[:, :128] = mat[pl.ds(first, 128), pl.ds(first, 128)]
        work[:, 128:] = eye
        rows = [jnp.broadcast_to(work[p : p + 1, :], (8, 256)) for p in range(8)]
        for jb in range(16):
            j = jb * 8
            e = [[None] * 8 for _ in range(8)]
            for p in range(8):
                for q in range(p, 8):
                    e[p][q] = jnp.broadcast_to(rows[p][:, j + q : j + q + 1], (8, 128))
            block = None
            done = []
            for p in range(8):
                rinv = lax.rsqrt(e[p][p])
                for q in range(p + 1, 8):
                    e[p][q] = e[p][q] * rinv
                for q in range(p + 1, 8):
                    for s in range(q, 8):
                        e[q][s] = e[q][s] - e[p][q] * e[p][s]
                row = rows[p]
                for m in range(p):
                    row = row - jnp.concatenate([e[m][p]] * 2, axis=1) * done[m]
                row = row * jnp.concatenate([rinv] * 2, axis=1)
                done.append(row)
                block = row if p == 0 else jnp.where(sub8 == p, row, block)
            work[j : j + 8, :] = block
            if jb < 15:
                rows = []
                for p in range(j + 8, j + 16):
                    row = jnp.broadcast_to(work[p : p + 1, :], (8, 256))
                    for m in range(8):
                        factor_m = jnp.broadcast_to(done[m][:, p : p + 1], (8, 128))
                        row = row - jnp.concatenate([factor_m] * 2, axis=1) * done[m]
                    rows.append(row)
            if jb < 14:
                left, right = six_products(block, block, 0)
                outer = lax.dot_general(
                    left[:, :128], right, (((0,), (0,)), ((), ())), preferred_element_type=jnp.float32
                )
                work[j + 16 :, :] = work[j + 16 :, :] - outer[j + 16 :, :]
        for n in range(2 * half, 2 * half + 2):
            pl.when(kb == n)(functools.partial(eliminate, n))
        return carry

    lax.fori_loop(2 * half, 2 * half + 2, column, 0)
    if half:
        hi, lo = split(mat[PANEL:, :])
        out_ref[:, :PANEL] = hi
        out_ref[:, PANEL:] = lo


def factor_half(x, half):
    shape = (
        jax.ShapeDtypeStruct((PANEL, 2 * PANEL), jnp.bfloat16)
        if half
        else jax.ShapeDtypeStruct((2 * PANEL, PANEL), jnp.float32)
    )
    return pl.pallas_call(
        functools.partial(factor_kernel, half=half),
        out_shape=shape,
        in_specs=[pl.BlockSpec(memory_space=pltpu.VMEM)],
        out_specs=pl.BlockSpec(memory_space=pltpu.VMEM),
        scratch_shapes=[
            pltpu.VMEM((2 * PANEL, PANEL), jnp.float32),
            pltpu.VMEM((128, 256), jnp.float32),
        ],
        name="factor",
        cost_estimate=pl.CostEstimate(flops=int(12e9), bytes_accessed=int(2e6), transcendentals=0),
    )(x)


def tiles_kernel(
    where_ref, near_ref, far_ref, cols_ref, out_ref, cols, gram, inv_ac, scl_ac, inv_dn, scl_dn
):
    step = pl.program_id(0)
    row_index = where_ref[0]
    col_index = where_ref[1]
    count = cols_ref.shape[0] // TILE_C

    @pl.when(step == 0)
    def _():
        def body(t, carry):
            source = pl.multiple_of(gathered_at(t, where_ref) * TILE_C, TILE_C)
            x = in_order(cols_ref[pl.ds(source, TILE_C), :])
            cols[pl.ds(pl.multiple_of(t * TILE_C, TILE_C), TILE_C), :] = x
            n = norms_across(x)
            r = lax.rsqrt(n)
            inv_ac[t] = r
            scl_ac[t] = n * r * SCALE
            return carry

        lax.fori_loop(0, count, body, 0)

    _, other = slot_of(step, where_ref)
    x = jnp.where(other == 1, far_ref[0], near_ref[0])
    n = norms_down(x)
    r = lax.rsqrt(n)
    inv_dn[...] = r
    scl_dn[...] = n * r * SCALE
    chunk = 32

    def product(t):
        start = pl.multiple_of(t * TILE_C, TILE_C)
        gram[...] = dot_nt(x, cols[pl.ds(start, TILE_C), :])

    def piece(t, k):
        rows = slice(k * chunk, k * chunk + chunk)
        inv_r = jnp.concatenate([inv_dn[rows, :]] * 2, axis=1)
        scl_r = jnp.concatenate([scl_dn[rows, :]] * 2, axis=1)
        raw = gram[rows, :] * inv_r * inv_ac[t][0:1]
        value = tangent_of(raw, raw) * scl_r * scl_ac[t][0:1]
        out_ref[rows, pl.ds(pl.multiple_of(t * TILE_C, TILE_C), TILE_C)] = value

    product(0)

    def tile(t, carry):
        for k in range(TILE_R // chunk):
            piece(t, k)
        product(t + 1)
        return carry

    lax.fori_loop(0, step, tile, 0)

    def above(t, carry):
        first = pl.multiple_of(t * TILE_C, TILE_C)
        out_ref[:, pl.ds(first, TILE_C)] = jnp.zeros((TILE_R, TILE_C), jnp.float32)
        return carry

    lax.fori_loop(step + 1, count, above, 0)
    out_ref[:64, pl.ds(pl.multiple_of(step * TILE_C + 128, 128), 128)] = jnp.zeros(
        (64, 128), jnp.float32
    )

    for half in range(2):
        rows = slice(half * 64, half * 64 + 64)
        for lane in range(half + 1):
            lanes = slice(lane * 128, lane * 128 + 128)
            raw = gram[rows, lanes] * inv_dn[rows, :] * inv_ac[step][0:1, lanes]
            u = half * 64 + lax.broadcasted_iota(jnp.int32, (64, 128), 0)
            v = lane * 128 + lax.broadcasted_iota(jnp.int32, (64, 128), 1)
            row_id = u // 32 * PANEL + row_index * 32 + u % 32
            col_id = v // 64 * PANEL + col_index * 64 + v % 64
            on_diag = row_id == col_id
            tangent = tangent_of(jnp.where(on_diag, 1.0, raw), raw)
            value = tangent * scl_dn[rows, :] * scl_ac[step][0:1, lanes]
            value = value + jnp.where(on_diag, 1.0, 0.0)
            first = pl.multiple_of(step * TILE_C + lane * 128, 128)
            out_ref[rows, pl.ds(first, 128)] = value


def tiles(where, near, far, cols):
    n_rows, n_cols = 8 * TILE_R, cols.shape[0]
    piece = pl.BlockSpec((1, TILE_R, FEAT), lambda i, where: (slot_of(i, where)[0], 0, 0))
    return pl.pallas_call(
        tiles_kernel,
        out_shape=jax.ShapeDtypeStruct((n_rows, n_cols), jnp.float32),
        grid_spec=pltpu.PrefetchScalarGridSpec(
            num_scalar_prefetch=1,
            grid=(n_rows // TILE_R,),
            in_specs=[
                piece,
                piece,
                pl.BlockSpec((n_cols, FEAT), lambda i, where: (0, 0)),
            ],
            out_specs=pl.BlockSpec((TILE_R, n_cols), lambda i, where: (i, 0)),
            scratch_shapes=[
                pltpu.VMEM((n_cols, FEAT), jnp.bfloat16),
                pltpu.VMEM((TILE_R, TILE_C), jnp.float32),
                pltpu.VMEM((n_cols // TILE_C, 8, TILE_C), jnp.float32),
                pltpu.VMEM((n_cols // TILE_C, 8, TILE_C), jnp.float32),
                pltpu.VMEM((TILE_R, 128), jnp.float32),
                pltpu.VMEM((TILE_R, 128), jnp.float32),
            ],
        ),
        name="tiles",
        cost_estimate=pl.CostEstimate(flops=int(30e9), bytes_accessed=int(12e6), transcendentals=0),
    )(where, near, far, cols)


def solve(x, v_ref):
    hi, lo = split(x)
    parts = []
    for start in range(0, PANEL, 256):
        depth = start + 256
        v_hi = v_ref[:depth, start:depth]
        v_lo = v_ref[:depth, PANEL + start : PANEL + depth]
        left = jnp.concatenate([hi[:, :depth], hi[:, :depth], lo[:, :depth]], axis=1)
        right = jnp.concatenate([v_hi, v_lo, v_hi], axis=0)
        parts.append(jnp.dot(left, right, preferred_element_type=jnp.float32))
    return jnp.concatenate(parts, axis=1)


def update_kernel(
    where_ref, kernel_hbm, near_hbm, far_hbm, cols_hbm, v_hbm, out_hbm, *scratch
):
    slabs = scratch[:4]
    cols, rows, v_ref, both_c, left, v_sem, cols_sem, rows_sem, in_sem, out_sem = scratch[4:]
    row_index = where_ref[0]
    col_index = where_ref[1]
    tall = 2 * TILE_R
    count = cols.shape[0] // TILE_C

    def v_copy():
        return pltpu.make_async_copy(v_hbm, v_ref, v_sem)

    def cols_copy(t):
        part = pl.ds(pl.multiple_of(t * TILE_C, TILE_C), TILE_C)
        source = pl.multiple_of(gathered_at(t, where_ref) * TILE_C, TILE_C)
        return pltpu.make_async_copy(
            cols_hbm.at[pl.ds(source, TILE_C)], cols.at[part], cols_sem.at[t]
        )

    def rows_copy(k, start):
        slot, other = slot_of(k, where_ref)
        for source, match in ((near_hbm, 0), (far_hbm, 1)):

            @pl.when(other == match)
            def _():
                part = pl.ds(k * TILE_R, TILE_R)
                copy = pltpu.make_async_copy(source.at[slot], rows.at[part], rows_sem.at[k])
                if start:
                    copy.start()
                else:
                    copy.wait()

    def place(step):
        return pl.ds(step * tall, tall), pl.ds(0, (step + 1) * 2 * TILE_C)

    def in_copy(step):
        return pltpu.make_async_copy(kernel_hbm.at[place(step)], slabs[step], in_sem.at[step])

    def out_copy(step):
        return pltpu.make_async_copy(slabs[step], out_hbm.at[place(step)], out_sem.at[step])

    v_copy().start()
    for t in range(count):
        cols_copy(t).start()
    for k in range(8):
        rows_copy(k, True)
    for step in (3, 2, 1, 0):
        in_copy(step).start()
    v_copy().wait()

    def solve_columns(t, carry):
        cols_copy(t).wait()
        part = pl.ds(pl.multiple_of(t * TILE_C, TILE_C), TILE_C)
        hi, lo = split(solve(in_order(cols[part, :]), v_ref))
        both_c[part, :PANEL] = hi
        both_c[part, PANEL:] = lo
        return carry

    lax.fori_loop(0, count, solve_columns, 0)

    for step in (3, 2, 1, 0):
        slab = slabs[step]
        rows_copy(2 * step, False)
        rows_copy(2 * step + 1, False)
        solved = solve(rows[step * tall : step * tall + tall, :], v_ref)
        if step < 3:
            out_copy(step + 1).start()
        hi_r, lo_r = split(solved)
        all_r = jnp.concatenate([hi_r, hi_r, lo_r], axis=1)
        for n in range(4):
            left[n] = solved[:, n * 128 : n * 128 + 128]
        in_copy(step).wait()
        for t in range(2 * step + 2):
            lanes = slice(t * TILE_C, t * TILE_C + TILE_C)
            all_c = jnp.concatenate([both_c[lanes, :], both_c[lanes, :PANEL]], axis=1)
            value = slab[:, lanes] - dot_nt(all_r, all_c)
            v = lax.broadcasted_iota(jnp.int32, (tall, TILE_C), 1)
            if t == 0:
                mine = left[col_index // 2]
                mine = jnp.where(col_index % 2 == 1, pltpu.roll(mine, 64, 1), mine)
                mine = jnp.concatenate([mine, mine], axis=1)
                value = jnp.where(v < 64, mine, value)
            if t >= 2 * step:
                s = lax.broadcasted_iota(jnp.int32, (tall, TILE_C), 0)
                row_id = (step * 8 + s // 32) * PANEL + row_index * 32 + s % 32
                col_id = (t * 4 + v // 64) * PANEL + col_index * 64 + v % 64
                value = jnp.where(row_id >= col_id, value, 0.0)
            slab[:, lanes] = value
    out_copy(0).start()
    for step in range(4):
        out_copy(step).wait()


def update(where, kernel, near, far, cols, v):
    n_rows, n_cols = kernel.shape
    tall = 2 * TILE_R
    count = n_cols // TILE_C
    hbm = pl.BlockSpec(memory_space=pl.ANY)
    return pl.pallas_call(
        update_kernel,
        out_shape=jax.ShapeDtypeStruct((n_rows, n_cols), jnp.float32),
        in_specs=[pl.BlockSpec(memory_space=pltpu.SMEM)] + [hbm] * 5,
        out_specs=hbm,
        scratch_shapes=[pltpu.VMEM((tall, (k + 1) * 2 * TILE_C), jnp.float32) for k in range(4)]
        + [
            pltpu.VMEM((n_cols, PANEL), jnp.float32),
            pltpu.VMEM((n_rows, PANEL), jnp.float32),
            pltpu.VMEM((PANEL, 2 * PANEL), jnp.bfloat16),
            pltpu.VMEM((n_cols, 2 * PANEL), jnp.bfloat16),
            pltpu.VMEM((4, tall, 128), jnp.float32),
            pltpu.SemaphoreType.DMA,
            pltpu.SemaphoreType.DMA((count,)),
            pltpu.SemaphoreType.DMA((8,)),
            pltpu.SemaphoreType.DMA((4,)),
            pltpu.SemaphoreType.DMA((4,)),
        ],
        input_output_aliases={1: 0},
        name="update",
        cost_estimate=pl.CostEstimate(flops=int(6e9), bytes_accessed=int(20e6), transcendentals=0),
    )(where, kernel, near, far, cols, v)


def send(x, target):
    pairs = [(r * 8 + k, target(r, k)) for r in range(16) for k in range(8)]
    return lax.ppermute(x, ("row", "col"), [(s, t[0] * 8 + t[1]) for s, t in pairs if t])


def along_z(d):
    return lambda r, k: (r, (k + 2 * d) % 8)


def along_y(d):
    return lambda r, k: ((r + 4 * d) % 16, k)


def along_x(d):
    return lambda r, k: (r // 4 * 4 + (r + d) % 4, k)


def other_core(r, k):
    return r, k ^ 1


def across(r, k):
    return (r // 4 + k // 2) % 4 * 4 + k % 2 * 2 + r % 2, r // 2


def to_all(x, moved):
    head = jnp.where(lax.axis_index("col") == 0, x[:32], jnp.zeros((32, FEAT), x.dtype))
    for bit in (1, 2, 4):
        head = head + send(head, lambda r, k: (r, k | bit) if k < bit else None)
    head, moved = lax.optimization_barrier((head, moved))
    column = jnp.stack([head] + [send(head, along_y(d)) for d in (1, 2, 3)])
    column, x = lax.optimization_barrier((column, x))
    return [column] + [send(column, along_x(d)) for d in (1, 2, 3)], moved, along_column(x)


def along_column(x):
    return [send(x, along_z(d)) for d in (1, 2, 3)]


def per_device(samples):
    where = jnp.stack([lax.axis_index("row"), lax.axis_index("col")]).astype(jnp.int32)
    pieces, moved, feats = to_all(samples, send(samples, across))
    col_feats = lax.all_gather(moved, "row", axis=0, tiled=True)
    corner, own = leading(where, pieces, samples)
    feats, own, corner = lax.optimization_barrier((feats, own, corner))
    moved = send(own, across)
    near_feats = jnp.stack([samples] + feats)
    far_feats = send(near_feats, other_core)
    columns = along_column(own)
    half = factor_half(corner, 0)
    moved, far_feats, columns, half = lax.optimization_barrier((moved, far_feats, columns, half))
    own_cols = lax.all_gather(moved, "row", axis=0, tiled=True)
    near = jnp.stack([own] + columns)
    far = send(near, other_core)
    v = factor_half(half, 1)
    kernel = tiles(where, near_feats, far_feats, col_feats)
    return update(where, kernel, near, far, own_cols, v)


def solution(mesh):
    return jax.shard_map(
        per_device,
        mesh=mesh,
        in_specs=(P(("row", "col"), None),),
        out_specs=P("row", "col"),
        check_vma=False,
    )
```

```python
import functools
import math

import jax
import jax.numpy as jnp
import numpy as np
from jax import lax
from jax.experimental import pallas as pl
from jax.experimental.pallas import tpu as pltpu
from jax.sharding import PartitionSpec as P

FEAT = 768
PANEL = 512
LAYERS = 8
TILE_R = 128
TILE_C = 256

ARC = (
    (1.570796265e+00, -9.999884905e-01, 7.850416849e-01, -6.623695706e-01, 5.625094387e-01, -4.372503233e-01, 2.693842319e-01, -1.086155413e-01, 2.049311747e-02),
    (1.570796265e+00, -9.999884905e-01, 7.850416849e-01, -6.623695706e-01, 5.625094387e-01, -4.372503233e-01, 2.693842319e-01, -1.086155413e-01, 2.049311747e-02),
    (1.570326531e+00, -9.935370566e-01, 7.471319178e-01, -5.376914312e-01, 3.111383121e-01, -1.187027540e-01, 2.133516172e-02),
    (1.567898155e+00, -9.719742948e-01, 6.682907781e-01, -3.857788817e-01, 1.484597498e-01, -2.689621130e-02),
    (1.566642297e+00, -9.635808948e-01, 6.460403822e-01, -3.565340200e-01, 1.294006162e-01, -2.196850873e-02),
    (1.558633208e+00, -9.141686374e-01, 5.246089379e-01, -2.079489415e-01, 3.887608390e-02),
    (1.557122831e+00, -9.070176865e-01, 5.119586953e-01, -1.980387362e-01, 3.597512846e-02),
    (1.555954084e+00, -9.016562063e-01, 5.027575168e-01, -1.910373211e-01, 3.398202014e-02),
)


def scales():
    out = [np.float32(1.0)]
    for _ in range(LAYERS):
        out.append(np.float32(np.float32(math.pi) * out[-1]))
    return out


KAPPA = scales()


def polynomial(coefs, c):
    value = c * coefs[-1] + coefs[-2]
    for coef in coefs[-3::-1]:
        value = value * c + coef
    return value


def tangent_of(cosine, tangent):
    for layer in range(LAYERS):
        kappa = KAPPA[layer]
        coefs = [float(a / np.float64(kappa) ** (k + 1)) for k, a in enumerate(ARC[layer])]
        size = jnp.abs(cosine) if layer == 0 else cosine
        square = jnp.maximum(float(np.float32(kappa * kappa)) - size * size, 1e-30)
        sine = square * lax.rsqrt(square)
        angle = sine * polynomial(coefs, size)
        rest = math.pi - angle
        if layer == 0:
            rest = jnp.where(cosine < 0.0, angle, rest)
        cosine = sine + rest * cosine
        tangent = cosine + rest * tangent
    return tangent


def dot_nt(a, b, precision=None):
    return lax.dot_general(
        a, b, (((1,), (1,)), ((), ())), precision=precision, preferred_element_type=jnp.float32
    )


def own_products(x):
    on = lax.broadcasted_iota(jnp.int32, (128, 128), 0) == lax.broadcasted_iota(
        jnp.int32, (128, 128), 1
    )
    for start in range(0, x.shape[0], 128):
        part = x[start : start + 128]
        yield jnp.where(on, dot_nt(part, part), 0.0)


def norms_down(x):
    sums = [jnp.sum(part, axis=1, keepdims=True) for part in own_products(x)]
    return jnp.concatenate([jnp.broadcast_to(n, (128, 128)) for n in sums], axis=0)


def norms_across(x):
    sums = [jnp.sum(part, axis=0, keepdims=True) for part in own_products(x)]
    return jnp.concatenate([jnp.broadcast_to(n, (8, 128)) for n in sums], axis=1)


SCALE = 1.0 / math.sqrt(FEAT * (LAYERS + 1.0) * float(KAPPA[LAYERS]))


def in_order(x):
    return jnp.concatenate(
        [x[m * 128 + a * 32 : m * 128 + a * 32 + 32] for a in range(4) for m in range(2)], axis=0
    )


def gathered_at(t, where):
    return (where[1] // 2 + t // 2) % 4 * 2 + t % 2


def split(x):
    hi = x.astype(jnp.bfloat16)
    return hi, (x - hi.astype(jnp.float32)).astype(jnp.bfloat16)


def slot_of(step, where):
    other = (step + where[1]) % 2
    mine = where[1] + other * (1 - 2 * (where[1] % 2))
    return ((mine - step + 8) % 8) // 2, other


def leading_kernel(
    where_ref, g0, g1, g2, g3, own_ref, corner_ref, out_ref, lead, inv_dn, scl_dn, inv_ac, scl_ac
):
    row_index = where_ref[0]
    col_index = where_ref[1]
    for dx, piece in enumerate((g0, g1, g2, g3)):
        for dy in range(4):
            r = (row_index // 4 + 4 - dy) % 4 * 4 + (row_index % 4 + 4 - dx) % 4
            lead[pl.ds(pl.multiple_of(r * 32, 32), 32), :] = piece[dy]

    def norms(x, start, count):
        n = norms_down(x)
        r = lax.rsqrt(n)
        inv_dn[start : start + count, :] = r
        scl_dn[start : start + count, :] = n * r * SCALE

    x = lead[...]
    norms(x, 0, PANEL)
    n = norms_across(x)
    r = lax.rsqrt(n)
    inv_ac[...] = r
    scl_ac[...] = n * r * SCALE
    norms(own_ref[...], PANEL, 128)
    chunk = 64
    for jb in range(4):
        lanes = slice(jb * 128, jb * 128 + 128)
        cols = lead[lanes, :]
        corner_ref[jb * 128 :, lanes] = dot_nt(lead[jb * 128 :, :], cols)
        out_ref[:, lanes] = dot_nt(own_ref[...], cols)
        inv_c = inv_ac[0:1, lanes]
        scl_c = scl_ac[0:1, lanes]

        def body(step, carry, ref, base):
            start = pl.multiple_of(step * chunk, chunk)
            rows = pl.ds(start, chunk)
            down = pl.ds(start + base, chunk)
            raw = ref[rows, lanes] * inv_dn[down, :] * inv_c
            local = start + lax.broadcasted_iota(jnp.int32, (chunk, 128), 0)
            if base:
                block = local // 32
                local = (col_index * 4 + block) * PANEL + row_index * 32 + local - block * 32
            col_id = jb * 128 + lax.broadcasted_iota(jnp.int32, (chunk, 128), 1)
            on_diag = local == col_id
            tangent = tangent_of(jnp.where(on_diag, 1.0, raw), raw)
            ref[rows, lanes] = tangent * scl_dn[down, :] * scl_c + jnp.where(on_diag, 1.0, 0.0)
            return carry

        lax.fori_loop(0, 128 // chunk, functools.partial(body, ref=out_ref, base=PANEL), 0, unroll=2)
        lax.fori_loop(
            jb * (128 // chunk), PANEL // chunk, functools.partial(body, ref=corner_ref, base=0), 0
        )


def leading(where, pieces, own):
    vmem = pl.BlockSpec(memory_space=pltpu.VMEM)
    return pl.pallas_call(
        leading_kernel,
        out_shape=(
            jax.ShapeDtypeStruct((PANEL, PANEL), jnp.float32),
            jax.ShapeDtypeStruct((128, PANEL), jnp.float32),
        ),
        in_specs=[pl.BlockSpec(memory_space=pltpu.SMEM)] + [vmem] * 5,
        out_specs=(vmem, vmem),
        scratch_shapes=[
            pltpu.VMEM((PANEL, FEAT), jnp.bfloat16),
            pltpu.VMEM((PANEL + 128, 128), jnp.float32),
            pltpu.VMEM((PANEL + 128, 128), jnp.float32),
            pltpu.VMEM((8, PANEL), jnp.float32),
            pltpu.VMEM((8, PANEL), jnp.float32),
        ],
        name="leading",
        cost_estimate=pl.CostEstimate(flops=int(8e9), bytes_accessed=int(2e6), transcendentals=0),
    )(where, *pieces, own)


def thirds(x):
    wide = x.astype(jnp.bfloat16).astype(jnp.float32)
    rest = x - wide
    middle = rest.astype(jnp.bfloat16).astype(jnp.float32)
    return wide, middle, rest - middle


def six_products(x, y, axis):
    a, b, c = thirds(x)
    d, e, f = (a, b, c) if y is x else thirds(y)
    left = jnp.concatenate([a, a, b, a, b, c], axis=axis)
    right = jnp.concatenate([d, e, d, f, e, d], axis=axis)
    return left.astype(jnp.bfloat16), right.astype(jnp.bfloat16)


def product_nt(x, y):
    return dot_nt(*six_products(x, y, 1))


def factor_kernel(in_ref, out_ref, mat, work, *, half):
    eye = jnp.where(
        lax.broadcasted_iota(jnp.int32, (128, 128), 1)
        == lax.broadcasted_iota(jnp.int32, (128, 128), 0),
        1.0,
        0.0,
    )
    sub8 = lax.broadcasted_iota(jnp.int32, (8, 256), 0)
    if half:
        mat[...] = in_ref[...]
    else:
        mat = out_ref
        mat[:PANEL, :] = in_ref[...]
        mat[PANEL:, :] = jnp.zeros((PANEL, PANEL), jnp.float32)

    def eliminate(kb):
        lanes = slice(kb * 128, kb * 128 + 128)
        linv = work[:, 128:]
        inverse = jnp.transpose(linv)
        top = PANEL + kb * 128
        if kb:
            upper = product_nt(mat[PANEL:top, lanes], linv)
            mat[PANEL:top, lanes] = upper
            upper = jnp.concatenate([upper, inverse], axis=0)
        else:
            upper = inverse
        mat[top : top + 128, lanes] = inverse
        if kb < 3:
            below = (kb + 1) * 128
            solved = product_nt(mat[below:PANEL, lanes], linv)
            mat[below:PANEL, below:] = mat[below:PANEL, below:] - product_nt(solved, solved)
            mat[PANEL : top + 128, below:] = mat[PANEL : top + 128, below:] - product_nt(
                upper, solved
            )

    def column(kb, carry):
        first = pl.multiple_of(kb * 128, 128)
        work[:, :128] = mat[pl.ds(first, 128), pl.ds(first, 128)]
        work[:, 128:] = eye
        rows = [jnp.broadcast_to(work[p : p + 1, :], (8, 256)) for p in range(8)]
        for jb in range(16):
            j = jb * 8
            e = [[None] * 8 for _ in range(8)]
            for p in range(8):
                for q in range(p, 8):
                    e[p][q] = jnp.broadcast_to(rows[p][:, j + q : j + q + 1], (8, 128))
            block = None
            done = []
            for p in range(8):
                rinv = lax.rsqrt(e[p][p])
                for q in range(p + 1, 8):
                    e[p][q] = e[p][q] * rinv
                for q in range(p + 1, 8):
                    for s in range(q, 8):
                        e[q][s] = e[q][s] - e[p][q] * e[p][s]
                row = rows[p]
                for m in range(p):
                    row = row - jnp.concatenate([e[m][p]] * 2, axis=1) * done[m]
                row = row * jnp.concatenate([rinv] * 2, axis=1)
                done.append(row)
                block = row if p == 0 else jnp.where(sub8 == p, row, block)
            work[j : j + 8, :] = block
            if jb < 15:
                rows = []
                for p in range(j + 8, j + 16):
                    row = jnp.broadcast_to(work[p : p + 1, :], (8, 256))
                    for m in range(8):
                        factor_m = jnp.broadcast_to(done[m][:, p : p + 1], (8, 128))
                        row = row - jnp.concatenate([factor_m] * 2, axis=1) * done[m]
                    rows.append(row)
            if jb < 14:
                left, right = six_products(block, block, 0)
                outer = lax.dot_general(
                    left[:, :128], right, (((0,), (0,)), ((), ())), preferred_element_type=jnp.float32
                )
                work[j + 16 :, :] = work[j + 16 :, :] - outer[j + 16 :, :]
        for n in range(2 * half, 2 * half + 2):
            pl.when(kb == n)(functools.partial(eliminate, n))
        return carry

    lax.fori_loop(2 * half, 2 * half + 2, column, 0)
    if half:
        hi, lo = split(mat[PANEL:, :])
        out_ref[:, :PANEL] = hi
        out_ref[:, PANEL:] = lo


def factor_half(x, half):
    shape = (
        jax.ShapeDtypeStruct((PANEL, 2 * PANEL), jnp.bfloat16)
        if half
        else jax.ShapeDtypeStruct((2 * PANEL, PANEL), jnp.float32)
    )
    return pl.pallas_call(
        functools.partial(factor_kernel, half=half),
        out_shape=shape,
        in_specs=[pl.BlockSpec(memory_space=pltpu.VMEM)],
        out_specs=pl.BlockSpec(memory_space=pltpu.VMEM),
        scratch_shapes=[
            pltpu.VMEM((2 * PANEL, PANEL), jnp.float32),
            pltpu.VMEM((128, 256), jnp.float32),
        ],
        name="factor",
        cost_estimate=pl.CostEstimate(flops=int(12e9), bytes_accessed=int(2e6), transcendentals=0),
    )(x)


def tiles_kernel(
    where_ref, near_ref, far_ref, cols_ref, out_ref, cols, gram, inv_ac, scl_ac, inv_dn, scl_dn
):
    step = pl.program_id(0)
    row_index = where_ref[0]
    col_index = where_ref[1]
    count = cols_ref.shape[0] // TILE_C

    @pl.when(step == 0)
    def _():
        def body(t, carry):
            source = pl.multiple_of(gathered_at(t, where_ref) * TILE_C, TILE_C)
            x = in_order(cols_ref[pl.ds(source, TILE_C), :])
            cols[pl.ds(pl.multiple_of(t * TILE_C, TILE_C), TILE_C), :] = x
            n = norms_across(x)
            r = lax.rsqrt(n)
            inv_ac[t] = r
            scl_ac[t] = n * r * SCALE
            return carry

        lax.fori_loop(0, count, body, 0)

    _, other = slot_of(step, where_ref)
    x = jnp.where(other == 1, far_ref[0], near_ref[0])
    n = norms_down(x)
    r = lax.rsqrt(n)
    inv_dn[...] = r
    scl_dn[...] = n * r * SCALE
    chunk = 32

    def product(t):
        start = pl.multiple_of(t * TILE_C, TILE_C)
        gram[...] = dot_nt(x, cols[pl.ds(start, TILE_C), :])

    def piece(t, k):
        rows = slice(k * chunk, k * chunk + chunk)
        inv_r = jnp.concatenate([inv_dn[rows, :]] * 2, axis=1)
        scl_r = jnp.concatenate([scl_dn[rows, :]] * 2, axis=1)
        raw = gram[rows, :] * inv_r * inv_ac[t][0:1]
        value = tangent_of(raw, raw) * scl_r * scl_ac[t][0:1]
        out_ref[rows, pl.ds(pl.multiple_of(t * TILE_C, TILE_C), TILE_C)] = value

    product(0)

    def tile(t, carry):
        for k in range(TILE_R // chunk):
            piece(t, k)
        product(t + 1)
        return carry

    lax.fori_loop(0, step, tile, 0)

    def above(t, carry):
        first = pl.multiple_of(t * TILE_C, TILE_C)
        out_ref[:, pl.ds(first, TILE_C)] = jnp.zeros((TILE_R, TILE_C), jnp.float32)
        return carry

    lax.fori_loop(step + 1, count, above, 0)
    out_ref[:64, pl.ds(pl.multiple_of(step * TILE_C + 128, 128), 128)] = jnp.zeros(
        (64, 128), jnp.float32
    )

    for half in range(2):
        rows = slice(half * 64, half * 64 + 64)
        for lane in range(half + 1):
            lanes = slice(lane * 128, lane * 128 + 128)
            raw = gram[rows, lanes] * inv_dn[rows, :] * inv_ac[step][0:1, lanes]
            u = half * 64 + lax.broadcasted_iota(jnp.int32, (64, 128), 0)
            v = lane * 128 + lax.broadcasted_iota(jnp.int32, (64, 128), 1)
            row_id = u // 32 * PANEL + row_index * 32 + u % 32
            col_id = v // 64 * PANEL + col_index * 64 + v % 64
            on_diag = row_id == col_id
            tangent = tangent_of(jnp.where(on_diag, 1.0, raw), raw)
            value = tangent * scl_dn[rows, :] * scl_ac[step][0:1, lanes]
            value = value + jnp.where(on_diag, 1.0, 0.0)
            first = pl.multiple_of(step * TILE_C + lane * 128, 128)
            out_ref[rows, pl.ds(first, 128)] = value


def tiles(where, near, far, cols):
    n_rows, n_cols = 8 * TILE_R, cols.shape[0]
    piece = pl.BlockSpec((1, TILE_R, FEAT), lambda i, where: (slot_of(i, where)[0], 0, 0))
    return pl.pallas_call(
        tiles_kernel,
        out_shape=jax.ShapeDtypeStruct((n_rows, n_cols), jnp.float32),
        grid_spec=pltpu.PrefetchScalarGridSpec(
            num_scalar_prefetch=1,
            grid=(n_rows // TILE_R,),
            in_specs=[
                piece,
                piece,
                pl.BlockSpec((n_cols, FEAT), lambda i, where: (0, 0)),
            ],
            out_specs=pl.BlockSpec((TILE_R, n_cols), lambda i, where: (i, 0)),
            scratch_shapes=[
                pltpu.VMEM((n_cols, FEAT), jnp.bfloat16),
                pltpu.VMEM((TILE_R, TILE_C), jnp.float32),
                pltpu.VMEM((n_cols // TILE_C, 8, TILE_C), jnp.float32),
                pltpu.VMEM((n_cols // TILE_C, 8, TILE_C), jnp.float32),
                pltpu.VMEM((TILE_R, 128), jnp.float32),
                pltpu.VMEM((TILE_R, 128), jnp.float32),
            ],
        ),
        name="tiles",
        cost_estimate=pl.CostEstimate(flops=int(30e9), bytes_accessed=int(12e6), transcendentals=0),
    )(where, near, far, cols)


def solve(x, v_ref):
    hi, lo = split(x)
    parts = []
    for start in range(0, PANEL, 256):
        depth = start + 256
        v_hi = v_ref[:depth, start:depth]
        v_lo = v_ref[:depth, PANEL + start : PANEL + depth]
        left = jnp.concatenate([hi[:, :depth], hi[:, :depth], lo[:, :depth]], axis=1)
        right = jnp.concatenate([v_hi, v_lo, v_hi], axis=0)
        parts.append(jnp.dot(left, right, preferred_element_type=jnp.float32))
    return jnp.concatenate(parts, axis=1)


def update_kernel(
    where_ref, kernel_hbm, near_hbm, far_hbm, cols_hbm, v_hbm, out_hbm, *scratch
):
    slabs = scratch[:4]
    cols, rows, v_ref, both_c, left, v_sem, cols_sem, rows_sem, in_sem, out_sem = scratch[4:]
    row_index = where_ref[0]
    col_index = where_ref[1]
    tall = 2 * TILE_R
    count = cols.shape[0] // TILE_C

    def v_copy():
        return pltpu.make_async_copy(v_hbm, v_ref, v_sem)

    def cols_copy(t):
        part = pl.ds(pl.multiple_of(t * TILE_C, TILE_C), TILE_C)
        source = pl.multiple_of(gathered_at(t, where_ref) * TILE_C, TILE_C)
        return pltpu.make_async_copy(
            cols_hbm.at[pl.ds(source, TILE_C)], cols.at[part], cols_sem.at[t]
        )

    def rows_copy(k, start):
        slot, other = slot_of(k, where_ref)
        for source, match in ((near_hbm, 0), (far_hbm, 1)):

            @pl.when(other == match)
            def _():
                part = pl.ds(k * TILE_R, TILE_R)
                copy = pltpu.make_async_copy(source.at[slot], rows.at[part], rows_sem.at[k])
                if start:
                    copy.start()
                else:
                    copy.wait()

    def place(step):
        return pl.ds(step * tall, tall), pl.ds(0, (step + 1) * 2 * TILE_C)

    def in_copy(step):
        return pltpu.make_async_copy(kernel_hbm.at[place(step)], slabs[step], in_sem.at[step])

    def out_copy(step):
        return pltpu.make_async_copy(slabs[step], out_hbm.at[place(step)], out_sem.at[step])

    v_copy().start()
    for t in range(count):
        cols_copy(t).start()
    for k in range(8):
        rows_copy(k, True)
    for step in (3, 2, 1, 0):
        in_copy(step).start()
    v_copy().wait()

    def solve_columns(t, carry):
        cols_copy(t).wait()
        part = pl.ds(pl.multiple_of(t * TILE_C, TILE_C), TILE_C)
        hi, lo = split(solve(in_order(cols[part, :]), v_ref))
        both_c[part, :PANEL] = hi
        both_c[part, PANEL:] = lo
        return carry

    lax.fori_loop(0, count, solve_columns, 0)

    for step in (3, 2, 1, 0):
        slab = slabs[step]
        rows_copy(2 * step, False)
        rows_copy(2 * step + 1, False)
        solved = solve(rows[step * tall : step * tall + tall, :], v_ref)
        if step < 3:
            out_copy(step + 1).start()
        hi_r, lo_r = split(solved)
        all_r = jnp.concatenate([hi_r, hi_r, lo_r], axis=1)
        for n in range(4):
            left[n] = solved[:, n * 128 : n * 128 + 128]
        in_copy(step).wait()
        for t in range(2 * step + 2):
            lanes = slice(t * TILE_C, t * TILE_C + TILE_C)
            all_c = jnp.concatenate([both_c[lanes, :], both_c[lanes, :PANEL]], axis=1)
            value = slab[:, lanes] - dot_nt(all_r, all_c)
            v = lax.broadcasted_iota(jnp.int32, (tall, TILE_C), 1)
            if t == 0:
                mine = left[col_index // 2]
                mine = jnp.where(col_index % 2 == 1, pltpu.roll(mine, 64, 1), mine)
                mine = jnp.concatenate([mine, mine], axis=1)
                value = jnp.where(v < 64, mine, value)
            if t >= 2 * step:
                s = lax.broadcasted_iota(jnp.int32, (tall, TILE_C), 0)
                row_id = (step * 8 + s // 32) * PANEL + row_index * 32 + s % 32
                col_id = (t * 4 + v // 64) * PANEL + col_index * 64 + v % 64
                value = jnp.where(row_id >= col_id, value, 0.0)
            slab[:, lanes] = value
    out_copy(0).start()
    for step in range(4):
        out_copy(step).wait()


def update(where, kernel, near, far, cols, v):
    n_rows, n_cols = kernel.shape
    tall = 2 * TILE_R
    count = n_cols // TILE_C
    hbm = pl.BlockSpec(memory_space=pl.ANY)
    return pl.pallas_call(
        update_kernel,
        out_shape=jax.ShapeDtypeStruct((n_rows, n_cols), jnp.float32),
        in_specs=[pl.BlockSpec(memory_space=pltpu.SMEM)] + [hbm] * 5,
        out_specs=hbm,
        scratch_shapes=[pltpu.VMEM((tall, (k + 1) * 2 * TILE_C), jnp.float32) for k in range(4)]
        + [
            pltpu.VMEM((n_cols, PANEL), jnp.float32),
            pltpu.VMEM((n_rows, PANEL), jnp.float32),
            pltpu.VMEM((PANEL, 2 * PANEL), jnp.bfloat16),
            pltpu.VMEM((n_cols, 2 * PANEL), jnp.bfloat16),
            pltpu.VMEM((4, tall, 128), jnp.float32),
            pltpu.SemaphoreType.DMA,
            pltpu.SemaphoreType.DMA((count,)),
            pltpu.SemaphoreType.DMA((8,)),
            pltpu.SemaphoreType.DMA((4,)),
            pltpu.SemaphoreType.DMA((4,)),
        ],
        input_output_aliases={1: 0},
        name="update",
        cost_estimate=pl.CostEstimate(flops=int(6e9), bytes_accessed=int(20e6), transcendentals=0),
    )(where, kernel, near, far, cols, v)


def send(x, target):
    pairs = [(r * 8 + k, target(r, k)) for r in range(16) for k in range(8)]
    return lax.ppermute(x, ("row", "col"), [(s, t[0] * 8 + t[1]) for s, t in pairs if t])


def along_z(d):
    return lambda r, k: (r, (k + 2 * d) % 8)


def along_y(d):
    return lambda r, k: ((r + 4 * d) % 16, k)


def along_x(d):
    return lambda r, k: (r // 4 * 4 + (r + d) % 4, k)


def other_core(r, k):
    return r, k ^ 1


def across(r, k):
    return (r // 4 + k // 2) % 4 * 4 + k % 2 * 2 + r % 2, r // 2


def to_all(x, moved):
    head = jnp.where(lax.axis_index("col") == 0, x[:32], jnp.zeros((32, FEAT), x.dtype))
    for bit in (1, 2, 4):
        head = head + send(head, lambda r, k: (r, k | bit) if k < bit else None)
    head, moved = lax.optimization_barrier((head, moved))
    column = jnp.stack([head] + [send(head, along_y(d)) for d in (1, 2, 3)])
    column, x = lax.optimization_barrier((column, x))
    return [column] + [send(column, along_x(d)) for d in (1, 2, 3)], moved, along_column(x)


def along_column(x):
    return [send(x, along_z(d)) for d in (1, 2, 3)]


def per_device(samples):
    where = jnp.stack([lax.axis_index("row"), lax.axis_index("col")]).astype(jnp.int32)
    pieces, moved, feats = to_all(samples, send(samples, across))
    col_feats = lax.all_gather(moved, "row", axis=0, tiled=True)
    corner, own = leading(where, pieces, samples)
    feats, own, corner = lax.optimization_barrier((feats, own, corner))
    moved = send(own, across)
    near_feats = jnp.stack([samples] + feats)
    far_feats = send(near_feats, other_core)
    columns = along_column(own)
    half = factor_half(corner, 0)
    moved, far_feats, columns, half = lax.optimization_barrier((moved, far_feats, columns, half))
    own_cols = lax.all_gather(moved, "row", axis=0, tiled=True)
    near = jnp.stack([own] + columns)
    far = send(near, other_core)
    v = factor_half(half, 1)
    kernel = tiles(where, near_feats, far_feats, col_feats)
    return update(where, kernel, near, far, own_cols, v)


def solution(mesh):
    return jax.shard_map(
        per_device,
        mesh=mesh,
        in_specs=(P(("row", "col"), None),),
        out_specs=P("row", "col"),
        check_vma=False,
    )
```

```python
import functools
import math

import jax
import jax.numpy as jnp
import numpy as np
from jax import lax
from jax.experimental import pallas as pl
from jax.experimental.pallas import tpu as pltpu
from jax.sharding import PartitionSpec as P

FEAT = 768
PANEL = 512
LAYERS = 8
TILE_R = 128
TILE_C = 256

ARC = (
    (1.570796265e+00, -9.999884905e-01, 7.850416849e-01, -6.623695706e-01, 5.625094387e-01, -4.372503233e-01, 2.693842319e-01, -1.086155413e-01, 2.049311747e-02),
    (1.570796265e+00, -9.999884905e-01, 7.850416849e-01, -6.623695706e-01, 5.625094387e-01, -4.372503233e-01, 2.693842319e-01, -1.086155413e-01, 2.049311747e-02),
    (1.570326531e+00, -9.935370566e-01, 7.471319178e-01, -5.376914312e-01, 3.111383121e-01, -1.187027540e-01, 2.133516172e-02),
    (1.567898155e+00, -9.719742948e-01, 6.682907781e-01, -3.857788817e-01, 1.484597498e-01, -2.689621130e-02),
    (1.566642297e+00, -9.635808948e-01, 6.460403822e-01, -3.565340200e-01, 1.294006162e-01, -2.196850873e-02),
    (1.558633208e+00, -9.141686374e-01, 5.246089379e-01, -2.079489415e-01, 3.887608390e-02),
    (1.557122831e+00, -9.070176865e-01, 5.119586953e-01, -1.980387362e-01, 3.597512846e-02),
    (1.555954084e+00, -9.016562063e-01, 5.027575168e-01, -1.910373211e-01, 3.398202014e-02),
)


def scales():
    out = [np.float32(1.0)]
    for _ in range(LAYERS):
        out.append(np.float32(np.float32(math.pi) * out[-1]))
    return out


KAPPA = scales()


def polynomial(coefs, c):
    value = c * coefs[-1] + coefs[-2]
    for coef in coefs[-3::-1]:
        value = value * c + coef
    return value


def tangent_of(cosine, tangent):
    for layer in range(LAYERS):
        kappa = KAPPA[layer]
        coefs = [float(a / np.float64(kappa) ** (k + 1)) for k, a in enumerate(ARC[layer])]
        size = jnp.abs(cosine) if layer == 0 else cosine
        square = jnp.maximum(float(np.float32(kappa * kappa)) - size * size, 1e-30)
        sine = square * lax.rsqrt(square)
        angle = sine * polynomial(coefs, size)
        rest = math.pi - angle
        if layer == 0:
            rest = jnp.where(cosine < 0.0, angle, rest)
        cosine = sine + rest * cosine
        tangent = cosine + rest * tangent
    return tangent


def dot_nt(a, b, precision=None):
    return lax.dot_general(
        a, b, (((1,), (1,)), ((), ())), precision=precision, preferred_element_type=jnp.float32
    )


def own_products(x):
    on = lax.broadcasted_iota(jnp.int32, (128, 128), 0) == lax.broadcasted_iota(
        jnp.int32, (128, 128), 1
    )
    for start in range(0, x.shape[0], 128):
        part = x[start : start + 128]
        yield jnp.where(on, dot_nt(part, part), 0.0)


def norms_down(x):
    sums = [jnp.sum(part, axis=1, keepdims=True) for part in own_products(x)]
    return jnp.concatenate([jnp.broadcast_to(n, (128, 128)) for n in sums], axis=0)


def norms_across(x):
    sums = [jnp.sum(part, axis=0, keepdims=True) for part in own_products(x)]
    return jnp.concatenate([jnp.broadcast_to(n, (8, 128)) for n in sums], axis=1)


SCALE = 1.0 / math.sqrt(FEAT * (LAYERS + 1.0) * float(KAPPA[LAYERS]))


def in_order(x):
    return jnp.concatenate(
        [x[m * 128 + a * 32 : m * 128 + a * 32 + 32] for a in range(4) for m in range(2)], axis=0
    )


def gathered_at(t, where):
    return (where[1] // 2 + t // 2) % 4 * 2 + t % 2


def split(x):
    hi = x.astype(jnp.bfloat16)
    return hi, (x - hi.astype(jnp.float32)).astype(jnp.bfloat16)


def slot_of(step, where):
    other = (step + where[1]) % 2
    mine = where[1] + other * (1 - 2 * (where[1] % 2))
    return ((mine - step + 8) % 8) // 2, other


def leading_kernel(
    where_ref, g0, g1, g2, g3, own_ref, corner_ref, out_ref, lead, inv_dn, scl_dn, inv_ac, scl_ac
):
    row_index = where_ref[0]
    col_index = where_ref[1]
    for dx, piece in enumerate((g0, g1, g2, g3)):
        for dy in range(4):
            r = (row_index // 4 + 4 - dy) % 4 * 4 + (row_index % 4 + 4 - dx) % 4
            lead[pl.ds(pl.multiple_of(r * 32, 32), 32), :] = piece[dy]

    def norms(x, start, count):
        n = norms_down(x)
        r = lax.rsqrt(n)
        inv_dn[start : start + count, :] = r
        scl_dn[start : start + count, :] = n * r * SCALE

    x = lead[...]
    norms(x, 0, PANEL)
    n = norms_across(x)
    r = lax.rsqrt(n)
    inv_ac[...] = r
    scl_ac[...] = n * r * SCALE
    norms(own_ref[...], PANEL, 128)
    chunk = 64
    for jb in range(4):
        lanes = slice(jb * 128, jb * 128 + 128)
        cols = lead[lanes, :]
        corner_ref[jb * 128 :, lanes] = dot_nt(lead[jb * 128 :, :], cols)
        out_ref[:, lanes] = dot_nt(own_ref[...], cols)
        inv_c = inv_ac[0:1, lanes]
        scl_c = scl_ac[0:1, lanes]

        def body(step, carry, ref, base):
            start = pl.multiple_of(step * chunk, chunk)
            rows = pl.ds(start, chunk)
            down = pl.ds(start + base, chunk)
            raw = ref[rows, lanes] * inv_dn[down, :] * inv_c
            local = start + lax.broadcasted_iota(jnp.int32, (chunk, 128), 0)
            if base:
                block = local // 32
                local = (col_index * 4 + block) * PANEL + row_index * 32 + local - block * 32
            col_id = jb * 128 + lax.broadcasted_iota(jnp.int32, (chunk, 128), 1)
            on_diag = local == col_id
            tangent = tangent_of(jnp.where(on_diag, 1.0, raw), raw)
            ref[rows, lanes] = tangent * scl_dn[down, :] * scl_c + jnp.where(on_diag, 1.0, 0.0)
            return carry

        lax.fori_loop(0, 128 // chunk, functools.partial(body, ref=out_ref, base=PANEL), 0, unroll=2)
        lax.fori_loop(
            jb * (128 // chunk), PANEL // chunk, functools.partial(body, ref=corner_ref, base=0), 0
        )


def leading(where, pieces, own):
    vmem = pl.BlockSpec(memory_space=pltpu.VMEM)
    return pl.pallas_call(
        leading_kernel,
        out_shape=(
            jax.ShapeDtypeStruct((PANEL, PANEL), jnp.float32),
            jax.ShapeDtypeStruct((128, PANEL), jnp.float32),
        ),
        in_specs=[pl.BlockSpec(memory_space=pltpu.SMEM)] + [vmem] * 5,
        out_specs=(vmem, vmem),
        scratch_shapes=[
            pltpu.VMEM((PANEL, FEAT), jnp.bfloat16),
            pltpu.VMEM((PANEL + 128, 128), jnp.float32),
            pltpu.VMEM((PANEL + 128, 128), jnp.float32),
            pltpu.VMEM((8, PANEL), jnp.float32),
            pltpu.VMEM((8, PANEL), jnp.float32),
        ],
        name="leading",
        cost_estimate=pl.CostEstimate(flops=int(8e9), bytes_accessed=int(2e6), transcendentals=0),
    )(where, *pieces, own)


def thirds(x):
    wide = x.astype(jnp.bfloat16).astype(jnp.float32)
    rest = x - wide
    middle = rest.astype(jnp.bfloat16).astype(jnp.float32)
    return wide, middle, rest - middle


def six_products(x, y, axis):
    a, b, c = thirds(x)
    d, e, f = (a, b, c) if y is x else thirds(y)
    left = jnp.concatenate([a, a, b, a, b, c], axis=axis)
    right = jnp.concatenate([d, e, d, f, e, d], axis=axis)
    return left.astype(jnp.bfloat16), right.astype(jnp.bfloat16)


def product_nt(x, y):
    return dot_nt(*six_products(x, y, 1))


def factor_kernel(in_ref, out_ref, mat, work, *, half):
    eye = jnp.where(
        lax.broadcasted_iota(jnp.int32, (128, 128), 1)
        == lax.broadcasted_iota(jnp.int32, (128, 128), 0),
        1.0,
        0.0,
    )
    sub8 = lax.broadcasted_iota(jnp.int32, (8, 256), 0)
    if half:
        mat[...] = in_ref[...]
    else:
        mat = out_ref
        mat[:PANEL, :] = in_ref[...]
        mat[PANEL:, :] = jnp.zeros((PANEL, PANEL), jnp.float32)

    def eliminate(kb):
        lanes = slice(kb * 128, kb * 128 + 128)
        linv = work[:, 128:]
        inverse = jnp.transpose(linv)
        top = PANEL + kb * 128
        if kb:
            upper = product_nt(mat[PANEL:top, lanes], linv)
            mat[PANEL:top, lanes] = upper
            upper = jnp.concatenate([upper, inverse], axis=0)
        else:
            upper = inverse
        mat[top : top + 128, lanes] = inverse
        if kb < 3:
            below = (kb + 1) * 128
            solved = product_nt(mat[below:PANEL, lanes], linv)
            mat[below:PANEL, below:] = mat[below:PANEL, below:] - product_nt(solved, solved)
            mat[PANEL : top + 128, below:] = mat[PANEL : top + 128, below:] - product_nt(
                upper, solved
            )

    def column(kb, carry):
        first = pl.multiple_of(kb * 128, 128)
        work[:, :128] = mat[pl.ds(first, 128), pl.ds(first, 128)]
        work[:, 128:] = eye
        rows = [jnp.broadcast_to(work[p : p + 1, :], (8, 256)) for p in range(8)]
        for jb in range(16):
            j = jb * 8
            e = [[None] * 8 for _ in range(8)]
            for p in range(8):
                for q in range(p, 8):
                    e[p][q] = jnp.broadcast_to(rows[p][:, j + q : j + q + 1], (8, 128))
            block = None
            done = []
            for p in range(8):
                rinv = lax.rsqrt(e[p][p])
                for q in range(p + 1, 8):
                    e[p][q] = e[p][q] * rinv
                for q in range(p + 1, 8):
                    for s in range(q, 8):
                        e[q][s] = e[q][s] - e[p][q] * e[p][s]
                row = rows[p]
                for m in range(p):
                    row = row - jnp.concatenate([e[m][p]] * 2, axis=1) * done[m]
                row = row * jnp.concatenate([rinv] * 2, axis=1)
                done.append(row)
                block = row if p == 0 else jnp.where(sub8 == p, row, block)
            work[j : j + 8, :] = block
            if jb < 15:
                rows = []
                for p in range(j + 8, j + 16):
                    row = jnp.broadcast_to(work[p : p + 1, :], (8, 256))
                    for m in range(8):
                        factor_m = jnp.broadcast_to(done[m][:, p : p + 1], (8, 128))
                        row = row - jnp.concatenate([factor_m] * 2, axis=1) * done[m]
                    rows.append(row)
            if jb < 14:
                left, right = six_products(block, block, 0)
                outer = lax.dot_general(
                    left[:, :128], right, (((0,), (0,)), ((), ())), preferred_element_type=jnp.float32
                )
                work[j + 16 :, :] = work[j + 16 :, :] - outer[j + 16 :, :]
        for n in range(2 * half, 2 * half + 2):
            pl.when(kb == n)(functools.partial(eliminate, n))
        return carry

    lax.fori_loop(2 * half, 2 * half + 2, column, 0)
    if half:
        hi, lo = split(mat[PANEL:, :])
        out_ref[:, :PANEL] = hi
        out_ref[:, PANEL:] = lo


def factor_half(x, half):
    shape = (
        jax.ShapeDtypeStruct((PANEL, 2 * PANEL), jnp.bfloat16)
        if half
        else jax.ShapeDtypeStruct((2 * PANEL, PANEL), jnp.float32)
    )
    return pl.pallas_call(
        functools.partial(factor_kernel, half=half),
        out_shape=shape,
        in_specs=[pl.BlockSpec(memory_space=pltpu.VMEM)],
        out_specs=pl.BlockSpec(memory_space=pltpu.VMEM),
        scratch_shapes=[
            pltpu.VMEM((2 * PANEL, PANEL), jnp.float32),
            pltpu.VMEM((128, 256), jnp.float32),
        ],
        name="factor",
        cost_estimate=pl.CostEstimate(flops=int(12e9), bytes_accessed=int(2e6), transcendentals=0),
    )(x)


def tiles_kernel(
    where_ref, near_ref, far_ref, cols_ref, out_ref, cols, gram, inv_ac, scl_ac, inv_dn, scl_dn
):
    step = pl.program_id(0)
    row_index = where_ref[0]
    col_index = where_ref[1]
    count = cols_ref.shape[0] // TILE_C

    @pl.when(step == 0)
    def _():
        def body(t, carry):
            source = pl.multiple_of(gathered_at(t, where_ref) * TILE_C, TILE_C)
            x = in_order(cols_ref[pl.ds(source, TILE_C), :])
            cols[pl.ds(pl.multiple_of(t * TILE_C, TILE_C), TILE_C), :] = x
            n = norms_across(x)
            r = lax.rsqrt(n)
            inv_ac[t] = r
            scl_ac[t] = n * r * SCALE
            return carry

        lax.fori_loop(0, count, body, 0)

    _, other = slot_of(step, where_ref)
    x = jnp.where(other == 1, far_ref[0], near_ref[0])
    n = norms_down(x)
    r = lax.rsqrt(n)
    inv_dn[...] = r
    scl_dn[...] = n * r * SCALE
    chunk = 32

    def product(t):
        start = pl.multiple_of(t * TILE_C, TILE_C)
        gram[...] = dot_nt(x, cols[pl.ds(start, TILE_C), :])

    def piece(t, k):
        rows = slice(k * chunk, k * chunk + chunk)
        inv_r = jnp.concatenate([inv_dn[rows, :]] * 2, axis=1)
        scl_r = jnp.concatenate([scl_dn[rows, :]] * 2, axis=1)
        raw = gram[rows, :] * inv_r * inv_ac[t][0:1]
        value = tangent_of(raw, raw) * scl_r * scl_ac[t][0:1]
        out_ref[rows, pl.ds(pl.multiple_of(t * TILE_C, TILE_C), TILE_C)] = value

    product(0)

    def tile(t, carry):
        for k in range(TILE_R // chunk):
            piece(t, k)
        product(t + 1)
        return carry

    lax.fori_loop(0, step, tile, 0)

    def above(t, carry):
        first = pl.multiple_of(t * TILE_C, TILE_C)
        out_ref[:, pl.ds(first, TILE_C)] = jnp.zeros((TILE_R, TILE_C), jnp.float32)
        return carry

    lax.fori_loop(step + 1, count, above, 0)
    out_ref[:64, pl.ds(pl.multiple_of(step * TILE_C + 128, 128), 128)] = jnp.zeros(
        (64, 128), jnp.float32
    )

    for half in range(2):
        rows = slice(half * 64, half * 64 + 64)
        for lane in range(half + 1):
            lanes = slice(lane * 128, lane * 128 + 128)
            raw = gram[rows, lanes] * inv_dn[rows, :] * inv_ac[step][0:1, lanes]
            u = half * 64 + lax.broadcasted_iota(jnp.int32, (64, 128), 0)
            v = lane * 128 + lax.broadcasted_iota(jnp.int32, (64, 128), 1)
            row_id = u // 32 * PANEL + row_index * 32 + u % 32
            col_id = v // 64 * PANEL + col_index * 64 + v % 64
            on_diag = row_id == col_id
            tangent = tangent_of(jnp.where(on_diag, 1.0, raw), raw)
            value = tangent * scl_dn[rows, :] * scl_ac[step][0:1, lanes]
            value = value + jnp.where(on_diag, 1.0, 0.0)
            first = pl.multiple_of(step * TILE_C + lane * 128, 128)
            out_ref[rows, pl.ds(first, 128)] = value


def tiles(where, near, far, cols):
    n_rows, n_cols = 8 * TILE_R, cols.shape[0]
    piece = pl.BlockSpec((1, TILE_R, FEAT), lambda i, where: (slot_of(i, where)[0], 0, 0))
    return pl.pallas_call(
        tiles_kernel,
        out_shape=jax.ShapeDtypeStruct((n_rows, n_cols), jnp.float32),
        grid_spec=pltpu.PrefetchScalarGridSpec(
            num_scalar_prefetch=1,
            grid=(n_rows // TILE_R,),
            in_specs=[
                piece,
                piece,
                pl.BlockSpec((n_cols, FEAT), lambda i, where: (0, 0)),
            ],
            out_specs=pl.BlockSpec((TILE_R, n_cols), lambda i, where: (i, 0)),
            scratch_shapes=[
                pltpu.VMEM((n_cols, FEAT), jnp.bfloat16),
                pltpu.VMEM((TILE_R, TILE_C), jnp.float32),
                pltpu.VMEM((n_cols // TILE_C, 8, TILE_C), jnp.float32),
                pltpu.VMEM((n_cols // TILE_C, 8, TILE_C), jnp.float32),
                pltpu.VMEM((TILE_R, 128), jnp.float32),
                pltpu.VMEM((TILE_R, 128), jnp.float32),
            ],
        ),
        name="tiles",
        cost_estimate=pl.CostEstimate(flops=int(30e9), bytes_accessed=int(12e6), transcendentals=0),
    )(where, near, far, cols)


def solve(x, v_ref):
    hi, lo = split(x)
    parts = []
    for start in range(0, PANEL, 256):
        depth = start + 256
        v_hi = v_ref[:depth, start:depth]
        v_lo = v_ref[:depth, PANEL + start : PANEL + depth]
        left = jnp.concatenate([hi[:, :depth], hi[:, :depth], lo[:, :depth]], axis=1)
        right = jnp.concatenate([v_hi, v_lo, v_hi], axis=0)
        parts.append(jnp.dot(left, right, preferred_element_type=jnp.float32))
    return jnp.concatenate(parts, axis=1)


def update_kernel(
    where_ref, kernel_hbm, near_hbm, far_hbm, cols_hbm, v_hbm, out_hbm, *scratch
):
    slabs = scratch[:4]
    cols, rows, v_ref, both_c, left, v_sem, cols_sem, rows_sem, in_sem, out_sem = scratch[4:]
    row_index = where_ref[0]
    col_index = where_ref[1]
    tall = 2 * TILE_R
    count = cols.shape[0] // TILE_C

    def v_copy():
        return pltpu.make_async_copy(v_hbm, v_ref, v_sem)

    def cols_copy(t):
        part = pl.ds(pl.multiple_of(t * TILE_C, TILE_C), TILE_C)
        source = pl.multiple_of(gathered_at(t, where_ref) * TILE_C, TILE_C)
        return pltpu.make_async_copy(
            cols_hbm.at[pl.ds(source, TILE_C)], cols.at[part], cols_sem.at[t]
        )

    def rows_copy(k, start):
        slot, other = slot_of(k, where_ref)
        for source, match in ((near_hbm, 0), (far_hbm, 1)):

            @pl.when(other == match)
            def _():
                part = pl.ds(k * TILE_R, TILE_R)
                copy = pltpu.make_async_copy(source.at[slot], rows.at[part], rows_sem.at[k])
                if start:
                    copy.start()
                else:
                    copy.wait()

    def place(step):
        return pl.ds(step * tall, tall), pl.ds(0, (step + 1) * 2 * TILE_C)

    def in_copy(step):
        return pltpu.make_async_copy(kernel_hbm.at[place(step)], slabs[step], in_sem.at[step])

    def out_copy(step):
        return pltpu.make_async_copy(slabs[step], out_hbm.at[place(step)], out_sem.at[step])

    v_copy().start()
    for t in range(count):
        cols_copy(t).start()
    for k in range(8):
        rows_copy(k, True)
    for step in (3, 2, 1, 0):
        in_copy(step).start()
    v_copy().wait()

    def solve_columns(t, carry):
        cols_copy(t).wait()
        part = pl.ds(pl.multiple_of(t * TILE_C, TILE_C), TILE_C)
        hi, lo = split(solve(in_order(cols[part, :]), v_ref))
        both_c[part, :PANEL] = hi
        both_c[part, PANEL:] = lo
        return carry

    lax.fori_loop(0, count, solve_columns, 0)

    for step in (3, 2, 1, 0):
        slab = slabs[step]
        rows_copy(2 * step, False)
        rows_copy(2 * step + 1, False)
        solved = solve(rows[step * tall : step * tall + tall, :], v_ref)
        if step < 3:
            out_copy(step + 1).start()
        hi_r, lo_r = split(solved)
        all_r = jnp.concatenate([hi_r, hi_r, lo_r], axis=1)
        for n in range(4):
            left[n] = solved[:, n * 128 : n * 128 + 128]
        in_copy(step).wait()
        for t in range(2 * step + 2):
            lanes = slice(t * TILE_C, t * TILE_C + TILE_C)
            all_c = jnp.concatenate([both_c[lanes, :], both_c[lanes, :PANEL]], axis=1)
            value = slab[:, lanes] - dot_nt(all_r, all_c)
            v = lax.broadcasted_iota(jnp.int32, (tall, TILE_C), 1)
            if t == 0:
                mine = left[col_index // 2]
                mine = jnp.where(col_index % 2 == 1, pltpu.roll(mine, 64, 1), mine)
                mine = jnp.concatenate([mine, mine], axis=1)
                value = jnp.where(v < 64, mine, value)
            if t >= 2 * step:
                s = lax.broadcasted_iota(jnp.int32, (tall, TILE_C), 0)
                row_id = (step * 8 + s // 32) * PANEL + row_index * 32 + s % 32
                col_id = (t * 4 + v // 64) * PANEL + col_index * 64 + v % 64
                value = jnp.where(row_id >= col_id, value, 0.0)
            slab[:, lanes] = value
    out_copy(0).start()
    for step in range(4):
        out_copy(step).wait()


def update(where, kernel, near, far, cols, v):
    n_rows, n_cols = kernel.shape
    tall = 2 * TILE_R
    count = n_cols // TILE_C
    hbm = pl.BlockSpec(memory_space=pl.ANY)
    return pl.pallas_call(
        update_kernel,
        out_shape=jax.ShapeDtypeStruct((n_rows, n_cols), jnp.float32),
        in_specs=[pl.BlockSpec(memory_space=pltpu.SMEM)] + [hbm] * 5,
        out_specs=hbm,
        scratch_shapes=[pltpu.VMEM((tall, (k + 1) * 2 * TILE_C), jnp.float32) for k in range(4)]
        + [
            pltpu.VMEM((n_cols, PANEL), jnp.float32),
            pltpu.VMEM((n_rows, PANEL), jnp.float32),
            pltpu.VMEM((PANEL, 2 * PANEL), jnp.bfloat16),
            pltpu.VMEM((n_cols, 2 * PANEL), jnp.bfloat16),
            pltpu.VMEM((4, tall, 128), jnp.float32),
            pltpu.SemaphoreType.DMA,
            pltpu.SemaphoreType.DMA((count,)),
            pltpu.SemaphoreType.DMA((8,)),
            pltpu.SemaphoreType.DMA((4,)),
            pltpu.SemaphoreType.DMA((4,)),
        ],
        input_output_aliases={1: 0},
        name="update",
        cost_estimate=pl.CostEstimate(flops=int(6e9), bytes_accessed=int(20e6), transcendentals=0),
    )(where, kernel, near, far, cols, v)


def send(x, target):
    pairs = [(r * 8 + k, target(r, k)) for r in range(16) for k in range(8)]
    return lax.ppermute(x, ("row", "col"), [(s, t[0] * 8 + t[1]) for s, t in pairs if t])


def along_z(d):
    return lambda r, k: (r, (k + 2 * d) % 8)


def along_y(d):
    return lambda r, k: ((r + 4 * d) % 16, k)


def along_x(d):
    return lambda r, k: (r // 4 * 4 + (r + d) % 4, k)


def other_core(r, k):
    return r, k ^ 1


def across(r, k):
    return (r // 4 + k // 2) % 4 * 4 + k % 2 * 2 + r % 2, r // 2


def to_all(x, moved):
    head = jnp.where(lax.axis_index("col") == 0, x[:32], jnp.zeros((32, FEAT), x.dtype))
    first = [send(head, lambda r, k: (r, t) if k == 0 else None) for t in (1, 2, 6)]
    head = head + (first[0] + first[1] + first[2])
    onward = {0: 3, 1: 7, 2: 4, 6: 5}
    head = head + send(head, lambda r, k: (r, onward[k]) if k in onward else None)
    head, moved = lax.optimization_barrier((head, moved))
    column = jnp.stack([head] + [send(head, along_y(d)) for d in (1, 2, 3)])
    column, x = lax.optimization_barrier((column, x))
    return [column] + [send(column, along_x(d)) for d in (1, 2, 3)], moved, along_column(x)


def along_column(x):
    return [send(x, along_z(d)) for d in (1, 2, 3)]


def per_device(samples):
    where = jnp.stack([lax.axis_index("row"), lax.axis_index("col")]).astype(jnp.int32)
    pieces, moved, feats = to_all(samples, send(samples, across))
    col_feats = lax.all_gather(moved, "row", axis=0, tiled=True)
    corner, own = leading(where, pieces, samples)
    feats, own, corner = lax.optimization_barrier((feats, own, corner))
    moved = send(own, across)
    near_feats = jnp.stack([samples] + feats)
    far_feats = send(near_feats, other_core)
    columns = along_column(own)
    half = factor_half(corner, 0)
    moved, far_feats, columns, half = lax.optimization_barrier((moved, far_feats, columns, half))
    own_cols = lax.all_gather(moved, "row", axis=0, tiled=True)
    near = jnp.stack([own] + columns)
    far = send(near, other_core)
    v = factor_half(half, 1)
    kernel = tiles(where, near_feats, far_feats, col_feats)
    return update(where, kernel, near, far, own_cols, v)


def solution(mesh):
    return jax.shard_map(
        per_device,
        mesh=mesh,
        in_specs=(P(("row", "col"), None),),
        out_specs=P("row", "col"),
        check_vma=False,
    )
```
